32 devices in a mesh: samp: 4 (over y, x), box: 8 (over z, core).
Axes of the slice: x: 2, y: 2, z: 4, core: 2. Of those that a mesh axis runs over, the one named last changes fastest.
Arguments:
- pattern_a: float32 [1024, 2, 18432], P('box', None, 'samp'), may hold values from -6 to 6
- children_b: int32 [256, 8], P('box'), may hold values from -1 to 1023, as said below
- children_c: int32 [64, 8], P('box'), may hold values from -1 to 255, as said below
- theta_ab: float32 [96, 128], replicated, may hold values from -0.625 to 0.625
- theta_bc: float32 [128, 160], replicated, may hold values from -0.5 to 0.5
- phi_start_b: int32 [256], P('samp'), may hold values from 0 to 191, as said below
- phi_weight_b: float32 [4, 256], P(None, 'samp'), may hold values from -0.25 to 1
- phi_start_c: int32 [320], P('samp'), may hold values from 0 to 255, as said below
- phi_weight_c: float32 [4, 320], P(None, 'samp'), may hold values from -0.25 to 1
- translation: float32 [316, 2, 51200], P(None, None, 'samp'), may hold values from -0.1875 to 0.1875
- list_src: int32 [64, 32], P('box'), may hold values from 0 to 63
- list_vec: int32 [64, 32], P('box'), may hold values from 0 to 315
Outputs:
- incoming: float32 [64, 2, 51200], P('box', None, 'samp')
The draws below stay inside these ranges and needn't reach their ends.
Inputs may be any that keep to these rules, and one draw needn't show every extreme that they name: `children_b`: entry o of a row is -1 or the level-A box in octant o = 4 ox + 2 oy + oz of that level-B box; level-B box p and its children lie on the same index of box, boxes p // 32 and c // 128 being equal; every level-A box is the child of exactly one level-B box. `children_c`: entry o of a row is -1 or the level-B box in octant o of that level-C box; p // 8 equals c // 32; every level-B box is the child of exactly one level-C box. phi_start_b[m] is (m * 192 // 256 - 1) or (m * 192 // 256 - 2), modulo 192. phi_start_c[m] is (m * 256 // 320 - 1) or (m * 256 // 320 - 2), modulo 256.
All inputs are finite; a program needn't handle non-finite values.
Results may differ from the reference program's by a relative error of at most 0.000071.
Values sent between devices are 32-bit elements; how exact they have to be, the bound alone decides.
A program may use at most 192 MiB of HBM per device.

```python
import jax
import jax.numpy as jnp
from jax import lax

THETA_A = 96
PHI_A = 192
THETA_B = 128
PHI_B = 256
THETA_C = 160
PHI_C = 320
SIZE_B = 8
SIZE_C = 16
LIST = 32
VECTORS = 316
BC_DEV = 8
BB_DEV = 32
BA_DEV = 128
NBA = 1024
NBB = 256
NBC = 64


def octree_slots(key, parents_dev, children_dev, parents_all):

    def one_block(block_id):
        ranking = jax.random.permutation(jax.random.fold_in(key, block_id), 8 * parents_dev).astype(jnp.int32)
        return jnp.where(ranking < children_dev, ranking + block_id * children_dev, -1).reshape(parents_dev, 8)
    block_ids = jnp.arange(parents_all // parents_dev, dtype=jnp.int32)
    blocks = jax.vmap(one_block)(block_ids)
    return blocks.reshape(parents_all, 8).astype(jnp.int32)


def stencil_starts(key, n_parent, n_child):
    parent_ids = jnp.arange(n_parent, dtype=jnp.int32)
    nearest = parent_ids * n_child // n_parent
    backoff = jax.random.randint(key, (n_parent,), 1, 3, dtype=jnp.int32)
    return ((nearest - backoff) % n_child).astype(jnp.int32)


def draw_children_b(key, part):
    return octree_slots(jax.random.fold_in(key, 101), BB_DEV, BA_DEV, NBB)


def draw_children_c(key, part):
    return octree_slots(jax.random.fold_in(key, 202), BC_DEV, BB_DEV, NBC)


def draw_phi_start_b(key, part):
    return stencil_starts(jax.random.fold_in(key, 303), PHI_B, PHI_A)


def draw_phi_start_c(key, part):
    return stencil_starts(jax.random.fold_in(key, 404), PHI_C, PHI_B)


def plant(drawn, stream_key, low, largest):
    shape = drawn.shape
    spot = [jax.random.randint(jax.random.fold_in(stream_key, axis), (), 0, shape[axis]) for axis in range(len(shape))]
    drawn = drawn.at[tuple(spot)].set(low)
    longest = shape.index(max(shape))
    spot[longest] = (spot[longest] + 1) % shape[longest]
    return drawn.at[tuple(spot)].set(largest)


def level_of(rng, dims, shards, low, largest):
    factor_of = 1.0
    for position, shards_of in shards:
        draws = jax.random.uniform(jax.random.fold_in(jax.random.fold_in(rng, 6), position), (shards_of,), jnp.float32, low / len(shards), largest / len(shards))
        factor_of = factor_of * jnp.repeat(jnp.exp(draws), dims[position] // shards_of).reshape((-1,) + (1,) * (len(dims) - 1 - position))
    return factor_of


def noise(key, extent, width, bound, pieces=(), kind=jnp.bfloat16):
    gain = level_of(key, extent, pieces, -0.22, 0.18) if pieces else 1.0
    array = jax.random.normal(key, extent, jnp.float32) * width * gain
    return jnp.minimum(jnp.maximum(array, -bound), bound).astype(kind)


def setup_inputs(seed: int = 0) -> dict:
    arg_keys = jax.random.split(jax.random.key(seed), 13)
    pattern_a = noise(arg_keys[0], (NBA, 2, PHI_A * THETA_A), 1.0, 6.0, ((0, 8), (2, 4)), jnp.float32)
    children_b = draw_children_b(jax.random.fold_in(arg_keys[12], 71), 0)
    children_c = draw_children_c(jax.random.fold_in(arg_keys[12], 71), 0)
    theta_ab = noise(arg_keys[3], (THETA_A, THETA_B), THETA_A ** -0.5, 0.625, (), jnp.float32)
    theta_bc = noise(arg_keys[4], (THETA_B, THETA_C), THETA_B ** -0.5, 0.5, (), jnp.float32)
    phi_start_b = draw_phi_start_b(jax.random.fold_in(arg_keys[12], 71), 0)
    phi_weight_b = jnp.clip(-0.25 + 1.25 * jax.random.uniform(arg_keys[6], (4, PHI_B), jnp.float32) ** level_of(arg_keys[6], (4, PHI_B), ((1, 4),), -0.2, 0.2), -0.25, 1.0)
    phi_start_c = draw_phi_start_c(jax.random.fold_in(arg_keys[12], 71), 0)
    phi_weight_c = jnp.clip(-0.25 + 1.25 * jax.random.uniform(arg_keys[8], (4, PHI_C), jnp.float32) ** level_of(arg_keys[8], (4, PHI_C), ((1, 4),), -0.2, 0.2), -0.25, 1.0)
    translation = noise(arg_keys[9], (VECTORS, 2, PHI_C * THETA_C), 0.03, 0.1875, ((2, 4),), jnp.float32)
    list_src = plant(jax.random.randint(arg_keys[10], (NBC, LIST), 0, NBC), jax.random.fold_in(arg_keys[10], 1), 0, NBC - 1).astype(jnp.int32)
    list_vec = plant(jax.random.randint(arg_keys[11], (NBC, LIST), 0, VECTORS), jax.random.fold_in(arg_keys[11], 1), 0, VECTORS - 1).astype(jnp.int32)
    return dict(pattern_a=pattern_a, children_b=children_b, children_c=children_c, theta_ab=theta_ab, theta_bc=theta_bc, phi_start_b=phi_start_b, phi_weight_b=phi_weight_b, phi_start_c=phi_start_c, phi_weight_c=phi_weight_c, translation=translation, list_src=list_src, list_vec=list_vec)


PRECISE = lax.Precision.HIGHEST


def directions(n_theta, n_phi, phi_first, phi_count):
    polar = jnp.pi * (jnp.arange(n_theta, dtype=jnp.int32).astype(jnp.float32) + 0.5) / n_theta
    azimuth = 2.0 * jnp.pi * (phi_first + jnp.arange(phi_count, dtype=jnp.int32)).astype(jnp.float32) / n_phi
    polar_sine = jnp.sin(polar)[None, :]
    dir_x = jnp.cos(azimuth)[:, None] * polar_sine
    dir_y = jnp.sin(azimuth)[:, None] * polar_sine
    dir_z = jnp.broadcast_to(jnp.cos(polar)[None, :], dir_x.shape)
    return dir_x, dir_y, dir_z


def aggregate(level, children, first_box, box_size, n_phi, phi_first):
    box_count = level.shape[0]
    flat = level.reshape(box_count, 2, level.shape[2] * level.shape[3])
    dir_x, dir_y, dir_z = directions(level.shape[3], n_phi, phi_first, level.shape[2])
    summed = jnp.zeros((children.shape[0], 2, flat.shape[2]), jnp.float32)
    for octant in range(8):
        sign_x = 2.0 * ((octant >> 2) & 1) - 1.0
        sign_y = 2.0 * ((octant >> 1) & 1) - 1.0
        sign_z = 2.0 * (octant & 1) - 1.0
        phase = (0.5 * jnp.pi * box_size) * (sign_x * dir_x + sign_y * dir_y + sign_z * dir_z)
        cosine = jnp.cos(phase).reshape(-1)
        sine_part = jnp.sin(phase).reshape(-1)
        child_ids = (children[:, octant] - first_box).astype(jnp.int32)
        present = (children[:, octant] >= 0).astype(jnp.float32)[:, None]
        picked = jnp.take(flat, jnp.clip(child_ids, 0, box_count - 1), axis=0)
        real_part = picked[:, 0] * cosine - picked[:, 1] * sine_part
        imag_part = picked[:, 0] * sine_part + picked[:, 1] * cosine
        summed = summed + jnp.stack([present * real_part, present * imag_part], axis=1)
    return summed


def translate(rows, operators, vectors):
    picked = jnp.take(operators, vectors.reshape(-1), axis=0).reshape(rows.shape)
    real_part = jnp.sum(picked[:, :, 0] * rows[:, :, 0] - picked[:, :, 1] * rows[:, :, 1], axis=1)
    imag_part = jnp.sum(picked[:, :, 0] * rows[:, :, 1] + picked[:, :, 1] * rows[:, :, 0], axis=1)
    return jnp.stack([real_part, imag_part], axis=1)


def interpolate(pattern, theta_matrix, phi_start, phi_weight, n_phi_child, n_theta_child):
    box_count = pattern.shape[0]
    grid = pattern.reshape(box_count, 2, n_phi_child, n_theta_child)
    grid = jnp.einsum('bcpt,tu->bcpu', grid, theta_matrix, precision=PRECISE)
    summed = jnp.zeros((box_count, 2, phi_start.shape[0], theta_matrix.shape[1]), jnp.float32)
    for offset in range(4):
        cell_ids = ((phi_start + offset) % n_phi_child).astype(jnp.int32)
        summed = summed + phi_weight[offset][None, None, :, None] * jnp.take(grid, cell_ids, axis=2)
    return summed


def reference(pattern_a, children_b, children_c, theta_ab, theta_bc, phi_start_b, phi_weight_b, phi_start_c, phi_weight_c, translation, list_src, list_vec):
    level_b = interpolate(pattern_a, theta_ab, phi_start_b, phi_weight_b, PHI_A, THETA_A)
    pattern_b = aggregate(level_b, children_b, 0, SIZE_B, PHI_B, 0)
    level_c = interpolate(pattern_b, theta_bc, phi_start_c, phi_weight_c, PHI_B, THETA_B)
    pattern_c = aggregate(level_c, children_c, 0, SIZE_C, PHI_C, 0)

    def one_target(entry):
        sources, vectors = entry
        rows = jnp.take(pattern_c, sources, axis=0)[None]
        return translate(rows, translation, vectors[None])[0]

    return lax.map(one_target, (list_src, list_vec))
```

```python
import functools
import math

import jax
import jax.numpy as jnp
import numpy as np
from jax import lax
from jax.experimental import pallas as pl
from jax.experimental.layout import Layout, with_layout_constraint
from jax.experimental.pallas import tpu as pltpu
from jax.sharding import PartitionSpec as P

SIZE_B = 8
SIZE_C = 16
LANES = 128
MESH = pl.DeviceIdType.MESH
CHUNK = 2
GROUP = 4


def window(first, last, n_child, n_parent):
    low = 0
    while (low - 1) * n_child // n_parent + 2 >= first:
        low -= 1
    high = 0
    while (high + 1) * n_child // n_parent - 2 <= last:
        high += 1
    return low, high + 1


def phase_table(parts, per_part, low, high, n_theta, size):
    n_phi = parts * per_part
    theta = np.pi * (np.arange(n_theta) + 0.5) / n_theta
    first = np.arange(parts)[:, None] * per_part
    phi = 2.0 * np.pi * (first + np.arange(low, high)[None]) / n_phi
    u_x = np.cos(phi)[..., None] * np.sin(theta)
    u_y = np.sin(phi)[..., None] * np.sin(theta)
    u_z = np.broadcast_to(np.cos(theta), u_x.shape)
    psi = []
    for o in range(8):
        s_x, s_y, s_z = 2 * (o >> 2 & 1) - 1, 2 * (o >> 1 & 1) - 1, 2 * (o & 1) - 1
        psi.append(0.5 * np.pi * size * (s_x * u_x + s_y * u_y + s_z * u_z))
    psi = np.stack(psi, axis=2)
    return np.concatenate([np.cos(psi), np.sin(psi)], axis=2).astype(np.float32)


def split(x):
    high = x.astype(jnp.bfloat16)
    return high, (x - high.astype(jnp.float32)).astype(jnp.bfloat16)


def split_outside(x):
    high = lax.reduce_precision(x, exponent_bits=8, mantissa_bits=7)
    return high.astype(jnp.bfloat16), (x - high).astype(jnp.bfloat16)


def mm(a, b):
    return jnp.dot(a, b, preferred_element_type=jnp.float32)


def aggregate_kernel(
    steps, az_step, wb, wc, ext, plan,
    samp, idx_b, wgt_b, idx_c, wgt_c,
    x_ref, tab_ref, sb_ref, phb_ref, tbc_ref, sc_ref, phc_ref,
    o_ref, grid_a, grid_b,
):
    step = pl.program_id(0)
    count_a = x_ref.shape[0]
    rows_x = x_ref.shape[1]
    rows = x_ref.reshape(count_a * rows_x, LANES)
    for c in range(2):
        for q in range(az_step // GROUP):
            tiles = [
                split(rows[pl.ds(6 * q + 2 * j + c, count_a, stride=rows_x), :]) for j in range(3)
            ]
            for pair in range(2):
                high = jnp.concatenate([tiles[pair][0], tiles[pair + 1][0]], axis=1)
                low = jnp.concatenate([tiles[pair][1], tiles[pair + 1][1]], axis=1)
                both = mm(high, tab_ref[pair, 0]) + mm(low, tab_ref[pair, 0]) + mm(high, tab_ref[pair, 1])
                for k in range(2):
                    place = step * az_step + q * GROUP + pair * 2 + k
                    grid_a[place, c * count_a : (c + 1) * count_a, :] = both[:, k * LANES : (k + 1) * LANES]

    @pl.when(step == steps - 1)
    def _():
        count_b = sb_ref.shape[0] // 8
        n_theta_c = tbc_ref.shape[2]

        def level_b(m, carry):
            parts = []
            for c in range(2):
                here = slice(c * count_a, (c + 1) * count_a)
                value = wgt_b[0, m] * grid_a[idx_b[0, m], here, :]
                for k in range(1, 4):
                    value = value + wgt_b[k, m] * grid_a[idx_b[k, m], here, :]
                parts.append(split(value))
            stacked = jnp.concatenate(
                [
                    jnp.concatenate([parts[0][0], parts[1][0]], axis=1),
                    jnp.concatenate([parts[0][1], parts[1][1]], axis=1),
                ],
                axis=0,
            )
            picked = mm(sb_ref[...], stacked)
            real = jnp.zeros((count_b, LANES), jnp.float32)
            imag = jnp.zeros((count_b, LANES), jnp.float32)
            for o in range(8):
                cosine = phb_ref[m, o : o + 1, :]
                sine = phb_ref[m, 8 + o : 9 + o, :]
                pr = picked[o * count_b : (o + 1) * count_b, :LANES]
                pi = picked[o * count_b : (o + 1) * count_b, LANES:]
                real = real + pr * cosine - pi * sine
                imag = imag + pr * sine + pi * cosine
            high, low = split(jnp.concatenate([real, imag], axis=0))
            both = jnp.concatenate([high, low], axis=1)
            grid_b[m] = mm(both, tbc_ref[0]) + mm(high, tbc_ref[1, :LANES])
            return carry

        lax.fori_loop(0, wb, level_b, 0)

        count_c = sc_ref.shape[0] // 8
        o_ref[...] = jnp.zeros(o_ref.shape, jnp.float32)
        edge, inner = ext // GROUP, wc // GROUP - 2 * (ext // GROUP)

        def level_c(g, carry):
            reals, imags = [], []
            for i in range(GROUP):
                n = g * GROUP + i
                value = wgt_c[0, n] * grid_b[idx_c[0, n]]
                for k in range(1, 4):
                    value = value + wgt_c[k, n] * grid_b[idx_c[k, n]]
                high, low = split(value)
                rr = mm(sc_ref[...], jnp.concatenate([high[:count_b], low[:count_b]], axis=0))
                ri = mm(sc_ref[...], jnp.concatenate([high[count_b:], low[count_b:]], axis=0))
                real = jnp.zeros((count_c, n_theta_c), jnp.float32)
                imag = jnp.zeros((count_c, n_theta_c), jnp.float32)
                for o in range(8):
                    cosine = phc_ref[n, o : o + 1, :]
                    sine = phc_ref[n, 8 + o : 9 + o, :]
                    pr = rr[o * count_c : (o + 1) * count_c]
                    pi = ri[o * count_c : (o + 1) * count_c]
                    real = real + pr * cosine - pi * sine
                    imag = imag + pr * sine + pi * cosine
                reals.append(real)
                imags.append(imag)
            for c, flat in enumerate((jnp.concatenate(reals, axis=1), jnp.concatenate(imags, axis=1))):
                tiles = flat.shape[1] // LANES
                base = jnp.where(
                    g < edge,
                    plan.padded + plan.left_pad + g * 2 * tiles,
                    jnp.where(
                        g < edge + inner,
                        (g - edge) * 2 * tiles,
                        plan.padded + plan.left_rows + (g - edge - inner) * 2 * tiles,
                    ),
                )
                for t in range(tiles):
                    o_ref[pl.ds(base + 2 * t + c, count_c, stride=plan.total), :] = flat[
                        :, t * LANES : (t + 1) * LANES
                    ]
            return carry

        lax.fori_loop(0, wc // GROUP, level_c, 0)


def far_kernel(
    plan, list_len, n_samp, wide, lists, t_hbm, o_ref,
    list_all, list_smem, halo_left, halo_right, swapped, res, psend, precv, *rest,
):
    n_chunk = len(plan.sizes)
    srcs, tbufs = rest[:n_chunk], rest[n_chunk : 2 * n_chunk]
    (list_sem, smem_sem, halo_sem, t_sem, src_send, src_recv, p_sem, out_sem) = rest[2 * n_chunk :]
    samp, box = lax.axis_index("samp"), lax.axis_index("box")
    n_box = plan.n_box
    n_chip = n_box // 2
    chip, core = box // 2, box % 2
    partner = chip * 2 + 1 - core
    own = wide.shape[0]
    first_end, last_end = chip == 0, chip == n_chip - 1
    is_end = first_end | last_end
    helps_first, helps_last = chip == 1, chip == n_chip - 2
    helps = helps_first | helps_last
    helped = jnp.where(helps_first, 0, n_chip - 1)
    helper = jnp.where(first_end, 1, n_chip - 2)
    left = (lax.rem(samp + n_samp - 1, n_samp), box)
    right = (lax.rem(samp + 1, n_samp), box)

    def remote(src, dst, send, recv, device):
        return pltpu.make_async_remote_copy(
            src_ref=src, dst_ref=dst, send_sem=send, recv_sem=recv, device_id=device, device_id_type=MESH
        )

    barrier = pltpu.get_barrier_semaphore()
    for other in range(n_box):
        @pl.when(box != other)
        def _():
            pl.semaphore_signal(barrier, inc=1, device_id=(samp, other), device_id_type=MESH)
    for device in (left, right):
        pl.semaphore_signal(barrier, inc=1, device_id=device, device_id_type=MESH)
    pl.semaphore_wait(barrier, n_box + 1)

    def half_rows(which, c):
        count = 8 * plan.sizes[c]
        low = 8 * (plan.split - plan.starts[c]) - count
        high = 8 * (plan.split + plan.starts[c])
        return pl.ds(pl.multiple_of(jnp.where(which == 0, low, high), 8), count)

    def has(which, c):
        return (which == 0) | plan.both[c]

    def t_copy(c):
        return pltpu.make_async_copy(t_hbm.at[:, half_rows(core, c), :], tbufs[c], t_sem.at[c])

    def when_has(which, c, do):
        if plan.both[c]:
            do()
        else:
            pl.when(which == 0)(do)

    to_left = remote(wide.at[:, plan.left_at, :], halo_right, halo_sem.at[0], halo_sem.at[1], left)
    to_right = remote(wide.at[:, plan.right_at, :], halo_left, halo_sem.at[2], halo_sem.at[3], right)
    to_left.start()
    to_right.start()

    def list_copy(slot, device, k):
        return remote(lists, list_all.at[slot], list_sem.at[k], list_sem.at[3 + slot], device)

    list_copy(core, (samp, partner), 0).start()

    @pl.when(is_end)
    def _():
        for d in range(2):
            list_copy(2 + core, (samp, helper * 2 + d), 1 + d).start()

    def src_copy(c, chip_to, d):
        index = c * n_box + chip_to * 2 + d
        return remote(
            wide.at[:, half_rows(d, c), :],
            srcs[c].at[pl.ds(pl.multiple_of(own * box, 8), own)],
            src_send.at[index],
            src_recv.at[c * n_box + box],
            (samp, chip_to * 2 + d),
        )

    def send_chunk(c, act):
        def to_partner():
            act(src_copy(c, chip, 1 - core))

        when_has(1 - core, c, to_partner)
        for chip_to in range(1, n_chip - 1):
            @pl.when(chip != chip_to)
            def _():
                for d in range(2):
                    if d == 0 or plan.both[c]:
                        act(src_copy(c, chip_to, d))

    for c in range(plan.early):
        send_chunk(c, lambda copy: copy.start())
    for c in range(n_chunk):
        when_has(core, c, lambda c=c: t_copy(c).start())

    list_all[core] = lists[...]
    to_left.wait_recv()
    to_right.wait_recv()
    at_end = pl.ds(plan.end_at, halo_right.shape[1])
    wide[:, at_end, :] = wide[:, at_end, :] + halo_right[...]
    at_start = pl.ds(0, halo_left.shape[1])
    wide[:, at_start, :] = wide[:, at_start, :] + halo_left[...]
    for c in range(plan.early, n_chunk):
        send_chunk(c, lambda copy: copy.start())

    list_copy(1 - core, (samp, partner), 0).wait_recv()

    @pl.when(helps)
    def _():
        for d in range(2):
            list_copy(2 + d, (samp, partner), 0).wait_recv()

    n_src = own * n_box
    low = jnp.where(last_end, n_src - 2 * own, 0)
    high = jnp.where(first_end, 2 * own, n_src)
    low_p = jnp.where(helps_first, 2 * own, 0)
    high_p = jnp.where(helps_last, n_src - 2 * own, n_src)
    lane = lax.broadcasted_iota(jnp.int32, list_all.shape[1:], 1)
    for slot in range(4):
        a, b = (low, high) if slot < 2 else (low_p, high_p)
        value = list_all[slot]
        gone = (lane < list_len) & ((value < a) | (value >= b))
        list_all[slot] = jnp.where(gone, n_src, value)
    to_smem = pltpu.make_async_copy(list_all, list_smem, smem_sem)
    to_smem.start()
    to_smem.wait()

    even = lax.rem(lax.broadcasted_iota(jnp.int32, (8, LANES), 0), 2) == 0

    def turn(x):
        return jnp.where(even, pltpu.roll(x, 7, 0), pltpu.roll(x, 1, 0))

    def gather_sum(c, slot, i):
        size = plan.sizes[c]
        by_same = [jnp.zeros((8, LANES), jnp.float32) for _ in range(size)]
        by_turned = [jnp.zeros((8, LANES), jnp.float32) for _ in range(size)]
        for l in range(list_len):
            s = list_smem[slot, i, l]
            v = list_smem[slot, i, list_len + l]
            for g in range(size):
                here = slice(8 * g, 8 * g + 8)
                t = tbufs[c][v, here, :]
                by_same[g] = by_same[g] + t * srcs[c][s, here, :]
                by_turned[g] = by_turned[g] + t * swapped[s, here, :]
        out = []
        for g in range(size):
            x, y = by_same[g], by_turned[g]
            out.append(jnp.where(even, x - pltpu.roll(x, 7, 0), y + pltpu.roll(y, 1, 0)))
        return out

    def result_copy(c):
        return remote(
            res.at[pl.ds(pl.multiple_of((1 - core) * own, 8), own), plan.local[c], :],
            o_ref.at[:, half_rows(core, c), :],
            out_sem.at[c],
            out_sem.at[n_chunk + c],
            (samp, partner),
        )

    def result_wait(c):
        return remote(
            res.at[pl.ds(pl.multiple_of((1 - core) * own, 8), own), plan.local[c], :],
            o_ref.at[:, half_rows(1 - core, c), :],
            out_sem.at[c],
            out_sem.at[n_chunk + c],
            (samp, partner),
        )

    def p_copy(c, chip_to):
        return remote(
            psend.at[:, plan.local[c], :],
            precv.at[:, plan.local[c], :],
            p_sem.at[c],
            p_sem.at[n_chunk + c],
            (samp, chip_to * 2 + core),
        )

    def one_chunk(c):
        size = plan.sizes[c]
        rows = 8 * size
        place = plan.local[c]
        srcs[c][pl.ds(pl.multiple_of(own * box, 8), own)] = wide[:, half_rows(core, c), :]
        srcs[c][pl.ds(n_src, 8)] = jnp.zeros((8, rows, LANES), jnp.float32)
        swapped[pl.ds(n_src, 8)] = jnp.zeros((8, swapped.shape[1], LANES), jnp.float32)
        t_copy(c).wait()

        def arrived(other):
            pltpu.make_async_copy(
                wide.at[:, half_rows(core, c), :],
                srcs[c].at[pl.ds(own * other, own)],
                src_recv.at[c * n_box + other],
            ).wait()

        for other in range(n_box):
            here = box != other
            if other // 2 != 0 or True:
                here = here & (jnp.logical_not(is_end) | (chip == other // 2))
            pl.when(here)(functools.partial(arrived, other))

        def swap_one(s, carry):
            for g in range(size):
                here = slice(8 * g, 8 * g + 8)
                swapped[s, here, :] = turn(srcs[c][s, here, :])
            return carry

        first = jnp.where(is_end, 2 * own * chip, 0)
        last = jnp.where(is_end, 2 * own * chip + 2 * own, n_src)
        lax.fori_loop(first, last, swap_one, 0)

        @pl.when(helps)
        def _():
            def one(p, carry):
                slot, i = 2 + p // own, lax.rem(p, own)
                for g, value in enumerate(gather_sum(c, slot, i)):
                    psend[p, pl.ds(place.start + 8 * g, 8), :] = value
                return carry

            lax.fori_loop(0, 2 * own, one, 0)
            p_copy(c, helped).start()

        def one(p, carry):
            slot, i = p // own, lax.rem(p, own)
            for g, value in enumerate(gather_sum(c, slot, i)):
                res[p, pl.ds(place.start + 8 * g, 8), :] = value
            return carry

        lax.fori_loop(0, 2 * own, one, 0)

    def deliver(c):
        place = plan.local[c]

        @pl.when(is_end)
        def _():
            p_copy(c, chip).wait_recv()
            res[:, place, :] = res[:, place, :] + precv[:, place, :]

        o_ref[:, half_rows(core, c), :] = res[pl.ds(pl.multiple_of(core * own, 8), own), place, :]
        result_copy(c).start()

    def chunk_mid(c):
        one_chunk(c)

        @pl.when(jnp.logical_not(is_end))
        def _():
            deliver_plain(c)

    def deliver_plain(c):
        place = plan.local[c]
        o_ref[:, half_rows(core, c), :] = res[pl.ds(pl.multiple_of(core * own, 8), own), place, :]
        result_copy(c).start()

    def deliver_end(c):
        place = plan.local[c]
        p_copy(c, chip).wait_recv()
        res[:, place, :] = res[:, place, :] + precv[:, place, :]
        deliver_plain(c)

    for c in range(n_chunk):
        when_has(core, c, lambda c=c: chunk_mid(c))

    @pl.when(is_end)
    def _():
        for c in range(n_chunk):
            when_has(core, c, lambda c=c: deliver_end(c))

    for c in range(n_chunk):
        when_has(1 - core, c, lambda c=c: result_wait(c).wait_recv())
        when_has(core, c, lambda c=c: result_copy(c).wait_send())
        send_chunk(c, lambda copy: copy.wait_send())

        @pl.when(helps)
        def _():
            when_has(core, c, lambda: p_copy(c, helped).wait_send())

    to_left.wait_send()
    to_right.wait_send()
    list_copy(core, (samp, partner), 0).wait_send()

    @pl.when(is_end)
    def _():
        for d in range(2):
            list_copy(2 + core, (samp, helper * 2 + d), 1 + d).wait_send()


class Plan:
    def __init__(self, n_box, rows, ext_rows, group):
        self.n_box = n_box
        self.rows = rows
        self.padded = -(-rows // 8) * 8
        groups = self.padded // 8
        self.split = -(-groups // 2)
        other = groups - self.split
        self.sizes = [group] * (other // group)
        self.sizes += [1] * (self.split - sum(self.sizes))
        self.starts = [sum(self.sizes[:c]) for c in range(len(self.sizes))]
        self.both = [self.starts[c] + self.sizes[c] <= other for c in range(len(self.sizes))]
        self.local = [pl.ds(8 * a, 8 * n) for a, n in zip(self.starts, self.sizes)]
        self.end_at = (rows - ext_rows) // 8 * 8
        self.left_rows = self.padded - self.end_at
        self.left_pad = rows - ext_rows - self.end_at
        self.right_rows = -(-ext_rows // 8) * 8
        self.left_at = pl.ds(self.padded, self.left_rows)
        self.right_at = pl.ds(self.padded + self.left_rows, self.right_rows)
        self.total = self.padded + self.left_rows + self.right_rows
        touched = max(self.left_rows, self.right_rows) // 8
        self.early = sum(self.starts[c] + self.sizes[c] <= other - touched for c in range(len(self.sizes)))


def interleave(x):
    x = x.reshape(x.shape[0], 2, -1, LANES).transpose(0, 2, 1, 3)
    x = with_layout_constraint(x, Layout(major_to_minor=(0, 1, 2, 3))).reshape(x.shape[0], -1, LANES)
    return jnp.pad(x, ((0, 0), (0, -x.shape[1] % 8), (0, 0))) if x.shape[1] % 8 else x


def separate(x, rows):
    x = x[:, :rows].reshape(x.shape[0], -1, 2, LANES)
    x = with_layout_constraint(x, Layout(major_to_minor=(0, 1, 2, 3)))
    return x.transpose(0, 2, 1, 3).reshape(x.shape[0], 2, -1)


def stencil(start, weight, first, low, high, src_low, src_high, n_child):
    nearest = start - first
    tap = nearest[None, :] + jnp.arange(4, dtype=jnp.int32)[:, None]
    half = n_child // 2
    tap = (tap + half) % n_child - half
    centre = (src_low + src_high) // 2
    tap = jnp.where(tap - centre > half, tap - n_child, tap)
    tap = jnp.where(tap - centre < -half, tap + n_child, tap)
    inside = (tap >= src_low) & (tap < src_high)
    rows = jnp.clip(tap - src_low, 0, src_high - src_low - 1)
    return rows.astype(jnp.int32), jnp.where(inside, weight, 0.0)


def one_hot(children, first, count):
    ids = (children - first).T.reshape(-1)
    hot = ((ids[:, None] == jnp.arange(count)[None, :]) & (children.T.reshape(-1) >= 0)[:, None]).astype(jnp.bfloat16)
    return jnp.concatenate([hot, hot], axis=1)


def per_device(
    n_samp, n_box,
    pattern_a, children_b, children_c, theta_ab, theta_bc,
    phi_start_b, phi_weight_b, phi_start_c, phi_weight_c,
    translation, list_src, list_vec,
):
    samp = lax.axis_index("samp")
    box = lax.axis_index("box")
    count_a, count_b, count_c = pattern_a.shape[0], children_b.shape[0], children_c.shape[0]
    theta_a, theta_b = theta_ab.shape
    theta_c = theta_bc.shape[1]
    pa = pattern_a.shape[2] // theta_a
    pb = phi_start_b.shape[0]
    pc = phi_start_c.shape[0]
    n_a, n_b, n_c = n_samp * pa, n_samp * pb, n_samp * pc
    low_b, high_b = window(0, pa - 1, n_a, n_b)
    low_c, high_c = window(low_b, high_b - 1, n_b, n_c)
    ext = -(-max(-low_c, high_c - pc) // GROUP) * GROUP
    low_c, high_c = -ext, pc + ext
    wb, wc = high_b - low_b, high_c - low_c

    up = [(i, (i + 1) % n_samp) for i in range(n_samp)]
    down = [((i + 1) % n_samp, i) for i in range(n_samp)]
    table_b = jnp.concatenate([phi_start_b.astype(jnp.float32)[None], phi_weight_b], axis=0)
    table_c = jnp.concatenate([phi_start_c.astype(jnp.float32)[None], phi_weight_c], axis=0)
    near = max(ext, -low_b, high_b - pb)
    left = lax.ppermute(jnp.concatenate([table_b[:, pb - near :], table_c[:, pc - near :]], 1), "samp", up)
    right = lax.ppermute(jnp.concatenate([table_b[:, :near], table_c[:, :near]], 1), "samp", down)
    table_b = jnp.concatenate([left[:, near + low_b : near], table_b, right[:, : high_b - pb]], 1)
    table_c = jnp.concatenate([left[:, 2 * near - ext :], table_c, right[:, near : near + ext]], 1)
    idx_b, wgt_b = stencil(
        table_b[0].astype(jnp.int32), table_b[1:], samp * pa, low_b, high_b, 0, pa, n_a
    )
    idx_c, wgt_c = stencil(
        table_c[0].astype(jnp.int32), table_c[1:], samp * pb, low_c, high_c, low_b, high_b, n_b
    )

    tab = []
    for pair in range(2):
        at = pair * (2 * theta_a - LANES)
        blocks = jnp.zeros((2 * LANES, 2 * theta_b), jnp.float32)
        for k in range(2):
            blocks = lax.dynamic_update_slice(blocks, theta_ab, (at + k * theta_a, k * theta_b))
        tab.append(jnp.stack(split_outside(blocks)))
    tab = jnp.stack(tab)
    high, low = split_outside(theta_bc)
    tbc = jnp.stack([jnp.concatenate([high, high], 0), jnp.concatenate([low, low], 0)])
    s_b = one_hot(children_b, box * count_a, count_a)
    s_c = one_hot(children_c, box * count_b, count_b)
    phb = jnp.asarray(phase_table(n_samp, pb, low_b, high_b, theta_b, SIZE_B))
    phc = jnp.asarray(phase_table(n_samp, pc, low_c, high_c, theta_c, SIZE_C))

    x = interleave(pattern_a)
    steps = pa // 16 if pa % 16 == 0 else 1
    rows_x = x.shape[1]
    az_step = pa // steps
    tiles = GROUP * theta_c // LANES
    ext_rows = ext // GROUP * 2 * tiles
    rows = pc // GROUP * 2 * tiles
    plan = Plan(n_box, rows, ext_rows, CHUNK)
    one = pl.Buffered(1)
    wide = pl.pallas_call(
        functools.partial(aggregate_kernel, steps, az_step, wb, wc, ext, plan),
        grid_spec=pltpu.PrefetchScalarGridSpec(
            num_scalar_prefetch=5,
            grid=(steps,),
            in_specs=[
                pl.BlockSpec((count_a, rows_x // steps, LANES), lambda i, *_: (0, i, 0)),
                pl.BlockSpec(tab.shape, lambda i, *_: (0, 0, 0, 0), pipeline_mode=one),
                pl.BlockSpec(s_b.shape, lambda i, *_: (0, 0), pipeline_mode=one),
                pl.BlockSpec((None,) + phb.shape[1:], lambda i, s, *_: (s[0], 0, 0, 0), pipeline_mode=one),
                pl.BlockSpec(tbc.shape, lambda i, *_: (0, 0, 0), pipeline_mode=one),
                pl.BlockSpec(s_c.shape, lambda i, *_: (0, 0), pipeline_mode=one),
                pl.BlockSpec((None,) + phc.shape[1:], lambda i, s, *_: (s[0], 0, 0, 0), pipeline_mode=one),
            ],
            out_specs=pl.BlockSpec((count_c * plan.total, LANES), lambda i, *_: (0, 0)),
            scratch_shapes=[
                pltpu.VMEM((pa, 2 * count_a, LANES), jnp.float32),
                pltpu.VMEM((wb, 2 * count_b, theta_c), jnp.float32),
            ],
        ),
        out_shape=jax.ShapeDtypeStruct((count_c * plan.total, LANES), jnp.float32),
        compiler_params=pltpu.CompilerParams(vmem_limit_bytes=48 << 20),
        name="aggregate",
    )(samp.reshape(1), idx_b, wgt_b, idx_c, wgt_c, x, tab, s_b, phb, tbc, s_c, phc)
    wide = wide.reshape(count_c, plan.total, LANES)

    list_len = list_src.shape[1]
    n_src = count_c * n_box
    lists = jnp.concatenate([list_src, list_vec], axis=1)
    lists = jnp.pad(lists, ((0, 0), (0, -lists.shape[1] % LANES)))
    t_view = interleave(translation)
    n_vec = t_view.shape[0]
    n_chunk = len(plan.sizes)
    big = 8 * CHUNK
    half = 8 * plan.split
    vmem = pl.BlockSpec(memory_space=pltpu.VMEM)
    out = pl.pallas_call(
        functools.partial(far_kernel, plan, list_len, n_samp),
        in_specs=[vmem, vmem, pl.BlockSpec(memory_space=pl.ANY)],
        out_specs=vmem,
        scratch_shapes=[
            pltpu.VMEM((4,) + lists.shape, jnp.int32),
            pltpu.SMEM((4,) + lists.shape, jnp.int32),
            pltpu.VMEM((count_c, plan.right_rows, LANES), jnp.float32),
            pltpu.VMEM((count_c, plan.left_rows, LANES), jnp.float32),
            pltpu.VMEM((n_src + 8, big, LANES), jnp.float32),
            pltpu.VMEM((2 * count_c, half, LANES), jnp.float32),
            pltpu.VMEM((2 * count_c, half, LANES), jnp.float32),
            pltpu.VMEM((2 * count_c, half, LANES), jnp.float32),
        ]
        + [pltpu.VMEM((n_src + 8, 8 * n, LANES), jnp.float32) for n in plan.sizes]
        + [pltpu.VMEM((n_vec, 8 * n, LANES), jnp.float32) for n in plan.sizes]
        + [
            pltpu.SemaphoreType.DMA((7,)),
            pltpu.SemaphoreType.DMA,
            pltpu.SemaphoreType.DMA((4,)),
            pltpu.SemaphoreType.DMA((n_chunk,)),
            pltpu.SemaphoreType.DMA((n_chunk * n_box,)),
            pltpu.SemaphoreType.DMA((n_chunk * n_box,)),
            pltpu.SemaphoreType.DMA((2 * n_chunk,)),
            pltpu.SemaphoreType.DMA((2 * n_chunk,)),
        ],
        out_shape=jax.ShapeDtypeStruct((count_c, plan.padded, LANES), jnp.float32),
        compiler_params=pltpu.CompilerParams(
            collective_id=0, has_side_effects=True, vmem_limit_bytes=58 << 20
        ),
        name="far",
    )(wide, lists, t_view)
    return separate(out, rows)


def solution(mesh):
    placed = (
        P("box", None, "samp"),
        P("box", None),
        P("box", None),
        P(),
        P(),
        P("samp"),
        P(None, "samp"),
        P("samp"),
        P(None, "samp"),
        P(None, None, "samp"),
        P("box", None),
        P("box", None),
    )
    return jax.shard_map(
        functools.partial(per_device, mesh.shape["samp"], mesh.shape["box"]),
        mesh=mesh, in_specs=placed, out_specs=P("box", None, "samp"), check_vma=False,
    )
```

```python
import functools

import jax
import jax.numpy as jnp
import numpy as np
from jax import lax
from jax.experimental import pallas as pl
from jax.experimental.layout import Layout, with_layout_constraint
from jax.experimental.pallas import tpu as pltpu
from jax.sharding import PartitionSpec as P

SIZE_B = 8
SIZE_C = 16
LANES = 128
MESH = pl.DeviceIdType.MESH
GROUP = 4
FIRST_CHUNKS = (2, 4, 4, 2, 1)
REPS = ((1, 1), (1, -1), (-1, 1), (-1, -1))


def window(first, last, n_child, n_parent):
    low = 0
    while (low - 1) * n_child // n_parent + 2 >= first:
        low -= 1
    high = 0
    while (high + 1) * n_child // n_parent - 2 <= last:
        high += 1
    return low, high + 1


def quarters(parts):
    return parts // 4 if parts % 4 == 0 else parts


def phase_table(parts, per_part, low, high, n_theta, size):
    n_phi = parts * per_part
    theta = np.pi * (np.arange(n_theta) + 0.5) / n_theta
    first = np.arange(quarters(parts))[:, None] * per_part
    phi = 2.0 * np.pi * (first + np.arange(low, high)[None]) / n_phi
    u_x = np.cos(phi)[..., None] * np.sin(theta)
    u_y = np.sin(phi)[..., None] * np.sin(theta)
    u_z = np.broadcast_to(np.cos(theta), u_x.shape)
    psi = np.stack([0.5 * np.pi * size * (s_x * u_x + s_y * u_y + u_z) for s_x, s_y in REPS], axis=2)
    return np.concatenate([np.cos(psi), np.sin(psi)], axis=2).astype(np.float32)


def octant(rep, turns):
    s_x, s_y = REPS[rep]
    for _ in range(turns):
        s_x, s_y = -s_y, s_x
    return 2 * (s_x + 1) + (s_y + 1) + 1


def split(x):
    high = x.astype(jnp.bfloat16)
    return high, (x - high.astype(jnp.float32)).astype(jnp.bfloat16)


def mm(a, b):
    return jnp.dot(a, b, preferred_element_type=jnp.float32)


def pick(index, values):
    out = jnp.int32(values[0])
    for k in range(1, len(values)):
        out = jnp.where(index == k, values[k], out)
    return out


class Plan:
    def __init__(self, n_samp, n_box, pa, pb, pc, theta_c):
        self.n_samp, self.n_box = n_samp, n_box
        self.pa, self.pb, self.pc = pa, pb, pc
        n_a, n_b, n_c = n_samp * pa, n_samp * pb, n_samp * pc
        self.low_b, self.high_b = window(0, pa - 1, n_a, n_b)
        low_c, high_c = window(self.low_b, self.high_b - 1, n_b, n_c)
        self.ext = -(-max(-low_c, high_c - pc) // GROUP) * GROUP
        self.low_c, self.high_c = -self.ext, pc + self.ext
        self.wb, self.wc = self.high_b - self.low_b, self.high_c - self.low_c
        self.unit_rows = 2 * GROUP * theta_c // LANES
        self.edge, self.inner = self.ext // GROUP, pc // GROUP
        self.rows = rows = self.inner * self.unit_rows
        ext_rows = self.edge * self.unit_rows
        self.padded = -(-rows // 8) * 8
        groups = self.padded // 8
        self.split = -(-groups // 2)
        other = groups - self.split
        self.sizes = []
        for size in FIRST_CHUNKS + (1,) * self.split:
            left = other - sum(self.sizes)
            if sum(self.sizes) < self.split:
                self.sizes.append(min(size, left) if left > 0 else 1)
        self.starts = [sum(self.sizes[:c]) for c in range(len(self.sizes))]
        ends = [a + n for a, n in zip(self.starts, self.sizes)]
        self.both = [end <= other for end in ends]
        self.local = [pl.ds(8 * a, 8 * n) for a, n in zip(self.starts, self.sizes)]
        self.end_at = (rows - ext_rows) // 8 * 8
        self.left_rows = self.padded - self.end_at
        self.left_pad = rows - ext_rows - self.end_at
        self.right_rows = -(-ext_rows // 8) * 8
        self.left_at = pl.ds(self.padded, self.left_rows)
        self.right_at = pl.ds(self.padded + self.left_rows, self.right_rows)
        self.total = self.padded + self.left_rows + self.right_rows
        touched = max(self.left_rows, self.right_rows) // 8
        self.early = sum(end <= other - touched for end in ends)
        c_low, c_high, b_low, b_high, a_low, a_high = [], [], [], [], [], []
        for c in range(self.early + 1):
            first, last = 0, self.edge * 2 + self.inner
            if c < self.early:
                first = self.edge + 8 * (self.split - ends[c]) // self.unit_rows
                last = min(last, self.edge - (-8 * (self.split + ends[c]) // self.unit_rows))
            c_low.append(first)
            c_high.append(last)
            b0, b1 = 0, self.wb
            if c < self.early:
                b0 = (self.low_c + GROUP * first) * n_b // n_c - 2 - self.low_b
                b1 = (self.low_c + GROUP * last - 1) * n_b // n_c + 3 - self.low_b
                b0, b1 = max(b0, 0), min(b1, self.wb)
            b_low.append(b0)
            b_high.append(b1)
            a0 = max((b0 + self.low_b) * n_a // n_b - 2, 0)
            a1 = min((b1 - 1 + self.low_b) * n_a // n_b + 3, pa)
            if c == self.early:
                a0, a1 = 0, pa
            a_low.append(a0 // GROUP)
            a_high.append(-(-a1 // GROUP))
        self.levels = (self.spans(a_low, a_high), self.spans(b_low, b_high), self.spans(c_low, c_high))

    @staticmethod
    def spans(low, high):
        before_low, before_high = [high[0]] + low[:-1], [high[0]] + high[:-1]
        left = [b - a for a, b in zip(low, before_low)]
        count = [n + b - a for n, a, b in zip(left, before_high, high)]
        return low, left, before_high, count


def stencil(plan, samp, start, weight):
    row = lax.broadcasted_iota(jnp.int32, start.shape, 0)
    at_b = row < 4
    n_a, n_b = plan.n_samp * plan.pa, plan.n_samp * plan.pb

    def choose(b, c):
        return jnp.where(at_b, b, c)

    tap = start + choose(row - samp * plan.pa, row - 4 - samp * plan.pb)
    count, half = choose(n_a, n_b), choose(n_a // 2, n_b // 2)
    low, high = choose(0, plan.low_b), choose(plan.pa, plan.high_b)
    centre = choose(plan.pa // 2, (plan.low_b + plan.high_b) // 2)
    for _ in range(2):
        tap = jnp.where(tap - centre > half, tap - count, tap)
        tap = jnp.where(tap - centre < -half, tap + count, tap)
    inside = (tap >= low) & (tap < high)
    return jnp.clip(tap - low, 0, high - low - 1), jnp.where(inside, weight, 0.0)


def far_kernel(
    plan, list_len,
    x_hbm, theta_ab, theta_bc, child_b, child_c, start_b, weight_b, start_c, weight_c,
    phb_hbm, phc_hbm, src_ref, vec_ref, t_hbm, o_ref,
    x_ref, grid_a, grid_b, phb, phc, tab, tbc, s_b, s_c, ints, floats, tables_i, tables_w, idx, wgt, wide,
    lists, list_all, list_smem, halo_left, halo_right, swapped, res, psend, precv, *rest,
):
    n_chunk = len(plan.sizes)
    srcs, tbufs = rest[:n_chunk], rest[n_chunk : 2 * n_chunk]
    (in_sem, table_sem, list_sem, smem_sem, halo_sem, t_sem, src_send, src_recv, p_sem, out_sem) = rest[2 * n_chunk :]
    samp, box = lax.axis_index("samp"), lax.axis_index("box")
    n_box, n_samp = plan.n_box, plan.n_samp
    n_chip = n_box // 2
    chip, core = box // 2, box % 2
    partner = chip * 2 + 1 - core
    own = wide.shape[0]
    first_end, last_end = chip == 0, chip == n_chip - 1
    is_end = first_end | last_end
    helps_first, helps_last = chip == 1, chip == n_chip - 2
    helps = helps_first | helps_last
    helped = jnp.where(helps_first, 0, n_chip - 1)
    helper = jnp.where(first_end, 1, n_chip - 2)
    left = (lax.rem(samp + n_samp - 1, n_samp), box)
    right = (lax.rem(samp + 1, n_samp), box)
    n_base = quarters(n_samp)

    in_copies = [
        pltpu.make_async_copy(x_hbm, x_ref, in_sem.at[0]),
        pltpu.make_async_copy(phb_hbm.at[lax.rem(samp, n_base)], phb, in_sem.at[1]),
        pltpu.make_async_copy(phc_hbm.at[lax.rem(samp, n_base)], phc, in_sem.at[2]),
    ]
    for copy in in_copies:
        copy.start()

    count_a, count_b, count_c = x_ref.shape[0], child_b.shape[0], child_c.shape[0]
    theta_a, theta_b = theta_ab.shape
    theta_c = theta_bc.shape[1]
    ints[1, 0:1, 0 : plan.pb] = start_b[...]
    ints[1, 1:2, 0 : plan.pc] = start_c[...]
    floats[1, 0:4, 0 : plan.pb] = weight_b[...]
    floats[1, 4:8, 0 : plan.pc] = weight_c[...]
    lists[:, 0:list_len] = src_ref[...]
    lists[:, list_len : 2 * list_len] = vec_ref[...]

    def remote(src, dst, send, recv, device):
        return pltpu.make_async_remote_copy(
            src_ref=src, dst_ref=dst, send_sem=send, recv_sem=recv, device_id=device, device_id_type=MESH
        )

    barrier = pltpu.get_barrier_semaphore()
    for other in range(n_box):
        @pl.when(box != other)
        def _():
            pl.semaphore_signal(barrier, inc=1, device_id=(samp, other), device_id_type=MESH)
    for device in (left, right):
        pl.semaphore_signal(barrier, inc=1, device_id=device, device_id_type=MESH)

    tab[...] = jnp.zeros(tab.shape, jnp.bfloat16)
    high, low = split(theta_ab[...])
    for pair in range(2):
        at = pair * (2 * theta_a - LANES)
        for k in range(2):
            rows = slice(at + k * theta_a, at + (k + 1) * theta_a)
            cols = slice(k * theta_b, (k + 1) * theta_b)
            tab[pair, 0, rows, cols] = high
            tab[pair, 1, rows, cols] = low
    high, low = split(theta_bc[...])
    tbc[0, :theta_b] = high
    tbc[0, theta_b:] = high
    tbc[1, :theta_b] = low
    tbc[1, theta_b:] = low
    turns = samp // n_base

    def one_hot(child, first, count):
        ids = child[...]
        lane = lax.broadcasted_iota(jnp.int32, (ids.shape[0], count), 1) + first
        plus, minus = [], []
        for rep in range(4):
            hots = []
            for flip in range(2):
                column = None
                for t in range(n_samp // n_base):
                    o = octant(rep, t)
                    o = 7 - o if flip else o
                    here = ids[:, o : o + 1]
                    column = here if column is None else jnp.where(turns == t, here, column)
                hots.append(jnp.where(column == lane, 1.0, 0.0))
            plus.append(hots[0] + hots[1])
            minus.append(hots[0] - hots[1])
        hot = jnp.concatenate(plus + minus, axis=0).astype(jnp.bfloat16)
        return jnp.concatenate([hot, hot], axis=1)

    s_b[...] = one_hot(child_b, box * count_a, count_a)
    s_c[...] = one_hot(child_c, box * count_b, count_b)
    wide[...] = jnp.zeros(wide.shape, jnp.float32)
    pl.semaphore_wait(barrier, n_box + 1)

    table_copies = []
    for k, ref in enumerate((ints, floats)):
        for d, (slot, device) in enumerate(((2, left), (0, right))):
            n = 4 * k + 2 * d
            table_copies.append(remote(ref.at[1], ref.at[slot], table_sem.at[n], table_sem.at[n + 1], device))
    for copy in table_copies:
        copy.start()

    def half_rows(which, c):
        count = 8 * plan.sizes[c]
        low = 8 * (plan.split - plan.starts[c]) - count
        high = 8 * (plan.split + plan.starts[c])
        return pl.ds(pl.multiple_of(jnp.where(which == 0, low, high), 8), count)

    def has(which, c):
        return (which == 0) | plan.both[c]

    def t_copy(c):
        return pltpu.make_async_copy(t_hbm.at[:, half_rows(core, c), :], tbufs[c], t_sem.at[c])

    def when_has(which, c, do):
        if plan.both[c]:
            do()
        else:
            pl.when(which == 0)(do)

    to_left = remote(wide.at[:, plan.left_at, :], halo_right, halo_sem.at[0], halo_sem.at[1], left)
    to_right = remote(wide.at[:, plan.right_at, :], halo_left, halo_sem.at[2], halo_sem.at[3], right)

    def list_copy(slot, device, k):
        return remote(lists, list_all.at[slot], list_sem.at[k], list_sem.at[3 + slot], device)

    list_copy(core, (samp, partner), 0).start()

    @pl.when(is_end)
    def _():
        for d in range(2):
            list_copy(2 + core, (samp, helper * 2 + d), 1 + d).start()

    def src_copy(c, chip_to, d):
        index = c * n_box + chip_to * 2 + d
        return remote(
            wide.at[:, half_rows(d, c), :],
            srcs[c].at[pl.ds(pl.multiple_of(own * box, 8), own)],
            src_send.at[index],
            src_recv.at[c * n_box + box],
            (samp, chip_to * 2 + d),
        )

    def send_chunk(c, act):
        def to_partner():
            act(src_copy(c, chip, 1 - core))

        when_has(1 - core, c, to_partner)
        for chip_to in range(1, n_chip - 1):
            @pl.when(chip != chip_to)
            def _():
                for d in range(2):
                    if d == 0 or plan.both[c]:
                        act(src_copy(c, chip_to, d))

    for c in range(n_chunk):
        when_has(core, c, lambda c=c: t_copy(c).start())
    list_all[core] = lists[...]

    x_rows = x_ref.reshape(count_a * x_ref.shape[1], LANES)
    wide_rows = wide.reshape(own * plan.total, LANES)
    stride_x = x_ref.shape[1]

    def theta_block(q):
        highs, lows = [], []
        for c in range(2):
            tiles = [split(x_rows[pl.ds(6 * q + 2 * j + c, count_a, stride=stride_x), :]) for j in range(3)]
            highs.append([t[0] for t in tiles])
            lows.append([t[1] for t in tiles])
        for pair in range(2):
            here = slice(pair, pair + 2)
            high = jnp.concatenate([jnp.concatenate(h[here], axis=1) for h in highs], axis=0)
            low = jnp.concatenate([jnp.concatenate(h[here], axis=1) for h in lows], axis=0)
            both = mm(high, tab[pair, 0]) + mm(low, tab[pair, 0]) + mm(high, tab[pair, 1])
            for k in range(2):
                grid_a[GROUP * q + 2 * pair + k] = both[:, k * LANES : (k + 1) * LANES]

    def taps(n, per_part, first_row):
        part = jnp.where(n >= 0, 1, 0) + jnp.where(n >= per_part, 1, 0)
        col = n + per_part * (1 - part)
        return [(idx[part, first_row + k, col], wgt[part, first_row + k, col]) for k in range(4)]

    def octants(phase, plus_r, plus_i, minus_r, minus_i, count):
        real = imag = None
        for j in range(4):
            cosine, sine = phase[j : j + 1, :], phase[4 + j : 5 + j, :]
            here = slice(j * count, (j + 1) * count)
            re = plus_r[here] * cosine - minus_i[here] * sine
            im = plus_i[here] * cosine + minus_r[here] * sine
            real, imag = (re, im) if real is None else (real + re, imag + im)
        return real, imag

    def level_b(m):
        stencil_b = taps(m + plan.low_b, plan.pb, 0)
        parts = []
        for c in range(2):
            here = slice(c * count_a, (c + 1) * count_a)
            value = None
            for at, weight in stencil_b:
                term = weight * grid_a[at, here, :]
                value = term if value is None else value + term
            parts.append(split(value))
        stacked = jnp.concatenate(
            [
                jnp.concatenate([parts[0][0], parts[1][0]], axis=1),
                jnp.concatenate([parts[0][1], parts[1][1]], axis=1),
            ],
            axis=0,
        )
        picked = mm(s_b[...], stacked)
        mid = 4 * count_b
        real, imag = octants(
            phb[m], picked[:mid, :LANES], picked[:mid, LANES:], picked[mid:, :LANES], picked[mid:, LANES:], count_b
        )
        high, low = split(jnp.concatenate([real, imag], axis=0))
        both = jnp.concatenate([high, low], axis=1)
        return mm(both, tbc[0]) + mm(high, tbc[1, :LANES])

    def level_c(g):
        reals, imags = [], []
        for i in range(GROUP):
            n = g * GROUP + i
            value = None
            for at, weight in taps(n + plan.low_c, plan.pc, 4):
                term = weight * grid_b[at]
                value = term if value is None else value + term
            high, low = split(value)
            rr = mm(s_c[...], jnp.concatenate([high[:count_b], low[:count_b]], axis=0))
            ri = mm(s_c[...], jnp.concatenate([high[count_b:], low[count_b:]], axis=0))
            mid = 4 * count_c
            real, imag = octants(phc[n], rr[:mid], ri[:mid], rr[mid:], ri[mid:], count_c)
            reals.append(real)
            imags.append(imag)
        base = jnp.where(
            g < plan.edge,
            plan.padded + plan.left_pad + g * plan.unit_rows,
            jnp.where(
                g < plan.edge + plan.inner,
                (g - plan.edge) * plan.unit_rows,
                plan.padded + plan.left_rows + (g - plan.edge - plan.inner) * plan.unit_rows,
            ),
        )
        for c, flat in enumerate((jnp.concatenate(reals, axis=1), jnp.concatenate(imags, axis=1))):
            for t in range(plan.unit_rows // 2):
                wide_rows[pl.ds(base + 2 * t + c, own, stride=plan.total), :] = flat[:, t * LANES : (t + 1) * LANES]

    for copy in table_copies:
        copy.wait_recv()
    for part in range(3):
        row = lax.broadcasted_iota(jnp.int32, ints.shape[1:], 0)
        start = jnp.where(row < 4, ints[part, 0:1, :], ints[part, 1:2, :])
        at, weight = stencil(plan, samp, start, floats[part])
        tables_i[part] = at
        tables_w[part] = weight
    to_idx = pltpu.make_async_copy(tables_i, idx, in_sem.at[3])
    to_wgt = pltpu.make_async_copy(tables_w, wgt, in_sem.at[4])
    to_idx.start()
    to_wgt.start()
    to_idx.wait()
    to_wgt.wait()
    for copy in in_copies:
        copy.wait()

    def phase(ph, carry):
        def items(level):
            low, before, after, count = (pick(ph, values) for values in plan.levels[level])
            return count, lambda i: jnp.where(i < before, low + i, after + i - before)

        count, item = items(0)

        def one_a(i, carry):
            theta_block(item(i))
            return carry

        lax.fori_loop(0, count, one_a, 0)
        count_m, item_m = items(1)

        def two_b(i, carry):
            m0, m1 = item_m(2 * i), item_m(jnp.minimum(2 * i + 1, count_m - 1))
            v0, v1 = level_b(m0), level_b(m1)
            grid_b[m0] = v0
            grid_b[m1] = v1
            return carry

        lax.fori_loop(0, pick(ph, [-(-n // 2) for n in plan.levels[1][3]]), two_b, 0)
        count_g, item_g = items(2)

        def one_c(i, carry):
            level_c(item_g(i))
            return carry

        lax.fori_loop(0, count_g, one_c, 0)
        for c in range(plan.early):
            @pl.when(ph == c)
            def _():
                send_chunk(c, lambda copy: copy.start())

        return carry

    lax.fori_loop(0, plan.early + 1, phase, 0)
    to_left.start()
    to_right.start()

    def finish_edges():
        to_left.wait_recv()
        to_right.wait_recv()
        at_end = pl.ds(plan.end_at, halo_right.shape[1])
        wide[:, at_end, :] = wide[:, at_end, :] + halo_right[...]
        at_start = pl.ds(0, halo_left.shape[1])
        wide[:, at_start, :] = wide[:, at_start, :] + halo_left[...]
        for c in range(plan.early, n_chunk):
            send_chunk(c, lambda copy: copy.start())

    list_copy(1 - core, (samp, partner), 0).wait_recv()

    @pl.when(helps)
    def _():
        for d in range(2):
            list_copy(2 + d, (samp, partner), 0).wait_recv()

    n_src = own * n_box
    low = jnp.where(last_end, n_src - 2 * own, 0)
    high = jnp.where(first_end, 2 * own, n_src)
    low_p = jnp.where(helps_first, 2 * own, 0)
    high_p = jnp.where(helps_last, n_src - 2 * own, n_src)
    lane = lax.broadcasted_iota(jnp.int32, list_all.shape[1:], 1)
    for slot in range(4):
        a, b = (low, high) if slot < 2 else (low_p, high_p)
        value = list_all[slot]
        gone = (lane < list_len) & ((value < a) | (value >= b))
        list_all[slot] = jnp.where(gone, n_src, value)
    to_smem = pltpu.make_async_copy(list_all, list_smem, smem_sem)
    to_smem.start()
    to_smem.wait()

    even = lax.rem(lax.broadcasted_iota(jnp.int32, (8, LANES), 0), 2) == 0

    def turn(x):
        return jnp.where(even, pltpu.roll(x, 7, 0), pltpu.roll(x, 1, 0))

    def gather_sum(c, slot, i):
        size = plan.sizes[c]
        by_same = [jnp.zeros((8, LANES), jnp.float32) for _ in range(size)]
        by_turned = [jnp.zeros((8, LANES), jnp.float32) for _ in range(size)]
        for l in range(list_len):
            s = list_smem[slot, i, l]
            v = list_smem[slot, i, list_len + l]
            for g in range(size):
                here = slice(8 * g, 8 * g + 8)
                t = tbufs[c][v, here, :]
                by_same[g] = by_same[g] + t * srcs[c][s, here, :]
                by_turned[g] = by_turned[g] + t * swapped[s, here, :]
        out = []
        for g in range(size):
            x, y = by_same[g], by_turned[g]
            out.append(jnp.where(even, x - pltpu.roll(x, 7, 0), y + pltpu.roll(y, 1, 0)))
        return out

    def result_copy(c):
        return remote(
            res.at[pl.ds(pl.multiple_of((1 - core) * own, 8), own), plan.local[c], :],
            o_ref.at[:, half_rows(core, c), :],
            out_sem.at[c],
            out_sem.at[n_chunk + c],
            (samp, partner),
        )

    def result_wait(c):
        return remote(
            res.at[pl.ds(pl.multiple_of((1 - core) * own, 8), own), plan.local[c], :],
            o_ref.at[:, half_rows(1 - core, c), :],
            out_sem.at[c],
            out_sem.at[n_chunk + c],
            (samp, partner),
        )

    def p_copy(c, chip_to):
        return remote(
            psend.at[:, plan.local[c], :],
            precv.at[:, plan.local[c], :],
            p_sem.at[c],
            p_sem.at[n_chunk + c],
            (samp, chip_to * 2 + core),
        )

    def one_chunk(c):
        size = plan.sizes[c]
        rows = 8 * size
        place = plan.local[c]
        srcs[c][pl.ds(pl.multiple_of(own * box, 8), own)] = wide[:, half_rows(core, c), :]
        srcs[c][pl.ds(n_src, 8)] = jnp.zeros((8, rows, LANES), jnp.float32)
        swapped[pl.ds(n_src, 8)] = jnp.zeros((8, swapped.shape[1], LANES), jnp.float32)
        t_copy(c).wait()

        def arrived(other):
            pltpu.make_async_copy(
                wide.at[:, half_rows(core, c), :],
                srcs[c].at[pl.ds(own * other, own)],
                src_recv.at[c * n_box + other],
            ).wait()

        for other in range(n_box):
            here = (box != other) & (jnp.logical_not(is_end) | (chip == other // 2))
            pl.when(here)(functools.partial(arrived, other))

        def swap_one(s, carry):
            for g in range(size):
                here = slice(8 * g, 8 * g + 8)
                swapped[s, here, :] = turn(srcs[c][s, here, :])
            return carry

        first = jnp.where(is_end, 2 * own * chip, 0)
        last = jnp.where(is_end, 2 * own * chip + 2 * own, n_src)
        lax.fori_loop(first, last, swap_one, 0)

        @pl.when(helps)
        def _():
            def one(p, carry):
                slot, i = 2 + p // own, lax.rem(p, own)
                for g, value in enumerate(gather_sum(c, slot, i)):
                    psend[p, pl.ds(place.start + 8 * g, 8), :] = value
                return carry

            lax.fori_loop(0, 2 * own, one, 0)
            p_copy(c, helped).start()

        def one(p, carry):
            slot, i = p // own, lax.rem(p, own)
            for g, value in enumerate(gather_sum(c, slot, i)):
                res[p, pl.ds(place.start + 8 * g, 8), :] = value
            return carry

        lax.fori_loop(0, 2 * own, one, 0)

    def chunk_mid(c):
        one_chunk(c)

        @pl.when(jnp.logical_not(is_end))
        def _():
            deliver_plain(c)

    def deliver_plain(c):
        place = plan.local[c]
        o_ref[:, half_rows(core, c), :] = res[pl.ds(pl.multiple_of(core * own, 8), own), place, :]
        result_copy(c).start()

    def deliver_end(c):
        place = plan.local[c]
        p_copy(c, chip).wait_recv()
        res[:, place, :] = res[:, place, :] + precv[:, place, :]
        deliver_plain(c)

    for c in range(n_chunk):
        if c == min(1, plan.early):
            finish_edges()
        when_has(core, c, lambda c=c: chunk_mid(c))

    @pl.when(is_end)
    def _():
        for c in range(n_chunk):
            when_has(core, c, lambda c=c: deliver_end(c))

    for c in range(n_chunk):
        when_has(1 - core, c, lambda c=c: result_wait(c).wait_recv())
        when_has(core, c, lambda c=c: result_copy(c).wait_send())
        send_chunk(c, lambda copy: copy.wait_send())

        @pl.when(helps)
        def _():
            when_has(core, c, lambda: p_copy(c, helped).wait_send())

    for copy in table_copies:
        copy.wait_send()
    to_left.wait_send()
    to_right.wait_send()
    list_copy(core, (samp, partner), 0).wait_send()

    @pl.when(is_end)
    def _():
        for d in range(2):
            list_copy(2 + core, (samp, helper * 2 + d), 1 + d).wait_send()


def interleave(x):
    x = x.reshape(x.shape[0], 2, -1, LANES).transpose(0, 2, 1, 3)
    x = with_layout_constraint(x, Layout(major_to_minor=(0, 1, 2, 3))).reshape(x.shape[0], -1, LANES)
    return jnp.pad(x, ((0, 0), (0, -x.shape[1] % 8), (0, 0))) if x.shape[1] % 8 else x


def separate(x, rows):
    x = x[:, :rows].reshape(x.shape[0], -1, 2, LANES)
    x = with_layout_constraint(x, Layout(major_to_minor=(0, 1, 2, 3)))
    return x.transpose(0, 2, 1, 3).reshape(x.shape[0], 2, -1)


def per_device(
    n_samp, n_box,
    pattern_a, children_b, children_c, theta_ab, theta_bc,
    phi_start_b, phi_weight_b, phi_start_c, phi_weight_c,
    translation, list_src, list_vec,
):
    count_a, count_b, count_c = pattern_a.shape[0], children_b.shape[0], children_c.shape[0]
    theta_a, theta_b = theta_ab.shape
    theta_c = theta_bc.shape[1]
    pa = pattern_a.shape[2] // theta_a
    plan = Plan(n_samp, n_box, pa, phi_start_b.shape[0], phi_start_c.shape[0], theta_c)
    phb = jnp.asarray(phase_table(n_samp, plan.pb, plan.low_b, plan.high_b, theta_b, SIZE_B))
    phc = jnp.asarray(phase_table(n_samp, plan.pc, plan.low_c, plan.high_c, theta_c, SIZE_C))
    x = interleave(pattern_a)
    t_view = interleave(translation)
    list_len = list_src.shape[1]
    n_src = count_c * n_box
    n_chunk = len(plan.sizes)
    big = 8 * max(plan.sizes)
    half = 8 * plan.split
    list_lanes = -(-2 * list_len // LANES) * LANES
    lanes = -(-max(plan.pb, plan.pc) // LANES) * LANES
    vmem = pl.BlockSpec(memory_space=pltpu.VMEM)
    hbm = pl.BlockSpec(memory_space=pl.ANY)
    f32, bf16, i32 = jnp.float32, jnp.bfloat16, jnp.int32
    out = pl.pallas_call(
        functools.partial(far_kernel, plan, list_len),
        in_specs=[hbm] + [vmem] * 8 + [hbm] * 2 + [vmem] * 2 + [hbm],
        out_specs=vmem,
        scratch_shapes=[
            pltpu.VMEM(x.shape, f32),
            pltpu.VMEM((pa, 2 * count_a, LANES), f32),
            pltpu.VMEM((plan.wb, 2 * count_b, theta_c), f32),
            pltpu.VMEM(phb.shape[1:], f32),
            pltpu.VMEM(phc.shape[1:], f32),
            pltpu.VMEM((2, 2, 2 * LANES, 2 * theta_b), bf16),
            pltpu.VMEM((2, 2 * theta_b, theta_c), bf16),
            pltpu.VMEM((8 * count_b, 2 * count_a), bf16),
            pltpu.VMEM((8 * count_c, 2 * count_b), bf16),
            pltpu.VMEM((3, 8, lanes), i32),
            pltpu.VMEM((3, 8, lanes), f32),
            pltpu.VMEM((3, 8, lanes), i32),
            pltpu.VMEM((3, 8, lanes), f32),
            pltpu.SMEM((3, 8, lanes), i32),
            pltpu.SMEM((3, 8, lanes), f32),
            pltpu.VMEM((count_c, plan.total, LANES), f32),
            pltpu.VMEM((count_c, list_lanes), i32),
            pltpu.VMEM((4, count_c, list_lanes), i32),
            pltpu.SMEM((4, count_c, list_lanes), i32),
            pltpu.VMEM((count_c, plan.right_rows, LANES), f32),
            pltpu.VMEM((count_c, plan.left_rows, LANES), f32),
            pltpu.VMEM((n_src + 8, big, LANES), f32),
            pltpu.VMEM((2 * count_c, half, LANES), f32),
            pltpu.VMEM((2 * count_c, half, LANES), f32),
            pltpu.VMEM((2 * count_c, half, LANES), f32),
        ]
        + [pltpu.VMEM((n_src + 8, 8 * n, LANES), f32) for n in plan.sizes]
        + [pltpu.VMEM((t_view.shape[0], 8 * n, LANES), f32) for n in plan.sizes]
        + [
            pltpu.SemaphoreType.DMA((5,)),
            pltpu.SemaphoreType.DMA((8,)),
            pltpu.SemaphoreType.DMA((7,)),
            pltpu.SemaphoreType.DMA,
            pltpu.SemaphoreType.DMA((4,)),
            pltpu.SemaphoreType.DMA((n_chunk,)),
            pltpu.SemaphoreType.DMA((n_chunk * n_box,)),
            pltpu.SemaphoreType.DMA((n_chunk * n_box,)),
            pltpu.SemaphoreType.DMA((2 * n_chunk,)),
            pltpu.SemaphoreType.DMA((2 * n_chunk,)),
        ],
        out_shape=jax.ShapeDtypeStruct((count_c, plan.padded, LANES), f32),
        compiler_params=pltpu.CompilerParams(
            collective_id=0, has_side_effects=True, vmem_limit_bytes=62 << 20
        ),
        name="far",
    )(
        x, theta_ab, theta_bc, children_b, children_c,
        phi_start_b.reshape(1, -1), phi_weight_b, phi_start_c.reshape(1, -1), phi_weight_c,
        phb, phc, list_src, list_vec, t_view,
    )
    return separate(out, plan.rows)


def solution(mesh):
    placed = (
        P("box", None, "samp"),
        P("box", None),
        P("box", None),
        P(),
        P(),
        P("samp"),
        P(None, "samp"),
        P("samp"),
        P(None, "samp"),
        P(None, None, "samp"),
        P("box", None),
        P("box", None),
    )
    return jax.shard_map(
        functools.partial(per_device, mesh.shape["samp"], mesh.shape["box"]),
        mesh=mesh, in_specs=placed, out_specs=P("box", None, "samp"), check_vma=False,
    )
```

```python
import functools

import jax
import jax.numpy as jnp
import numpy as np
from jax import lax
from jax.experimental import pallas as pl
from jax.experimental.layout import Layout, with_layout_constraint
from jax.experimental.pallas import tpu as pltpu
from jax.sharding import PartitionSpec as P

SIZE_B = 8
SIZE_C = 16
LANES = 128
MESH = pl.DeviceIdType.MESH
GROUP = 4
FIRST_CHUNKS = (2, 4, 3, 3, 1)
UNROLL_B = 4
UNROLL_T = 8
REPS = ((1, 1), (1, -1), (-1, 1), (-1, -1))


def window(first, last, n_child, n_parent):
    low = 0
    while (low - 1) * n_child // n_parent + 2 >= first:
        low -= 1
    high = 0
    while (high + 1) * n_child // n_parent - 2 <= last:
        high += 1
    return low, high + 1


def quarters(parts):
    return parts // 4 if parts % 4 == 0 else parts


def phase_table(parts, per_part, low, high, n_theta, size):
    n_phi = parts * per_part
    theta = np.pi * (np.arange(n_theta) + 0.5) / n_theta
    first = np.arange(quarters(parts))[:, None] * per_part
    phi = 2.0 * np.pi * (first + np.arange(low, high)[None]) / n_phi
    u_x = np.cos(phi)[..., None] * np.sin(theta)
    u_y = np.sin(phi)[..., None] * np.sin(theta)
    u_z = np.broadcast_to(np.cos(theta), u_x.shape)
    psi = np.stack([0.5 * np.pi * size * (s_x * u_x + s_y * u_y + u_z) for s_x, s_y in REPS], axis=2)
    return np.concatenate([np.cos(psi), np.sin(psi)], axis=2).astype(np.float32)


def octant(rep, turns):
    s_x, s_y = REPS[rep]
    for _ in range(turns):
        s_x, s_y = -s_y, s_x
    return 2 * (s_x + 1) + (s_y + 1) + 1


def split(x):
    high = x.astype(jnp.bfloat16)
    return high, (x - high.astype(jnp.float32)).astype(jnp.bfloat16)


def mm(a, b):
    return jnp.dot(a, b, preferred_element_type=jnp.float32)


def pick(index, values):
    out = jnp.int32(values[0])
    for k in range(1, len(values)):
        out = jnp.where(index == k, values[k], out)
    return out


class Plan:
    def __init__(self, n_samp, n_box, pa, pb, pc, theta_c):
        self.n_samp, self.n_box = n_samp, n_box
        self.pa, self.pb, self.pc = pa, pb, pc
        n_a, n_b, n_c = n_samp * pa, n_samp * pb, n_samp * pc
        self.low_b, self.high_b = window(0, pa - 1, n_a, n_b)
        low_c, high_c = window(self.low_b, self.high_b - 1, n_b, n_c)
        self.ext = -(-max(-low_c, high_c - pc) // GROUP) * GROUP
        self.low_c, self.high_c = -self.ext, pc + self.ext
        self.wb, self.wc = self.high_b - self.low_b, self.high_c - self.low_c
        self.unit_rows = 2 * GROUP * theta_c // LANES
        self.edge, self.inner = self.ext // GROUP, pc // GROUP
        self.rows = rows = self.inner * self.unit_rows
        ext_rows = self.edge * self.unit_rows
        self.padded = -(-rows // 8) * 8
        groups = self.padded // 8
        self.split = -(-groups // 2)
        other = groups - self.split
        self.sizes = []
        for size in FIRST_CHUNKS + (1,) * self.split:
            left = other - sum(self.sizes)
            if sum(self.sizes) < self.split:
                self.sizes.append(min(size, left) if left > 0 else 1)
        self.starts = [sum(self.sizes[:c]) for c in range(len(self.sizes))]
        ends = [a + n for a, n in zip(self.starts, self.sizes)]
        self.both = [end <= other for end in ends]
        self.local = [pl.ds(8 * a, 8 * n) for a, n in zip(self.starts, self.sizes)]
        self.end_at = (rows - ext_rows) // 8 * 8
        self.left_rows = self.padded - self.end_at
        self.left_pad = rows - ext_rows - self.end_at
        self.right_rows = -(-ext_rows // 8) * 8
        self.left_at = pl.ds(self.padded, self.left_rows)
        self.right_at = pl.ds(self.padded + self.left_rows, self.right_rows)
        self.total = self.padded + self.left_rows + self.right_rows
        touched = max(self.left_rows, self.right_rows) // 8
        self.early = sum(end <= other - touched for end in ends)
        c_low, c_high, b_low, b_high, a_low, a_high = [], [], [], [], [], []
        for c in range(self.early + 1):
            first, last = 0, self.edge * 2 + self.inner
            if c < self.early:
                first = self.edge + 8 * (self.split - ends[c]) // self.unit_rows
                last = min(last, self.edge - (-8 * (self.split + ends[c]) // self.unit_rows))
            c_low.append(first)
            c_high.append(last)
            b0, b1 = 0, self.wb
            if c < self.early:
                b0 = (self.low_c + GROUP * first) * n_b // n_c - 2 - self.low_b
                b1 = (self.low_c + GROUP * last - 1) * n_b // n_c + 3 - self.low_b
                b0, b1 = max(b0, 0), min(b1, self.wb)
            b_low.append(b0)
            b_high.append(b1)
            a0 = max((b0 + self.low_b) * n_a // n_b - 2, 0)
            a1 = min((b1 - 1 + self.low_b) * n_a // n_b + 3, pa)
            if c == self.early:
                a0, a1 = 0, pa
            a_low.append(a0 // GROUP)
            a_high.append(-(-a1 // GROUP))
        self.levels = (self.spans(a_low, a_high), self.spans(b_low, b_high), self.spans(c_low, c_high))

    @staticmethod
    def spans(low, high):
        before_low, before_high = [high[0]] + low[:-1], [high[0]] + high[:-1]
        left = [b - a for a, b in zip(low, before_low)]
        count = [n + b - a for n, a, b in zip(left, before_high, high)]
        return low, left, before_high, count


def stencil(plan, samp, start, weight):
    row = lax.broadcasted_iota(jnp.int32, start.shape, 0)
    at_b = row < 4
    n_a, n_b = plan.n_samp * plan.pa, plan.n_samp * plan.pb

    def choose(b, c):
        return jnp.where(at_b, b, c)

    tap = start + choose(row - samp * plan.pa, row - 4 - samp * plan.pb)
    count, half = choose(n_a, n_b), choose(n_a // 2, n_b // 2)
    low, high = choose(0, plan.low_b), choose(plan.pa, plan.high_b)
    centre = choose(plan.pa // 2, (plan.low_b + plan.high_b) // 2)
    for _ in range(2):
        tap = jnp.where(tap - centre > half, tap - count, tap)
        tap = jnp.where(tap - centre < -half, tap + count, tap)
    inside = (tap >= low) & (tap < high)
    return jnp.clip(tap - low, 0, high - low - 1), jnp.where(inside, weight, 0.0)


def far_kernel(
    plan, list_len,
    x_hbm, theta_ab, theta_bc, child_b, child_c, start_b, weight_b, start_c, weight_c,
    phb_hbm, phc_hbm, src_ref, vec_ref, t_hbm, o_ref,
    x_ref, grid_a, pattern_b, grid_b, phb, phc, tab, tbc, s_b, s_c, ints, floats, tables_i, tables_w, idx, wgt, wide,
    lists, list_all, list_smem, halo_left, halo_right, swapped, res, psend, precv, *rest,
):
    n_chunk = len(plan.sizes)
    srcs, tbufs = rest[:n_chunk], rest[n_chunk : 2 * n_chunk]
    (in_sem, table_sem, list_sem, smem_sem, halo_sem, t_sem, src_send, src_recv, p_sem, out_sem) = rest[2 * n_chunk :]
    samp, box = lax.axis_index("samp"), lax.axis_index("box")
    n_box, n_samp = plan.n_box, plan.n_samp
    n_chip = n_box // 2
    chip, core = box // 2, box % 2
    partner = chip * 2 + 1 - core
    own = wide.shape[0]
    first_end, last_end = chip == 0, chip == n_chip - 1
    is_end = first_end | last_end
    helps_first, helps_last = chip == 1, chip == n_chip - 2
    helps = helps_first | helps_last
    helped = jnp.where(helps_first, 0, n_chip - 1)
    helper = jnp.where(first_end, 1, n_chip - 2)
    left = (lax.rem(samp + n_samp - 1, n_samp), box)
    right = (lax.rem(samp + 1, n_samp), box)
    n_base = quarters(n_samp)

    in_copies = [
        pltpu.make_async_copy(x_hbm, x_ref, in_sem.at[0]),
        pltpu.make_async_copy(phb_hbm.at[lax.rem(samp, n_base)], phb, in_sem.at[1]),
        pltpu.make_async_copy(phc_hbm.at[lax.rem(samp, n_base)], phc, in_sem.at[2]),
    ]
    for copy in in_copies:
        copy.start()

    count_a, count_b, count_c = x_ref.shape[0], child_b.shape[1], child_c.shape[0]
    theta_a, theta_b = theta_ab.shape
    theta_c = theta_bc.shape[0]
    ints[1, 0:1, 0 : plan.pb] = start_b[...]
    ints[1, 1:2, 0 : plan.pc] = start_c[...]
    floats[1, 0:4, 0 : plan.pb] = weight_b[...]
    floats[1, 4:8, 0 : plan.pc] = weight_c[...]
    lists[:, 0:list_len] = src_ref[...]
    lists[:, list_len : 2 * list_len] = vec_ref[...]

    def remote(src, dst, send, recv, device):
        return pltpu.make_async_remote_copy(
            src_ref=src, dst_ref=dst, send_sem=send, recv_sem=recv, device_id=device, device_id_type=MESH
        )

    barrier = pltpu.get_barrier_semaphore()
    for other in range(n_box):
        @pl.when(box != other)
        def _():
            pl.semaphore_signal(barrier, inc=1, device_id=(samp, other), device_id_type=MESH)
    for device in (left, right):
        pl.semaphore_signal(barrier, inc=1, device_id=device, device_id_type=MESH)

    tab[...] = jnp.zeros(tab.shape, jnp.bfloat16)
    high, low = split(theta_ab[...])
    for pair in range(2):
        at = pair * (2 * theta_a - LANES)
        for k in range(2):
            rows = slice(at + k * theta_a, at + (k + 1) * theta_a)
            cols = slice(k * theta_b, (k + 1) * theta_b)
            tab[pair, 0, rows, cols] = high
            tab[pair, 1, rows, cols] = low
    high, low = split(theta_bc[...].T)
    tbc[0, :theta_b] = high
    tbc[0, theta_b:] = high
    tbc[1, :theta_b] = low
    tbc[1, theta_b:] = low
    turns = samp // n_base

    def one_hot(ids, first, count):
        lane = lax.broadcasted_iota(jnp.int32, (ids.shape[0], count), 1) + first
        plus, minus = [], []
        for rep in range(4):
            hots = []
            for flip in range(2):
                column = None
                for t in range(n_samp // n_base):
                    o = octant(rep, t)
                    o = 7 - o if flip else o
                    here = ids[:, o : o + 1]
                    column = here if column is None else jnp.where(turns == t, here, column)
                hots.append(jnp.where(column == lane, 1.0, 0.0))
            plus.append(hots[0] + hots[1])
            minus.append(hots[0] - hots[1])
        hot = jnp.concatenate(plus + minus, axis=0).astype(jnp.bfloat16)
        return jnp.concatenate([hot, hot], axis=1)

    s_b[...] = one_hot(child_b[...].T, box * count_a, count_a)
    s_c[...] = one_hot(child_c[...], box * count_b, count_b)
    wide[...] = jnp.zeros(wide.shape, jnp.float32)
    pl.semaphore_wait(barrier, n_box + 1)

    table_copies = []
    for k, ref in enumerate((ints, floats)):
        for d, (slot, device) in enumerate(((2, left), (0, right))):
            n = 4 * k + 2 * d
            table_copies.append(remote(ref.at[1], ref.at[slot], table_sem.at[n], table_sem.at[n + 1], device))
    for copy in table_copies:
        copy.start()

    def half_rows(which, c):
        count = 8 * plan.sizes[c]
        low = 8 * (plan.split - plan.starts[c]) - count
        high = 8 * (plan.split + plan.starts[c])
        return pl.ds(pl.multiple_of(jnp.where(which == 0, low, high), 8), count)

    def has(which, c):
        return (which == 0) | plan.both[c]

    def t_copy(c):
        return pltpu.make_async_copy(t_hbm.at[:, half_rows(core, c), :], tbufs[c], t_sem.at[c])

    def when_has(which, c, do):
        if plan.both[c]:
            do()
        else:
            pl.when(which == 0)(do)

    to_left = remote(wide.at[:, plan.left_at, :], halo_right, halo_sem.at[0], halo_sem.at[1], left)
    to_right = remote(wide.at[:, plan.right_at, :], halo_left, halo_sem.at[2], halo_sem.at[3], right)

    def list_copy(slot, device, k):
        return remote(lists, list_all.at[slot], list_sem.at[k], list_sem.at[3 + slot], device)

    list_copy(core, (samp, partner), 0).start()

    @pl.when(is_end)
    def _():
        for d in range(2):
            list_copy(2 + core, (samp, helper * 2 + d), 1 + d).start()

    def src_copy(c, chip_to, d):
        index = c * n_box + chip_to * 2 + d
        return remote(
            wide.at[:, half_rows(d, c), :],
            srcs[c].at[pl.ds(pl.multiple_of(own * box, 8), own)],
            src_send.at[index],
            src_recv.at[c * n_box + box],
            (samp, chip_to * 2 + d),
        )

    def send_chunk(c, act):
        def to_partner():
            act(src_copy(c, chip, 1 - core))

        when_has(1 - core, c, to_partner)
        for chip_to in range(1, n_chip - 1):
            @pl.when(chip != chip_to)
            def _():
                for d in range(2):
                    if d == 0 or plan.both[c]:
                        act(src_copy(c, chip_to, d))

    for c in range(n_chunk):
        when_has(core, c, lambda c=c: t_copy(c).start())
    list_all[core] = lists[...]

    x_rows = x_ref.reshape(count_a * x_ref.shape[1], LANES)
    wide_rows = wide.reshape(own * plan.total, LANES)
    stride_x = x_ref.shape[1]

    def theta_block(q):
        highs, lows = [], []
        for c in range(2):
            tiles = [split(x_rows[pl.ds(6 * q + 2 * j + c, count_a, stride=stride_x), :]) for j in range(3)]
            highs.append([t[0] for t in tiles])
            lows.append([t[1] for t in tiles])
        for pair in range(2):
            here = slice(pair, pair + 2)
            high = jnp.concatenate([jnp.concatenate(h[here], axis=1) for h in highs], axis=0)
            low = jnp.concatenate([jnp.concatenate(h[here], axis=1) for h in lows], axis=0)
            both = mm(high, tab[pair, 0]) + mm(low, tab[pair, 0]) + mm(high, tab[pair, 1])
            for k in range(2):
                grid_a[GROUP * q + 2 * pair + k] = both[:, k * LANES : (k + 1) * LANES]

    def taps(n, per_part, first_row):
        part = jnp.where(n >= 0, 1, 0) + jnp.where(n >= per_part, 1, 0)
        col = n + per_part * (1 - part)
        return [(idx[part, first_row + k, col], wgt[part, first_row + k, col]) for k in range(4)]

    def octants(phase, plus_r, plus_i, minus_r, minus_i, count):
        real = imag = None
        for j in range(4):
            cosine, sine = phase[j : j + 1, :], phase[4 + j : 5 + j, :]
            here = slice(j * count, (j + 1) * count)
            re = plus_r[here] * cosine - minus_i[here] * sine
            im = plus_i[here] * cosine + minus_r[here] * sine
            real, imag = (re, im) if real is None else (real + re, imag + im)
        return real, imag

    def level_b(m):
        stencil_b = taps(m + plan.low_b, plan.pb, 0)
        parts = []
        for c in range(2):
            here = slice(c * count_a, (c + 1) * count_a)
            value = None
            for at, weight in stencil_b:
                term = weight * grid_a[at, here, :]
                value = term if value is None else value + term
            parts.append(split(value))
        stacked = jnp.concatenate(
            [
                jnp.concatenate([parts[0][0], parts[1][0]], axis=1),
                jnp.concatenate([parts[0][1], parts[1][1]], axis=1),
            ],
            axis=0,
        )
        picked = mm(s_b[...], stacked)
        mid = 4 * count_b
        real, imag = octants(
            phb[m], picked[:mid, :LANES], picked[:mid, LANES:], picked[mid:, :LANES], picked[mid:, LANES:], count_b
        )
        high, low = split(jnp.concatenate([real, imag], axis=0))
        return jnp.concatenate([high, low], axis=1)

    def level_c(g):
        reals, imags = [], []
        for i in range(GROUP):
            n = g * GROUP + i
            value = None
            for at, weight in taps(n + plan.low_c, plan.pc, 4):
                term = weight * grid_b[at]
                value = term if value is None else value + term
            high, low = split(value)
            rr = mm(s_c[...], jnp.concatenate([high[:count_b], low[:count_b]], axis=0))
            ri = mm(s_c[...], jnp.concatenate([high[count_b:], low[count_b:]], axis=0))
            mid = 4 * count_c
            real, imag = octants(phc[n], rr[:mid], ri[:mid], rr[mid:], ri[mid:], count_c)
            reals.append(real)
            imags.append(imag)
        base = jnp.where(
            g < plan.edge,
            plan.padded + plan.left_pad + g * plan.unit_rows,
            jnp.where(
                g < plan.edge + plan.inner,
                (g - plan.edge) * plan.unit_rows,
                plan.padded + plan.left_rows + (g - plan.edge - plan.inner) * plan.unit_rows,
            ),
        )
        for c, flat in enumerate((jnp.concatenate(reals, axis=1), jnp.concatenate(imags, axis=1))):
            for t in range(plan.unit_rows // 2):
                wide_rows[pl.ds(base + 2 * t + c, own, stride=plan.total), :] = flat[:, t * LANES : (t + 1) * LANES]

    for copy in table_copies:
        copy.wait_recv()
    for part in range(3):
        row = lax.broadcasted_iota(jnp.int32, ints.shape[1:], 0)
        start = jnp.where(row < 4, ints[part, 0:1, :], ints[part, 1:2, :])
        at, weight = stencil(plan, samp, start, floats[part])
        tables_i[part] = at
        tables_w[part] = weight
    to_idx = pltpu.make_async_copy(tables_i, idx, in_sem.at[3])
    to_wgt = pltpu.make_async_copy(tables_w, wgt, in_sem.at[4])
    to_idx.start()
    to_wgt.start()
    to_idx.wait()
    to_wgt.wait()
    for copy in in_copies:
        copy.wait()

    def phase(ph, carry):
        def items(level):
            low, before, after, count = (pick(ph, values) for values in plan.levels[level])
            return count, lambda i: jnp.where(i < before, low + i, after + i - before)

        count, item = items(0)

        def one_a(i, carry):
            theta_block(item(i))
            return carry

        lax.fori_loop(0, count, one_a, 0)
        count_m, item_m = items(1)

        def some_m(i, n):
            return [item_m(jnp.minimum(n * i + k, count_m - 1)) for k in range(n)]

        def one_b(i, carry):
            at = some_m(i, UNROLL_B)
            values = [level_b(m) for m in at]
            for m, value in zip(at, values):
                pattern_b[m] = value
            return carry

        def one_theta(i, carry):
            at = some_m(i, UNROLL_T)
            both = jnp.concatenate([pattern_b[m] for m in at], axis=0)
            grid = mm(both, tbc[0]) + mm(both[:, :LANES], tbc[1, :LANES])
            for k, m in enumerate(at):
                grid_b[m] = grid[2 * count_b * k : 2 * count_b * (k + 1)]
            return carry

        lax.fori_loop(0, pick(ph, [-(-n // UNROLL_B) for n in plan.levels[1][3]]), one_b, 0)
        lax.fori_loop(0, pick(ph, [-(-n // UNROLL_T) for n in plan.levels[1][3]]), one_theta, 0)
        count_g, item_g = items(2)

        def one_c(i, carry):
            level_c(item_g(i))
            return carry

        lax.fori_loop(0, count_g, one_c, 0)
        for c in range(plan.early):
            @pl.when(ph == c)
            def _():
                send_chunk(c, lambda copy: copy.start())

        return carry

    lax.fori_loop(0, plan.early + 1, phase, 0)
    to_left.start()
    to_right.start()

    def finish_edges():
        to_left.wait_recv()
        to_right.wait_recv()
        at_end = pl.ds(plan.end_at, halo_right.shape[1])
        wide[:, at_end, :] = wide[:, at_end, :] + halo_right[...]
        at_start = pl.ds(0, halo_left.shape[1])
        wide[:, at_start, :] = wide[:, at_start, :] + halo_left[...]
        for c in range(plan.early, n_chunk):
            send_chunk(c, lambda copy: copy.start())

    list_copy(1 - core, (samp, partner), 0).wait_recv()

    @pl.when(helps)
    def _():
        for d in range(2):
            list_copy(2 + d, (samp, partner), 0).wait_recv()

    n_src = own * n_box
    low = jnp.where(last_end, n_src - 2 * own, 0)
    high = jnp.where(first_end, 2 * own, n_src)
    low_p = jnp.where(helps_first, 2 * own, 0)
    high_p = jnp.where(helps_last, n_src - 2 * own, n_src)
    lane = lax.broadcasted_iota(jnp.int32, list_all.shape[1:], 1)
    for slot in range(4):
        a, b = (low, high) if slot < 2 else (low_p, high_p)
        value = list_all[slot]
        gone = (lane < list_len) & ((value < a) | (value >= b))
        list_all[slot] = jnp.where(gone, n_src, value)
    to_smem = pltpu.make_async_copy(list_all, list_smem, smem_sem)
    to_smem.start()
    to_smem.wait()

    even = lax.rem(lax.broadcasted_iota(jnp.int32, (8, LANES), 0), 2) == 0

    def turn(x):
        return jnp.where(even, pltpu.roll(x, 7, 0), pltpu.roll(x, 1, 0))

    def gather_sum(c, slot, i):
        size = plan.sizes[c]
        by_same = [jnp.zeros((8, LANES), jnp.float32) for _ in range(size)]
        by_turned = [jnp.zeros((8, LANES), jnp.float32) for _ in range(size)]
        for l in range(list_len):
            s = list_smem[slot, i, l]
            v = list_smem[slot, i, list_len + l]
            for g in range(size):
                here = slice(8 * g, 8 * g + 8)
                t = tbufs[c][v, here, :]
                by_same[g] = by_same[g] + t * srcs[c][s, here, :]
                by_turned[g] = by_turned[g] + t * swapped[s, here, :]
        out = []
        for g in range(size):
            x, y = by_same[g], by_turned[g]
            out.append(jnp.where(even, x - pltpu.roll(x, 7, 0), y + pltpu.roll(y, 1, 0)))
        return out

    def result_copy(c):
        return remote(
            res.at[pl.ds(pl.multiple_of((1 - core) * own, 8), own), plan.local[c], :],
            o_ref.at[:, half_rows(core, c), :],
            out_sem.at[c],
            out_sem.at[n_chunk + c],
            (samp, partner),
        )

    def result_wait(c):
        return remote(
            res.at[pl.ds(pl.multiple_of((1 - core) * own, 8), own), plan.local[c], :],
            o_ref.at[:, half_rows(1 - core, c), :],
            out_sem.at[c],
            out_sem.at[n_chunk + c],
            (samp, partner),
        )

    def p_copy(c, chip_to):
        return remote(
            psend.at[:, plan.local[c], :],
            precv.at[:, plan.local[c], :],
            p_sem.at[c],
            p_sem.at[n_chunk + c],
            (samp, chip_to * 2 + core),
        )

    def one_chunk(c):
        size = plan.sizes[c]
        rows = 8 * size
        place = plan.local[c]
        srcs[c][pl.ds(pl.multiple_of(own * box, 8), own)] = wide[:, half_rows(core, c), :]
        srcs[c][pl.ds(n_src, 8)] = jnp.zeros((8, rows, LANES), jnp.float32)
        swapped[pl.ds(n_src, 8)] = jnp.zeros((8, swapped.shape[1], LANES), jnp.float32)
        t_copy(c).wait()

        def arrived(other):
            pltpu.make_async_copy(
                wide.at[:, half_rows(core, c), :],
                srcs[c].at[pl.ds(own * other, own)],
                src_recv.at[c * n_box + other],
            ).wait()

        for other in range(n_box):
            here = (box != other) & (jnp.logical_not(is_end) | (chip == other // 2))
            pl.when(here)(functools.partial(arrived, other))

        def swap_one(s, carry):
            for g in range(size):
                here = slice(8 * g, 8 * g + 8)
                swapped[s, here, :] = turn(srcs[c][s, here, :])
            return carry

        first = jnp.where(is_end, 2 * own * chip, 0)
        last = jnp.where(is_end, 2 * own * chip + 2 * own, n_src)
        lax.fori_loop(first, last, swap_one, 0)

        @pl.when(helps)
        def _():
            def one(p, carry):
                slot, i = 2 + p // own, lax.rem(p, own)
                for g, value in enumerate(gather_sum(c, slot, i)):
                    psend[p, pl.ds(place.start + 8 * g, 8), :] = value
                return carry

            lax.fori_loop(0, 2 * own, one, 0)
            p_copy(c, helped).start()

        def one(p, carry):
            slot, i = p // own, lax.rem(p, own)
            for g, value in enumerate(gather_sum(c, slot, i)):
                res[p, pl.ds(place.start + 8 * g, 8), :] = value
            return carry

        lax.fori_loop(0, 2 * own, one, 0)

    def chunk_mid(c):
        one_chunk(c)

        @pl.when(jnp.logical_not(is_end))
        def _():
            deliver_plain(c)

    def deliver_plain(c):
        place = plan.local[c]
        o_ref[:, half_rows(core, c), :] = res[pl.ds(pl.multiple_of(core * own, 8), own), place, :]
        result_copy(c).start()

    def deliver_end(c):
        place = plan.local[c]
        p_copy(c, chip).wait_recv()
        res[:, place, :] = res[:, place, :] + precv[:, place, :]
        deliver_plain(c)

    for c in range(n_chunk):
        if c == min(1, plan.early):
            finish_edges()
        when_has(core, c, lambda c=c: chunk_mid(c))

    @pl.when(is_end)
    def _():
        for c in range(n_chunk):
            when_has(core, c, lambda c=c: deliver_end(c))

    for c in range(n_chunk):
        when_has(1 - core, c, lambda c=c: result_wait(c).wait_recv())
        when_has(core, c, lambda c=c: result_copy(c).wait_send())
        send_chunk(c, lambda copy: copy.wait_send())

        @pl.when(helps)
        def _():
            when_has(core, c, lambda: p_copy(c, helped).wait_send())

    for copy in table_copies:
        copy.wait_send()
    to_left.wait_send()
    to_right.wait_send()
    list_copy(core, (samp, partner), 0).wait_send()

    @pl.when(is_end)
    def _():
        for d in range(2):
            list_copy(2 + core, (samp, helper * 2 + d), 1 + d).wait_send()


def interleave(x):
    x = x.reshape(x.shape[0], 2, -1, LANES).transpose(0, 2, 1, 3)
    x = with_layout_constraint(x, Layout(major_to_minor=(0, 1, 2, 3))).reshape(x.shape[0], -1, LANES)
    return jnp.pad(x, ((0, 0), (0, -x.shape[1] % 8), (0, 0))) if x.shape[1] % 8 else x


def separate(x, rows):
    x = x[:, :rows].reshape(x.shape[0], -1, 2, LANES)
    x = with_layout_constraint(x, Layout(major_to_minor=(0, 1, 2, 3)))
    return x.transpose(0, 2, 1, 3).reshape(x.shape[0], 2, -1)


def per_device(
    n_samp, n_box,
    pattern_a, children_b, children_c, theta_ab, theta_bc,
    phi_start_b, phi_weight_b, phi_start_c, phi_weight_c,
    translation, list_src, list_vec,
):
    count_a, count_b, count_c = pattern_a.shape[0], children_b.shape[0], children_c.shape[0]
    theta_a, theta_b = theta_ab.shape
    theta_c = theta_bc.shape[1]
    pa = pattern_a.shape[2] // theta_a
    plan = Plan(n_samp, n_box, pa, phi_start_b.shape[0], phi_start_c.shape[0], theta_c)
    phb = jnp.asarray(phase_table(n_samp, plan.pb, plan.low_b, plan.high_b, theta_b, SIZE_B))
    phc = jnp.asarray(phase_table(n_samp, plan.pc, plan.low_c, plan.high_c, theta_c, SIZE_C))
    x = interleave(pattern_a)
    t_view = interleave(translation)
    list_len = list_src.shape[1]
    n_src = count_c * n_box
    n_chunk = len(plan.sizes)
    big = 8 * max(plan.sizes)
    half = 8 * plan.split
    list_lanes = -(-2 * list_len // LANES) * LANES
    lanes = -(-max(plan.pb, plan.pc) // LANES) * LANES
    vmem = pl.BlockSpec(memory_space=pltpu.VMEM)
    hbm = pl.BlockSpec(memory_space=pl.ANY)
    f32, bf16, i32 = jnp.float32, jnp.bfloat16, jnp.int32
    out = pl.pallas_call(
        functools.partial(far_kernel, plan, list_len),
        in_specs=[hbm] + [vmem] * 8 + [hbm] * 2 + [vmem] * 2 + [hbm],
        out_specs=vmem,
        scratch_shapes=[
            pltpu.VMEM(x.shape, f32),
            pltpu.VMEM((pa, 2 * count_a, LANES), f32),
            pltpu.VMEM((plan.wb, 2 * count_b, 2 * theta_b), bf16),
            pltpu.VMEM((plan.wb, 2 * count_b, theta_c), f32),
            pltpu.VMEM(phb.shape[1:], f32),
            pltpu.VMEM(phc.shape[1:], f32),
            pltpu.VMEM((2, 2, 2 * LANES, 2 * theta_b), bf16),
            pltpu.VMEM((2, 2 * theta_b, theta_c), bf16),
            pltpu.VMEM((8 * count_b, 2 * count_a), bf16),
            pltpu.VMEM((8 * count_c, 2 * count_b), bf16),
            pltpu.VMEM((3, 8, lanes), i32),
            pltpu.VMEM((3, 8, lanes), f32),
            pltpu.VMEM((3, 8, lanes), i32),
            pltpu.VMEM((3, 8, lanes), f32),
            pltpu.SMEM((3, 8, lanes), i32),
            pltpu.SMEM((3, 8, lanes), f32),
            pltpu.VMEM((count_c, plan.total, LANES), f32),
            pltpu.VMEM((count_c, list_lanes), i32),
            pltpu.VMEM((4, count_c, list_lanes), i32),
            pltpu.SMEM((4, count_c, list_lanes), i32),
            pltpu.VMEM((count_c, plan.right_rows, LANES), f32),
            pltpu.VMEM((count_c, plan.left_rows, LANES), f32),
            pltpu.VMEM((n_src + 8, big, LANES), f32),
            pltpu.VMEM((2 * count_c, half, LANES), f32),
            pltpu.VMEM((2 * count_c, half, LANES), f32),
            pltpu.VMEM((2 * count_c, half, LANES), f32),
        ]
        + [pltpu.VMEM((n_src + 8, 8 * n, LANES), f32) for n in plan.sizes]
        + [pltpu.VMEM((t_view.shape[0], 8 * n, LANES), f32) for n in plan.sizes]
        + [
            pltpu.SemaphoreType.DMA((5,)),
            pltpu.SemaphoreType.DMA((8,)),
            pltpu.SemaphoreType.DMA((7,)),
            pltpu.SemaphoreType.DMA,
            pltpu.SemaphoreType.DMA((4,)),
            pltpu.SemaphoreType.DMA((n_chunk,)),
            pltpu.SemaphoreType.DMA((n_chunk * n_box,)),
            pltpu.SemaphoreType.DMA((n_chunk * n_box,)),
            pltpu.SemaphoreType.DMA((2 * n_chunk,)),
            pltpu.SemaphoreType.DMA((2 * n_chunk,)),
        ],
        out_shape=jax.ShapeDtypeStruct((count_c, plan.padded, LANES), f32),
        compiler_params=pltpu.CompilerParams(
            collective_id=0, has_side_effects=True, vmem_limit_bytes=62 << 20
        ),
        name="far",
    )(
        x, theta_ab, theta_bc.T, children_b.T, children_c,
        phi_start_b.reshape(1, -1), phi_weight_b, phi_start_c.reshape(1, -1), phi_weight_c,
        phb, phc, list_src, list_vec, t_view,
    )
    return separate(out, plan.rows)


def solution(mesh):
    placed = (
        P("box", None, "samp"),
        P("box", None),
        P("box", None),
        P(),
        P(),
        P("samp"),
        P(None, "samp"),
        P("samp"),
        P(None, "samp"),
        P(None, None, "samp"),
        P("box", None),
        P("box", None),
    )
    return jax.shard_map(
        functools.partial(per_device, mesh.shape["samp"], mesh.shape["box"]),
        mesh=mesh, in_specs=placed, out_specs=P("box", None, "samp"), check_vma=False,
    )
```

```python
import functools

import jax
import jax.numpy as jnp
import numpy as np
from jax import lax
from jax.experimental import pallas as pl
from jax.experimental.layout import Layout, with_layout_constraint
from jax.experimental.pallas import tpu as pltpu
from jax.sharding import PartitionSpec as P

SIZE_B = 8
SIZE_C = 16
LANES = 128
MESH = pl.DeviceIdType.MESH
GROUP = 4
CHUNKS = ((1, 2), (3,), (3,), (2,), (1,), (1,))
UNROLL_B = 6
UNROLL_T = 6
REPS = ((1, 1), (1, -1), (-1, 1), (-1, -1))


def window(first, last, n_child, n_parent):
    low = 0
    while (low - 1) * n_child // n_parent + 2 >= first:
        low -= 1
    high = 0
    while (high + 1) * n_child // n_parent - 2 <= last:
        high += 1
    return low, high + 1


def quarters(parts):
    return parts // 4 if parts % 4 == 0 else parts


def phase_table(parts, per_part, low, high, n_theta, size):
    n_phi = parts * per_part
    theta = np.pi * (np.arange(n_theta) + 0.5) / n_theta
    first = np.arange(quarters(parts))[:, None] * per_part
    phi = 2.0 * np.pi * (first + np.arange(low, high)[None]) / n_phi
    u_x = np.cos(phi)[..., None] * np.sin(theta)
    u_y = np.sin(phi)[..., None] * np.sin(theta)
    u_z = np.broadcast_to(np.cos(theta), u_x.shape)
    psi = np.stack([0.5 * np.pi * size * (s_x * u_x + s_y * u_y + u_z) for s_x, s_y in REPS], axis=2)
    return np.concatenate([np.cos(psi), np.sin(psi)], axis=2).astype(np.float32)


def octant(rep, turns):
    s_x, s_y = REPS[rep]
    for _ in range(turns):
        s_x, s_y = -s_y, s_x
    return 2 * (s_x + 1) + (s_y + 1) + 1


def split(x):
    high = x.astype(jnp.bfloat16)
    return high, (x - high.astype(jnp.float32)).astype(jnp.bfloat16)


def mm(a, b):
    return jnp.dot(a, b, preferred_element_type=jnp.float32)


def pick(index, values):
    if isinstance(index, int):
        return values[index]
    out = jnp.int32(values[0])
    for k in range(1, len(values)):
        out = jnp.where(index == k, values[k], out)
    return out


class Plan:
    def __init__(self, n_samp, n_box, pa, pb, pc, theta_c):
        self.n_samp, self.n_box = n_samp, n_box
        self.pa, self.pb, self.pc = pa, pb, pc
        n_a, n_b, n_c = n_samp * pa, n_samp * pb, n_samp * pc
        self.low_b, self.high_b = window(0, pa - 1, n_a, n_b)
        low_c, high_c = window(self.low_b, self.high_b - 1, n_b, n_c)
        self.ext = -(-max(-low_c, high_c - pc) // GROUP) * GROUP
        self.low_c, self.high_c = -self.ext, pc + self.ext
        self.wb, self.wc = self.high_b - self.low_b, self.high_c - self.low_c
        self.unit_rows = 2 * GROUP * theta_c // LANES
        self.edge, self.inner = self.ext // GROUP, pc // GROUP
        self.rows = rows = self.inner * self.unit_rows
        ext_rows = self.edge * self.unit_rows
        self.padded = -(-rows // 8) * 8
        groups = self.padded // 8
        self.split = -(-groups // 2)
        other = groups - self.split
        self.end_at = (rows - ext_rows) // 8 * 8
        self.left_rows = self.padded - self.end_at
        self.left_pad = rows - ext_rows - self.end_at
        self.right_rows = -(-ext_rows // 8) * 8
        self.left_at = pl.ds(self.padded, self.left_rows)
        self.right_at = pl.ds(self.padded + self.left_rows, self.right_rows)
        self.total = self.padded + self.left_rows + self.right_rows
        touched = max(self.left_rows, self.right_rows) // 8
        self.sizes, self.blocks = [], []
        for block in CHUNKS + ((1,),) * self.split:
            members = []
            for size in block:
                left = other - sum(self.sizes) - (0 if self.blocks else touched)
                if sum(self.sizes) < self.split and (left > 0 or self.blocks and not members):
                    members.append(len(self.sizes))
                    self.sizes.append(min(size, left) if left > 0 else 1)
            if members:
                self.blocks.append(members)
        self.starts = [sum(self.sizes[:c]) for c in range(len(self.sizes))]
        ends = [a + n for a, n in zip(self.starts, self.sizes)]
        self.both = [end <= other for end in ends]
        self.block_of = [k for k, members in enumerate(self.blocks) for _ in members]
        self.block_starts = [self.starts[members[0]] for members in self.blocks]
        self.block_sizes = [sum(self.sizes[c] for c in members) for members in self.blocks]
        self.block_both = [self.both[members[0]] for members in self.blocks]
        self.local = [pl.ds(8 * a, 8 * n) for a, n in zip(self.block_starts, self.block_sizes)]
        self.early = sum(end <= other - touched for end in ends)
        c_low, c_high, b_low, b_high, a_low, a_high = [], [], [], [], [], []
        for c in range(self.early + 1):
            first, last = 0, self.edge * 2 + self.inner
            if c < self.early:
                first = self.edge + 8 * (self.split - ends[c]) // self.unit_rows
                last = min(last, self.edge - (-8 * (self.split + ends[c]) // self.unit_rows))
            c_low.append(first)
            c_high.append(last)
            b0, b1 = 0, self.wb
            if c < self.early:
                b0 = (self.low_c + GROUP * first) * n_b // n_c - 2 - self.low_b
                b1 = (self.low_c + GROUP * last - 1) * n_b // n_c + 3 - self.low_b
                b0, b1 = max(b0, 0), min(b1, self.wb)
                if c:
                    b0, b1 = min(b0, b_low[-1]), max(b1, b_high[-1])
                inside_low, inside_high = -self.low_b, pb - self.low_b
                more = -(b1 - b0 - (b_high[-1] - b_low[-1] if c else 0)) % UNROLL_B
                for k in range(more):
                    if (k % 2 == 0 or b1 >= inside_high) and b0 > inside_low:
                        b0 -= 1
                    elif b1 < inside_high:
                        b1 += 1
            b_low.append(b0)
            b_high.append(b1)
            a0 = max((b0 + self.low_b) * n_a // n_b - 2, 0)
            a1 = min((b1 - 1 + self.low_b) * n_a // n_b + 3, pa)
            if c == self.early:
                a0, a1 = 0, pa
            a_low.append(a0 // GROUP)
            a_high.append(-(-a1 // GROUP))
        inside = [
            b0 + self.low_b >= 0 and b1 + self.low_b <= pb and self.edge <= c0 and c1 <= self.edge + self.inner
            for b0, b1, c0, c1 in zip(b_low, b_high, c_low, c_high)
        ]
        assert all(inside[: self.early]) and self.early
        assert self.early >= len(self.blocks[0]) and self.both[0]
        self.x_low, self.x_high = 6 * a_low[0] // 8 * 8, -(-6 * a_high[0] // 8) * 8
        self.levels = (self.spans(a_low, a_high), self.spans(b_low, b_high), self.spans(c_low, c_high))

    @staticmethod
    def spans(low, high):
        before_low, before_high = [high[0]] + low[:-1], [high[0]] + high[:-1]
        left = [b - a for a, b in zip(low, before_low)]
        count = [n + b - a for n, a, b in zip(left, before_high, high)]
        return low, left, before_high, count


def stencil(plan, samp, start, weight):
    row = lax.broadcasted_iota(jnp.int32, start.shape, 0)
    at_b = row < 4
    n_a, n_b = plan.n_samp * plan.pa, plan.n_samp * plan.pb

    def choose(b, c):
        return jnp.where(at_b, b, c)

    tap = start + choose(row - samp * plan.pa, row - 4 - samp * plan.pb)
    count, half = choose(n_a, n_b), choose(n_a // 2, n_b // 2)
    low, high = choose(0, plan.low_b), choose(plan.pa, plan.high_b)
    centre = choose(plan.pa // 2, (plan.low_b + plan.high_b) // 2)
    for _ in range(2):
        tap = jnp.where(tap - centre > half, tap - count, tap)
        tap = jnp.where(tap - centre < -half, tap + count, tap)
    inside = (tap >= low) & (tap < high)
    return jnp.clip(tap - low, 0, high - low - 1), jnp.where(inside, weight, 0.0)


def far_kernel(plan, list_len, x_hbm, *rest):
    small_hbm, (phb_hbm, phc_hbm, t_hbm, o_ref), small, rest = rest[:10], rest[10:14], rest[14:24], rest[24:]
    (theta_ab, theta_bc, child_b, child_c, start_b, weight_b, start_c, weight_c, src_ref, vec_ref) = small
    (
        x_ref, grid_a, pattern_b, grid_b, phb, phc, tab, tbc,
        s_b, s_c, ints, floats, tables_i, tables_w, idx, wgt,
        wide, lists, list_all, list_smem, halo_left, halo_right, res,
        psend, precv,
        *rest,
    ) = rest
    n_chunk, n_block = len(plan.sizes), len(plan.blocks)
    srcs, tbufs = rest[:n_block], rest[n_block : 2 * n_block]
    (in_sem, table_sem, list_sem, smem_sem, halo_sem, t_sem, src_send, src_recv, p_sem, out_sem) = rest[2 * n_block :]
    samp, box = lax.axis_index("samp"), lax.axis_index("box")
    n_box, n_samp = plan.n_box, plan.n_samp
    n_chip = n_box // 2
    chip, core = box // 2, box % 2
    partner = chip * 2 + 1 - core
    own = wide.shape[0]
    n_src = own * n_box
    first_end, last_end = chip == 0, chip == n_chip - 1
    is_end = first_end | last_end
    helps_first, helps_last = chip == 1, chip == n_chip - 2
    helps = helps_first | helps_last
    helped = jnp.where(helps_first, 0, n_chip - 1)
    helper = jnp.where(first_end, 1, n_chip - 2)
    left = (lax.rem(samp + n_samp - 1, n_samp), box)
    right = (lax.rem(samp + 1, n_samp), box)
    n_base = quarters(n_samp)

    barrier = pltpu.get_barrier_semaphore()
    for other in range(n_box):
        @pl.when(box != other)
        def _():
            pl.semaphore_signal(barrier, inc=1, device_id=(samp, other), device_id_type=MESH)
    for device in (left, right):
        pl.semaphore_signal(barrier, inc=1, device_id=device, device_id_type=MESH)

    x_rows_all = x_hbm.shape[1]
    pieces = [
        (first, last - first)
        for first, last in ((plan.x_low, plan.x_high), (0, plan.x_low), (plan.x_high, x_rows_all))
        if last > first
    ]
    in_copies = []
    for k, (first, n) in enumerate(pieces):
        here = pl.ds(first, n)
        in_copies.append(pltpu.make_async_copy(x_hbm.at[:, here, :], x_ref.at[:, here, :], in_sem.at[k]))
        if k == 0:
            base = lax.rem(samp, n_base)
            in_copies.append(pltpu.make_async_copy(phb_hbm.at[base], phb, in_sem.at[3]))
            in_copies.append(pltpu.make_async_copy(phc_hbm.at[base], phc, in_sem.at[4]))
    small_copies = [
        pltpu.make_async_copy(a, b, in_sem.at[5 + k]) for k, (a, b) in enumerate(zip(small_hbm, small))
    ]
    for copy in small_copies[:1] + in_copies[:1] + small_copies[1:] + in_copies[1:]:
        copy.start()
    small_copies[0].wait()
    count_a, count_b, count_c = x_ref.shape[0], child_b.shape[1], child_c.shape[0]
    theta_a, theta_b = theta_ab.shape
    theta_c = theta_bc.shape[0]
    def remote(src, dst, send, recv, device):
        return pltpu.make_async_remote_copy(
            src_ref=src, dst_ref=dst, send_sem=send, recv_sem=recv, device_id=device, device_id_type=MESH
        )

    tab[...] = jnp.zeros(tab.shape, jnp.bfloat16)
    high, low = split(theta_ab[...])
    for pair in range(2):
        at = pair * (2 * theta_a - LANES)
        for k in range(2):
            rows = slice(at + k * theta_a, at + (k + 1) * theta_a)
            cols = slice(k * theta_b, (k + 1) * theta_b)
            tab[pair, 0, rows, cols] = high
            tab[pair, 1, rows, cols] = low
    turns = samp // n_base

    def one_hot(ids, first, count):
        lane = lax.broadcasted_iota(jnp.int32, (ids.shape[0], count), 1) + first
        plus, minus = [], []
        for rep in range(4):
            hots = []
            for flip in range(2):
                column = None
                for t in range(n_samp // n_base):
                    o = octant(rep, t)
                    o = 7 - o if flip else o
                    here = ids[:, o : o + 1]
                    column = here if column is None else jnp.where(turns == t, here, column)
                hots.append(jnp.where(column == lane, 1.0, 0.0))
            plus.append(hots[0] + hots[1])
            minus.append(hots[0] - hots[1])
        hot = jnp.concatenate(plus + minus, axis=0).astype(jnp.bfloat16)
        return jnp.concatenate([hot, hot], axis=1)

    table_copies = []
    for k, ref in enumerate((ints, floats)):
        for d, (slot, device) in enumerate(((2, left), (0, right))):
            n = 4 * k + 2 * d
            table_copies.append(remote(ref.at[1], ref.at[slot], table_sem.at[n], table_sem.at[n + 1], device))
    def rows_of(which, start, size):
        low, high = 8 * (plan.split - start - size), 8 * (plan.split + start)
        return pl.ds(pl.multiple_of(jnp.where(which == 0, low, high), 8), 8 * size)

    def send_rows(which, c):
        return rows_of(which, plan.starts[c], plan.sizes[c])

    def half_rows(which, k):
        return rows_of(which, plan.block_starts[k], plan.block_sizes[k])

    def inner_rows(which, c):
        k = plan.block_of[c]
        after = plan.starts[c] - plan.block_starts[k]
        before = plan.block_sizes[k] - after - plan.sizes[c]
        return pl.ds(pl.multiple_of(jnp.where(which == 0, 8 * before, 8 * after), 8), 8 * plan.sizes[c])

    def t_copy(c):
        return pltpu.make_async_copy(t_hbm.at[:, half_rows(core, c), :], tbufs[c], t_sem.at[c])

    def when_has(which, c, do):
        if plan.block_both[c]:
            do()
        else:
            pl.when(which == 0)(do)

    to_left = remote(wide.at[:, plan.left_at, :], halo_right, halo_sem.at[0], halo_sem.at[1], left)
    to_right = remote(wide.at[:, plan.right_at, :], halo_left, halo_sem.at[2], halo_sem.at[3], right)

    def list_copy(slot, device, k):
        return remote(lists, list_all.at[slot], list_sem.at[k], list_sem.at[3 + slot], device)

    def src_copy(c, chip_to, d):
        index = c * n_box + chip_to * 2 + d
        return remote(
            wide.at[:, send_rows(d, c), :],
            srcs[plan.block_of[c]].at[pl.ds(pl.multiple_of(own * box, 8), own), inner_rows(d, c), :],
            src_send.at[index],
            src_recv.at[c * n_box + box],
            (samp, chip_to * 2 + d),
        )

    def send_chunk(c, act):
        def to_partner():
            act(src_copy(c, chip, 1 - core))

        when_has(1 - core, plan.block_of[c], to_partner)
        for chip_to in range(1, n_chip - 1):
            @pl.when(chip != chip_to)
            def _():
                for d in range(2):
                    if d == 0 or plan.both[c]:
                        act(src_copy(c, chip_to, d))

    x_rows = x_ref.reshape(count_a * x_ref.shape[1], LANES)
    wide_rows = wide.reshape(own * plan.total, LANES)
    stride_x = x_ref.shape[1]

    def theta_block(q):
        highs, lows = [], []
        for c in range(2):
            tiles = [split(x_rows[pl.ds(6 * q + 2 * j + c, count_a, stride=stride_x), :]) for j in range(3)]
            highs.append([t[0] for t in tiles])
            lows.append([t[1] for t in tiles])
        for pair in range(2):
            here = slice(pair, pair + 2)
            high = jnp.concatenate([jnp.concatenate(h[here], axis=1) for h in highs], axis=0)
            low = jnp.concatenate([jnp.concatenate(h[here], axis=1) for h in lows], axis=0)
            both = mm(high, tab[pair, 0]) + mm(low, tab[pair, 0]) + mm(high, tab[pair, 1])
            for k in range(2):
                grid_a[GROUP * q + 2 * pair + k] = both[:, k * LANES : (k + 1) * LANES]

    def taps(n, per_part, first_row):
        part = jnp.where(n >= 0, 1, 0) + jnp.where(n >= per_part, 1, 0)
        col = n + per_part * (1 - part)
        return [(idx[part, first_row + k, col], wgt[part, first_row + k, col]) for k in range(4)]

    def octants(phase, plus_r, plus_i, minus_r, minus_i, count):
        real = imag = None
        for j in range(4):
            cosine, sine = phase[j : j + 1, :], phase[4 + j : 5 + j, :]
            here = slice(j * count, (j + 1) * count)
            re = plus_r[here] * cosine - minus_i[here] * sine
            im = plus_i[here] * cosine + minus_r[here] * sine
            real, imag = (re, im) if real is None else (real + re, imag + im)
        return real, imag

    def level_b(m):
        stencil_b = taps(m + plan.low_b, plan.pb, 0)
        parts = []
        for c in range(2):
            here = slice(c * count_a, (c + 1) * count_a)
            value = None
            for at, weight in stencil_b:
                term = weight * grid_a[at, here, :]
                value = term if value is None else value + term
            parts.append(split(value))
        stacked = jnp.concatenate(
            [
                jnp.concatenate([parts[0][0], parts[1][0]], axis=1),
                jnp.concatenate([parts[0][1], parts[1][1]], axis=1),
            ],
            axis=0,
        )
        picked = mm(s_b[...], stacked)
        mid = 4 * count_b
        real, imag = octants(
            phb[m], picked[:mid, :LANES], picked[:mid, LANES:], picked[mid:, :LANES], picked[mid:, LANES:], count_b
        )
        high, low = split(jnp.concatenate([real, imag], axis=0))
        return jnp.concatenate([high, low], axis=1)

    def level_c(g):
        values = []
        for i in range(GROUP):
            value = None
            for at, weight in taps(g * GROUP + i + plan.low_c, plan.pc, 4):
                term = weight * grid_b[at]
                value = term if value is None else value + term
            values.append(value)
        high, low = split(jnp.concatenate(values, axis=1))
        rr = mm(s_c[...], jnp.concatenate([high[:count_b], low[:count_b]], axis=0))
        ri = mm(s_c[...], jnp.concatenate([high[count_b:], low[count_b:]], axis=0))
        mid = 4 * count_c
        real, imag = octants(phc[g], rr[:mid], ri[:mid], rr[mid:], ri[mid:], count_c)
        base = jnp.where(
            g < plan.edge,
            plan.padded + plan.left_pad + g * plan.unit_rows,
            jnp.where(
                g < plan.edge + plan.inner,
                (g - plan.edge) * plan.unit_rows,
                plan.padded + plan.left_rows + (g - plan.edge - plan.inner) * plan.unit_rows,
            ),
        )
        for c, flat in enumerate((real, imag)):
            for t in range(plan.unit_rows // 2):
                wide_rows[pl.ds(base + 2 * t + c, own, stride=plan.total), :] = flat[:, t * LANES : (t + 1) * LANES]

    def resolve(parts):
        copies = []
        for part in parts:
            row = lax.broadcasted_iota(jnp.int32, ints.shape[1:], 0)
            start = jnp.where(row < 4, ints[part, 0:1, :], ints[part, 1:2, :])
            at, weight = stencil(plan, samp, start, floats[part])
            tables_i[part] = at
            tables_w[part] = weight
            copies.append(pltpu.make_async_copy(tables_i.at[part], idx.at[part], smem_sem.at[part]))
            copies.append(pltpu.make_async_copy(tables_w.at[part], wgt.at[part], smem_sem.at[3 + part]))
        for copy in copies:
            copy.start()
        return copies

    def rest_of_setup():
        for copy in small_copies[1:]:
            copy.wait()
        ints[1, 0:1, 0 : plan.pb] = start_b[...]
        ints[1, 1:2, 0 : plan.pc] = start_c[...]
        floats[1, 0:4, 0 : plan.pb] = weight_b[...]
        floats[1, 4:8, 0 : plan.pc] = weight_c[...]
        lists[:, 0:list_len] = src_ref[...]
        lists[:, list_len : 2 * list_len] = vec_ref[...]
        own_tables = resolve((1,))
        high, low = split(theta_bc[...].T)
        tbc[0, :theta_b] = high
        tbc[0, theta_b:] = high
        tbc[1, :theta_b] = low
        tbc[1, theta_b:] = low
        s_b[...] = one_hot(child_b[...].T, box * count_a, count_a)
        s_c[...] = one_hot(child_c[...], box * count_b, count_b)
        blank = plan.rows // 8 * 8
        wide[:, blank:, :] = jnp.zeros((own, plan.total - blank, LANES), jnp.float32)
        for copy in own_tables + in_copies[1:3]:
            copy.wait()

    def phase(ph, carry):
        def items(level):
            low, before, after, count = (pick(ph, values) for values in plan.levels[level])
            return count, lambda i: jnp.where(i < before, low + i, after + i - before)

        count, item = items(0)

        def one_a(i, carry):
            theta_block(item(i))
            return carry

        lax.fori_loop(0, count, one_a, 0)
        if isinstance(ph, int):
            for k in range(n_block):
                when_has(core, k, lambda k=k: t_copy(k).start())
            rest_of_setup()
        count_m, item_m = items(1)

        def some_m(i, n):
            return [item_m(jnp.minimum(n * i + k, count_m - 1)) for k in range(n)]

        def one_b(i, carry):
            at = some_m(i, UNROLL_B)
            values = [level_b(m) for m in at]
            for m, value in zip(at, values):
                pattern_b[m] = value
            return carry

        def one_theta(i, carry):
            at = some_m(i, UNROLL_T)
            both = jnp.concatenate([pattern_b[m] for m in at], axis=0)
            grid = mm(both, tbc[0]) + mm(both[:, :LANES], tbc[1, :LANES])
            for k, m in enumerate(at):
                grid_b[m] = grid[2 * count_b * k : 2 * count_b * (k + 1)]
            return carry

        lax.fori_loop(0, pick(ph, [-(-n // UNROLL_B) for n in plan.levels[1][3]]), one_b, 0)
        lax.fori_loop(0, pick(ph, [-(-n // UNROLL_T) for n in plan.levels[1][3]]), one_theta, 0)
        count_g, item_g = items(2)

        def one_c(i, carry):
            level_c(item_g(i))
            return carry

        lax.fori_loop(0, count_g, one_c, 0)
        for c in range(1, 1 if isinstance(ph, int) else plan.early):
            @pl.when(ph == c)
            def _():
                send_chunk(c, lambda copy: copy.start())

        return carry

    even = lax.rem(lax.broadcasted_iota(jnp.int32, (8, LANES), 0), 2) == 0

    def turn(x):
        return jnp.where(even, pltpu.roll(x, 7, 0), pltpu.roll(x, 1, 0))

    def gather_sum(c, slot, i):
        size = plan.block_sizes[c]
        by_same = [jnp.zeros((8, LANES), jnp.float32) for _ in range(size)]
        by_turned = [jnp.zeros((8, LANES), jnp.float32) for _ in range(size)]
        for l in range(list_len):
            s = list_smem[slot, i, l]
            v = list_smem[slot, i, list_len + l]
            for g in range(size):
                here = slice(8 * g, 8 * g + 8)
                t = tbufs[c][v, here, :]
                by_same[g] = by_same[g] + t * srcs[c][s, here, :]
                by_turned[g] = by_turned[g] + t * srcs[c][s, slice(8 * (size + g), 8 * (size + g) + 8), :]
        out = []
        for g in range(size):
            x, y = by_same[g], by_turned[g]
            out.append(jnp.where(even, x - pltpu.roll(x, 7, 0), y + pltpu.roll(y, 1, 0)))
        return out

    def result_copy(c):
        return remote(
            res.at[pl.ds(pl.multiple_of((1 - core) * own, 8), own), plan.local[c], :],
            o_ref.at[:, half_rows(core, c), :],
            out_sem.at[c],
            out_sem.at[n_block + c],
            (samp, partner),
        )

    def result_wait(c):
        return remote(
            res.at[pl.ds(pl.multiple_of((1 - core) * own, 8), own), plan.local[c], :],
            o_ref.at[:, half_rows(1 - core, c), :],
            out_sem.at[c],
            out_sem.at[n_block + c],
            (samp, partner),
        )

    def p_copy(c, chip_to):
        return remote(
            psend.at[:, plan.local[c], :],
            precv.at[:, plan.local[c], :],
            p_sem.at[c],
            p_sem.at[n_block + c],
            (samp, chip_to * 2 + core),
        )

    def prepare(c):
        size = plan.block_sizes[c]
        rows = 8 * size
        srcs[c][pl.ds(pl.multiple_of(own * box, 8), own), 0:rows, :] = wide[:, half_rows(core, c), :]
        srcs[c][n_src] = jnp.zeros((2 * rows, LANES), jnp.float32)
        t_copy(c).wait()

        def arrived(other):
            for send in plan.blocks[c]:
                pltpu.make_async_copy(
                    wide.at[:, send_rows(core, send), :],
                    srcs[c].at[pl.ds(own * other, own), inner_rows(core, send), :],
                    src_recv.at[send * n_box + other],
                ).wait()

        for other in range(n_box):
            here = (box != other) & (jnp.logical_not(is_end) | (chip == other // 2))
            pl.when(here)(functools.partial(arrived, other))

        def swap_some(i, carry):
            for k in range(own):
                for g in range(size):
                    s = own * i + k
                    turned = turn(srcs[c][s, slice(8 * g, 8 * g + 8), :])
                    srcs[c][s, slice(8 * (size + g), 8 * (size + g) + 8), :] = turned
            return carry

        first = jnp.where(is_end, 2 * chip, 0)
        last = jnp.where(is_end, 2 * chip + 2, n_box)
        lax.fori_loop(first, last, swap_some, 0)

    def partial_sums(c):
        place = plan.local[c]

        @pl.when(helps)
        def _():
            def one(p, carry):
                slot, i = 2 + p // own, lax.rem(p, own)
                for g, value in enumerate(gather_sum(c, slot, i)):
                    psend[p, pl.ds(place.start + 8 * g, 8), :] = value
                return carry

            lax.fori_loop(0, 2 * own, one, 0)
            p_copy(c, helped).start()

    def own_sums(c):
        place = plan.local[c]

        def one(p, carry):
            slot, i = p // own, lax.rem(p, own)
            for g, value in enumerate(gather_sum(c, slot, i)):
                res[p, pl.ds(place.start + 8 * g, 8), :] = value
            return carry

        lax.fori_loop(0, 2 * own, one, 0)

    def finish(c):
        own_sums(c)

        @pl.when(jnp.logical_not(is_end))
        def _():
            deliver_plain(c)

    def deliver_plain(c):
        place = plan.local[c]
        o_ref[:, half_rows(core, c), :] = res[pl.ds(pl.multiple_of(core * own, 8), own), place, :]
        result_copy(c).start()

    def deliver_end(c):
        place = plan.local[c]
        p_copy(c, chip).wait_recv()
        res[:, place, :] = res[:, place, :] + precv[:, place, :]
        deliver_plain(c)

    def resolve_lists():
        list_copy(1 - core, (samp, partner), 0).wait_recv()

        @pl.when(helps)
        def _():
            for d in range(2):
                list_copy(2 + d, (samp, partner), 0).wait_recv()

        low = jnp.where(last_end, n_src - 2 * own, 0)
        high = jnp.where(first_end, 2 * own, n_src)
        low_p = jnp.where(helps_first, 2 * own, 0)
        high_p = jnp.where(helps_last, n_src - 2 * own, n_src)
        lane = lax.broadcasted_iota(jnp.int32, list_all.shape[1:], 1)
        for slot in range(4):
            a, b = (low, high) if slot < 2 else (low_p, high_p)
            value = list_all[slot]
            gone = (lane < list_len) & ((value < a) | (value >= b))
            list_all[slot] = jnp.where(gone, n_src, value)
        to_smem = pltpu.make_async_copy(list_all, list_smem, smem_sem.at[6])
        to_smem.start()
        to_smem.wait()

    def later_phase(ph, carry):
        @pl.when(ph == plan.early)
        def _():
            for copy in table_copies:
                copy.wait_recv()
            copies = resolve((0, 2))
            resolve_lists()
            prepare(0)
            partial_sums(0)
            for copy in copies:
                copy.wait()

        return phase(ph, carry)

    in_copies[0].wait()
    phase(0, 0)
    pl.semaphore_wait(barrier, n_box + 1)
    send_chunk(0, lambda copy: copy.start())
    for copy in table_copies:
        copy.start()
    list_copy(core, (samp, partner), 0).start()

    @pl.when(is_end)
    def _():
        for d in range(2):
            list_copy(2 + core, (samp, helper * 2 + d), 1 + d).start()

    list_all[core] = lists[...]
    for copy in in_copies[3:]:
        copy.wait()
    lax.fori_loop(1, plan.early + 1, later_phase, 0)
    to_left.start()
    to_right.start()

    def finish_edges():
        to_left.wait_recv()
        to_right.wait_recv()
        at_end = pl.ds(plan.end_at, halo_right.shape[1])
        wide[:, at_end, :] = wide[:, at_end, :] + halo_right[...]
        at_start = pl.ds(0, halo_left.shape[1])
        wide[:, at_start, :] = wide[:, at_start, :] + halo_left[...]
        for c in range(plan.early, n_chunk):
            send_chunk(c, lambda copy: copy.start())

    finish(0)
    finish_edges()

    def whole_block(k):
        prepare(k)
        partial_sums(k)
        finish(k)

    for k in range(1, n_block):
        when_has(core, k, functools.partial(whole_block, k))

    @pl.when(is_end)
    def _():
        for k in range(n_block):
            when_has(core, k, lambda k=k: deliver_end(k))

    for c in range(n_chunk):
        send_chunk(c, lambda copy: copy.wait_send())
    for k in range(n_block):
        when_has(core, k, lambda k=k: result_copy(k).wait_send())

        @pl.when(helps)
        def _():
            when_has(core, k, lambda: p_copy(k, helped).wait_send())

        when_has(1 - core, k, lambda k=k: result_wait(k).wait_recv())

    for copy in table_copies:
        copy.wait_send()
    to_left.wait_send()
    to_right.wait_send()
    list_copy(core, (samp, partner), 0).wait_send()

    @pl.when(is_end)
    def _():
        for d in range(2):
            list_copy(2 + core, (samp, helper * 2 + d), 1 + d).wait_send()


def interleave(x):
    x = x.reshape(x.shape[0], 2, -1, LANES).transpose(0, 2, 1, 3)
    x = with_layout_constraint(x, Layout(major_to_minor=(0, 1, 2, 3))).reshape(x.shape[0], -1, LANES)
    return jnp.pad(x, ((0, 0), (0, -x.shape[1] % 8), (0, 0))) if x.shape[1] % 8 else x


def separate(x, rows):
    x = x[:, :rows].reshape(x.shape[0], -1, 2, LANES)
    x = with_layout_constraint(x, Layout(major_to_minor=(0, 1, 2, 3)))
    return x.transpose(0, 2, 1, 3).reshape(x.shape[0], 2, -1)


def per_device(
    n_samp, n_box,
    pattern_a, children_b, children_c, theta_ab, theta_bc,
    phi_start_b, phi_weight_b, phi_start_c, phi_weight_c,
    translation, list_src, list_vec,
):
    count_a, count_b, count_c = pattern_a.shape[0], children_b.shape[0], children_c.shape[0]
    theta_a, theta_b = theta_ab.shape
    theta_c = theta_bc.shape[1]
    pa = pattern_a.shape[2] // theta_a
    plan = Plan(n_samp, n_box, pa, phi_start_b.shape[0], phi_start_c.shape[0], theta_c)
    phb = jnp.asarray(phase_table(n_samp, plan.pb, plan.low_b, plan.high_b, theta_b, SIZE_B))
    phc = phase_table(n_samp, plan.pc, plan.low_c, plan.high_c, theta_c, SIZE_C)
    phc = phc.reshape(phc.shape[0], -1, GROUP, 8, theta_c).transpose(0, 1, 3, 2, 4)
    phc = jnp.asarray(phc.reshape(phc.shape[:3] + (-1,)))
    x = interleave(pattern_a)
    t_view = interleave(translation)
    list_len = list_src.shape[1]
    n_src = count_c * n_box
    n_chunk, n_block = len(plan.sizes), len(plan.blocks)
    half = 8 * plan.split
    list_lanes = -(-2 * list_len // LANES) * LANES
    lanes = -(-max(plan.pb, plan.pc) // LANES) * LANES
    vmem = pl.BlockSpec(memory_space=pltpu.VMEM)
    hbm = pl.BlockSpec(memory_space=pl.ANY)
    f32, bf16, i32 = jnp.float32, jnp.bfloat16, jnp.int32
    small = (
        theta_ab, theta_bc.T, children_b.T, children_c,
        phi_start_b.reshape(1, -1), phi_weight_b, phi_start_c.reshape(1, -1), phi_weight_c,
        list_src, list_vec,
    )
    out = pl.pallas_call(
        functools.partial(far_kernel, plan, list_len),
        in_specs=[hbm] * 14,
        out_specs=vmem,
        scratch_shapes=[pltpu.VMEM(a.shape, a.dtype) for a in small]
        + [
            pltpu.VMEM(x.shape, f32),
            pltpu.VMEM((pa, 2 * count_a, LANES), f32),
            pltpu.VMEM((plan.wb, 2 * count_b, 2 * theta_b), bf16),
            pltpu.VMEM((plan.wb, 2 * count_b, theta_c), f32),
            pltpu.VMEM(phb.shape[1:], f32),
            pltpu.VMEM(phc.shape[1:], f32),
            pltpu.VMEM((2, 2, 2 * LANES, 2 * theta_b), bf16),
            pltpu.VMEM((2, 2 * theta_b, theta_c), bf16),
            pltpu.VMEM((8 * count_b, 2 * count_a), bf16),
            pltpu.VMEM((8 * count_c, 2 * count_b), bf16),
            pltpu.VMEM((3, 8, lanes), i32),
            pltpu.VMEM((3, 8, lanes), f32),
            pltpu.VMEM((3, 8, lanes), i32),
            pltpu.VMEM((3, 8, lanes), f32),
            pltpu.SMEM((3, 8, lanes), i32),
            pltpu.SMEM((3, 8, lanes), f32),
            pltpu.VMEM((count_c, plan.total, LANES), f32),
            pltpu.VMEM((count_c, list_lanes), i32),
            pltpu.VMEM((4, count_c, list_lanes), i32),
            pltpu.SMEM((4, count_c, list_lanes), i32),
            pltpu.VMEM((count_c, plan.right_rows, LANES), f32),
            pltpu.VMEM((count_c, plan.left_rows, LANES), f32),
            pltpu.VMEM((2 * count_c, half, LANES), f32),
            pltpu.VMEM((2 * count_c, half, LANES), f32),
            pltpu.VMEM((2 * count_c, half, LANES), f32),
        ]
        + [pltpu.VMEM((n_src + 1, 16 * n, LANES), f32) for n in plan.block_sizes]
        + [pltpu.VMEM((t_view.shape[0], 8 * n, LANES), f32) for n in plan.block_sizes]
        + [
            pltpu.SemaphoreType.DMA((15,)),
            pltpu.SemaphoreType.DMA((8,)),
            pltpu.SemaphoreType.DMA((7,)),
            pltpu.SemaphoreType.DMA((7,)),
            pltpu.SemaphoreType.DMA((4,)),
            pltpu.SemaphoreType.DMA((n_block,)),
            pltpu.SemaphoreType.DMA((n_chunk * n_box,)),
            pltpu.SemaphoreType.DMA((n_chunk * n_box,)),
            pltpu.SemaphoreType.DMA((2 * n_block,)),
            pltpu.SemaphoreType.DMA((2 * n_block,)),
        ],
        out_shape=jax.ShapeDtypeStruct((count_c, plan.padded, LANES), f32),
        compiler_params=pltpu.CompilerParams(
            collective_id=0, has_side_effects=True, vmem_limit_bytes=62 << 20
        ),
        name="far",
    )(x, *small, phb, phc, t_view)
    return separate(out, plan.rows)


def solution(mesh):
    placed = (
        P("box", None, "samp"),
        P("box", None),
        P("box", None),
        P(),
        P(),
        P("samp"),
        P(None, "samp"),
        P("samp"),
        P(None, "samp"),
        P(None, None, "samp"),
        P("box", None),
        P("box", None),
    )
    return jax.shard_map(
        functools.partial(per_device, mesh.shape["samp"], mesh.shape["box"]),
        mesh=mesh, in_specs=placed, out_specs=P("box", None, "samp"), check_vma=False,
    )
```

```python
import functools

import jax
import jax.numpy as jnp
import numpy as np
from jax import lax
from jax.experimental import pallas as pl
from jax.experimental.layout import Layout, with_layout_constraint
from jax.experimental.pallas import tpu as pltpu
from jax.sharding import PartitionSpec as P

SIZE_B = 8
SIZE_C = 16
LANES = 128
MESH = pl.DeviceIdType.MESH
GROUP = 4
CHUNKS = ((1, 2), (3,), (3,), (2,), (1,), (1,))
UNROLL_B = 6
UNROLL_T = 6
REPS = ((1, 1), (1, -1), (-1, 1), (-1, -1))


def window(first, last, n_child, n_parent):
    low = 0
    while (low - 1) * n_child // n_parent + 2 >= first:
        low -= 1
    high = 0
    while (high + 1) * n_child // n_parent - 2 <= last:
        high += 1
    return low, high + 1


def quarters(parts):
    return parts // 4 if parts % 4 == 0 else parts


def phase_table(parts, per_part, low, high, n_theta, size):
    n_phi = parts * per_part
    theta = np.pi * (np.arange(n_theta) + 0.5) / n_theta
    first = np.arange(quarters(parts))[:, None] * per_part
    phi = 2.0 * np.pi * (first + np.arange(low, high)[None]) / n_phi
    u_x = np.cos(phi)[..., None] * np.sin(theta)
    u_y = np.sin(phi)[..., None] * np.sin(theta)
    u_z = np.broadcast_to(np.cos(theta), u_x.shape)
    psi = np.stack([0.5 * np.pi * size * (s_x * u_x + s_y * u_y + u_z) for s_x, s_y in REPS], axis=2)
    return np.concatenate([np.cos(psi), np.sin(psi)], axis=2).astype(np.float32)


def octant(rep, turns):
    s_x, s_y = REPS[rep]
    for _ in range(turns):
        s_x, s_y = -s_y, s_x
    return 2 * (s_x + 1) + (s_y + 1) + 1


def split(x):
    high = x.astype(jnp.bfloat16)
    return high, (x - high.astype(jnp.float32)).astype(jnp.bfloat16)


def mm(a, b):
    return jnp.dot(a, b, preferred_element_type=jnp.float32)


def pick(index, values):
    if isinstance(index, int):
        return values[index]
    out = jnp.int32(values[0])
    for k in range(1, len(values)):
        out = jnp.where(index == k, values[k], out)
    return out


class Plan:
    def __init__(self, n_samp, n_box, pa, pb, pc, theta_c):
        self.n_samp, self.n_box = n_samp, n_box
        self.pa, self.pb, self.pc = pa, pb, pc
        n_a, n_b, n_c = n_samp * pa, n_samp * pb, n_samp * pc
        self.low_b, self.high_b = window(0, pa - 1, n_a, n_b)
        low_c, high_c = window(self.low_b, self.high_b - 1, n_b, n_c)
        self.ext = -(-max(-low_c, high_c - pc) // GROUP) * GROUP
        self.low_c, self.high_c = -self.ext, pc + self.ext
        self.wb, self.wc = self.high_b - self.low_b, self.high_c - self.low_c
        self.unit_rows = 2 * GROUP * theta_c // LANES
        self.edge, self.inner = self.ext // GROUP, pc // GROUP
        self.rows = rows = self.inner * self.unit_rows
        ext_rows = self.edge * self.unit_rows
        self.padded = -(-rows // 8) * 8
        groups = self.padded // 8
        self.split = -(-groups // 2)
        other = groups - self.split
        self.end_at = (rows - ext_rows) // 8 * 8
        self.left_rows = self.padded - self.end_at
        self.left_pad = rows - ext_rows - self.end_at
        self.right_rows = -(-ext_rows // 8) * 8
        self.left_at = pl.ds(self.padded, self.left_rows)
        self.right_at = pl.ds(self.padded + self.left_rows, self.right_rows)
        self.total = self.padded + self.left_rows + self.right_rows
        touched = max(self.left_rows, self.right_rows) // 8
        self.sizes, self.blocks = [], []
        for block in CHUNKS + ((1,),) * self.split:
            members = []
            for size in block:
                left = other - sum(self.sizes) - (0 if self.blocks else touched)
                if sum(self.sizes) < self.split and (left > 0 or self.blocks and not members):
                    members.append(len(self.sizes))
                    self.sizes.append(min(size, left) if left > 0 else 1)
            if members:
                self.blocks.append(members)
        self.starts = [sum(self.sizes[:c]) for c in range(len(self.sizes))]
        ends = [a + n for a, n in zip(self.starts, self.sizes)]
        self.both = [end <= other for end in ends]
        self.block_of = [k for k, members in enumerate(self.blocks) for _ in members]
        self.block_starts = [self.starts[members[0]] for members in self.blocks]
        self.block_sizes = [sum(self.sizes[c] for c in members) for members in self.blocks]
        self.block_both = [self.both[members[0]] for members in self.blocks]
        self.local = [pl.ds(8 * a, 8 * n) for a, n in zip(self.block_starts, self.block_sizes)]
        self.early = sum(end <= other - touched for end in ends)
        c_low, c_high, b_low, b_high, a_low, a_high = [], [], [], [], [], []
        for c in range(self.early + 1):
            first, last = 0, self.edge * 2 + self.inner
            if c < self.early:
                first = self.edge + 8 * (self.split - ends[c]) // self.unit_rows
                last = min(last, self.edge - (-8 * (self.split + ends[c]) // self.unit_rows))
            c_low.append(first)
            c_high.append(last)
            b0, b1 = 0, self.wb
            if c < self.early:
                b0 = (self.low_c + GROUP * first) * n_b // n_c - 2 - self.low_b
                b1 = (self.low_c + GROUP * last - 1) * n_b // n_c + 3 - self.low_b
                b0, b1 = max(b0, 0), min(b1, self.wb)
                if c:
                    b0, b1 = min(b0, b_low[-1]), max(b1, b_high[-1])
                inside_low, inside_high = -self.low_b, pb - self.low_b
                more = -(b1 - b0 - (b_high[-1] - b_low[-1] if c else 0)) % UNROLL_B
                for k in range(more):
                    if (k % 2 == 0 or b1 >= inside_high) and b0 > inside_low:
                        b0 -= 1
                    elif b1 < inside_high:
                        b1 += 1
            b_low.append(b0)
            b_high.append(b1)
            a0 = max((b0 + self.low_b) * n_a // n_b - 2, 0)
            a1 = min((b1 - 1 + self.low_b) * n_a // n_b + 3, pa)
            if c == self.early:
                a0, a1 = 0, pa
            a_low.append(a0 // GROUP)
            a_high.append(-(-a1 // GROUP))
        inside = [
            b0 + self.low_b >= 0 and b1 + self.low_b <= pb and self.edge <= c0 and c1 <= self.edge + self.inner
            for b0, b1, c0, c1 in zip(b_low, b_high, c_low, c_high)
        ]
        assert all(inside[: self.early]) and self.early
        assert self.early >= len(self.blocks[0]) and self.both[0]
        self.edges_late = self.block_both[1] and self.early > self.blocks[1][-1]
        self.x_low, self.x_high = 6 * a_low[0] // 8 * 8, -(-6 * a_high[0] // 8) * 8
        self.levels = (self.spans(a_low, a_high), self.spans(b_low, b_high), self.spans(c_low, c_high))

    @staticmethod
    def spans(low, high):
        before_low, before_high = [high[0]] + low[:-1], [high[0]] + high[:-1]
        left = [b - a for a, b in zip(low, before_low)]
        count = [n + b - a for n, a, b in zip(left, before_high, high)]
        return low, left, before_high, count


def stencil(plan, samp, start, weight):
    row = lax.broadcasted_iota(jnp.int32, start.shape, 0)
    at_b = row < 4
    n_a, n_b = plan.n_samp * plan.pa, plan.n_samp * plan.pb

    def choose(b, c):
        return jnp.where(at_b, b, c)

    tap = start + choose(row - samp * plan.pa, row - 4 - samp * plan.pb)
    count, half = choose(n_a, n_b), choose(n_a // 2, n_b // 2)
    low, high = choose(0, plan.low_b), choose(plan.pa, plan.high_b)
    centre = choose(plan.pa // 2, (plan.low_b + plan.high_b) // 2)
    for _ in range(2):
        tap = jnp.where(tap - centre > half, tap - count, tap)
        tap = jnp.where(tap - centre < -half, tap + count, tap)
    inside = (tap >= low) & (tap < high)
    return jnp.clip(tap - low, 0, high - low - 1), jnp.where(inside, weight, 0.0)


def far_kernel(plan, list_len, x_hbm, *rest):
    small_hbm, (phb_hbm, phc_hbm, t_hbm, o_ref), small, rest = rest[:10], rest[10:14], rest[14:24], rest[24:]
    (theta_ab, theta_bc, child_b, child_c, start_b, weight_b, start_c, weight_c, src_ref, vec_ref) = small
    (
        x_ref, grid_a, pattern_b, grid_b, phb, phc, tab, tbc,
        s_b, s_c, ints, floats, tables_i, tables_w, idx, wgt,
        wide, lists, list_all, list_smem, halo_left, halo_right, res,
        psend, precv,
        *rest,
    ) = rest
    n_chunk, n_block = len(plan.sizes), len(plan.blocks)
    srcs, tbufs = rest[:n_block], rest[n_block : 2 * n_block]
    (in_sem, table_sem, list_sem, smem_sem, halo_sem, t_sem, src_send, src_recv, p_sem, out_sem) = rest[2 * n_block :]
    samp, box = lax.axis_index("samp"), lax.axis_index("box")
    n_box, n_samp = plan.n_box, plan.n_samp
    n_chip = n_box // 2
    chip, core = box // 2, box % 2
    partner = chip * 2 + 1 - core
    own = wide.shape[0]
    n_src = own * n_box
    first_end, last_end = chip == 0, chip == n_chip - 1
    is_end = first_end | last_end
    helps_first, helps_last = chip == 1, chip == n_chip - 2
    helps = helps_first | helps_last
    helped = jnp.where(helps_first, 0, n_chip - 1)
    helper = jnp.where(first_end, 1, n_chip - 2)
    left = (lax.rem(samp + n_samp - 1, n_samp), box)
    right = (lax.rem(samp + 1, n_samp), box)
    n_base = quarters(n_samp)

    barrier = pltpu.get_barrier_semaphore()
    for other in range(n_box):
        @pl.when(box != other)
        def _():
            pl.semaphore_signal(barrier, inc=1, device_id=(samp, other), device_id_type=MESH)
    for device in (left, right):
        pl.semaphore_signal(barrier, inc=1, device_id=device, device_id_type=MESH)

    x_rows_all = x_hbm.shape[1]
    pieces = [
        (first, last - first)
        for first, last in ((plan.x_low, plan.x_high), (0, plan.x_low), (plan.x_high, x_rows_all))
        if last > first
    ]
    in_copies = []
    for k, (first, n) in enumerate(pieces):
        here = pl.ds(first, n)
        in_copies.append(pltpu.make_async_copy(x_hbm.at[:, here, :], x_ref.at[:, here, :], in_sem.at[k]))
        if k == 0:
            base = lax.rem(samp, n_base)
            in_copies.append(pltpu.make_async_copy(phb_hbm.at[base], phb, in_sem.at[3]))
            in_copies.append(pltpu.make_async_copy(phc_hbm.at[base], phc, in_sem.at[4]))
    small_copies = [
        pltpu.make_async_copy(a, b, in_sem.at[5 + k]) for k, (a, b) in enumerate(zip(small_hbm, small))
    ]
    for copy in small_copies[:1] + in_copies[:1] + small_copies[1:] + in_copies[1:]:
        copy.start()
    small_copies[0].wait()
    count_a, count_b, count_c = x_ref.shape[0], child_b.shape[1], child_c.shape[0]
    theta_a, theta_b = theta_ab.shape
    theta_c = theta_bc.shape[0]
    def remote(src, dst, send, recv, device):
        return pltpu.make_async_remote_copy(
            src_ref=src, dst_ref=dst, send_sem=send, recv_sem=recv, device_id=device, device_id_type=MESH
        )

    tab[...] = jnp.zeros(tab.shape, jnp.bfloat16)
    high, low = split(theta_ab[...])
    for pair in range(2):
        at = pair * (2 * theta_a - LANES)
        for k in range(2):
            rows = slice(at + k * theta_a, at + (k + 1) * theta_a)
            cols = slice(k * theta_b, (k + 1) * theta_b)
            tab[pair, 0, rows, cols] = high
            tab[pair, 1, rows, cols] = low
    turns = samp // n_base

    def one_hot(ids, first, count):
        lane = lax.broadcasted_iota(jnp.int32, (ids.shape[0], count), 1) + first
        plus, minus = [], []
        for rep in range(4):
            hots = []
            for flip in range(2):
                column = None
                for t in range(n_samp // n_base):
                    o = octant(rep, t)
                    o = 7 - o if flip else o
                    here = ids[:, o : o + 1]
                    column = here if column is None else jnp.where(turns == t, here, column)
                hots.append(jnp.where(column == lane, 1.0, 0.0))
            plus.append(hots[0] + hots[1])
            minus.append(hots[0] - hots[1])
        hot = jnp.concatenate(plus + minus, axis=0).astype(jnp.bfloat16)
        return jnp.concatenate([hot, hot], axis=1)

    table_copies = []
    for k, ref in enumerate((ints, floats)):
        for d, (slot, device) in enumerate(((2, left), (0, right))):
            n = 4 * k + 2 * d
            table_copies.append(remote(ref.at[1], ref.at[slot], table_sem.at[n], table_sem.at[n + 1], device))
    def rows_of(which, start, size):
        low, high = 8 * (plan.split - start - size), 8 * (plan.split + start)
        return pl.ds(pl.multiple_of(jnp.where(which == 0, low, high), 8), 8 * size)

    def send_rows(which, c):
        return rows_of(which, plan.starts[c], plan.sizes[c])

    def half_rows(which, k):
        return rows_of(which, plan.block_starts[k], plan.block_sizes[k])

    def inner_rows(which, c):
        k = plan.block_of[c]
        after = plan.starts[c] - plan.block_starts[k]
        before = plan.block_sizes[k] - after - plan.sizes[c]
        return pl.ds(pl.multiple_of(jnp.where(which == 0, 8 * before, 8 * after), 8), 8 * plan.sizes[c])

    def t_copy(c):
        return pltpu.make_async_copy(t_hbm.at[:, half_rows(core, c), :], tbufs[c], t_sem.at[c])

    def when_has(which, c, do):
        if plan.block_both[c]:
            do()
        else:
            pl.when(which == 0)(do)

    to_left = remote(wide.at[:, plan.left_at, :], halo_right, halo_sem.at[0], halo_sem.at[1], left)
    to_right = remote(wide.at[:, plan.right_at, :], halo_left, halo_sem.at[2], halo_sem.at[3], right)

    def list_copy(slot, device, k):
        return remote(lists, list_all.at[slot], list_sem.at[k], list_sem.at[3 + slot], device)

    def src_copy(c, chip_to, d):
        index = c * n_box + chip_to * 2 + d
        return remote(
            wide.at[:, send_rows(d, c), :],
            srcs[plan.block_of[c]].at[pl.ds(pl.multiple_of(own * box, 8), own), inner_rows(d, c), :],
            src_send.at[index],
            src_recv.at[c * n_box + box],
            (samp, chip_to * 2 + d),
        )

    def send_chunk(c, act):
        def to_partner():
            act(src_copy(c, chip, 1 - core))

        when_has(1 - core, plan.block_of[c], to_partner)
        for chip_to in range(1, n_chip - 1):
            @pl.when(chip != chip_to)
            def _():
                for d in range(2):
                    if d == 0 or plan.both[c]:
                        act(src_copy(c, chip_to, d))

    x_rows = x_ref.reshape(count_a * x_ref.shape[1], LANES)
    wide_rows = wide.reshape(own * plan.total, LANES)
    stride_x = x_ref.shape[1]

    def theta_blocks(blocks):
        highs, lows = [], []
        for q in blocks:
            for c in range(2):
                tiles = [split(x_rows[pl.ds(6 * q + 2 * j + c, count_a, stride=stride_x), :]) for j in range(3)]
                highs.append([t[0] for t in tiles])
                lows.append([t[1] for t in tiles])
        for pair in range(2):
            here = slice(pair, pair + 2)
            high = jnp.concatenate([jnp.concatenate(h[here], axis=1) for h in highs], axis=0)
            low = jnp.concatenate([jnp.concatenate(h[here], axis=1) for h in lows], axis=0)
            both = mm(high, tab[pair, 0]) + mm(low, tab[pair, 0]) + mm(high, tab[pair, 1])
            for n, q in enumerate(blocks):
                for k in range(2):
                    grid_a[GROUP * q + 2 * pair + k] = both[
                        2 * count_a * n : 2 * count_a * (n + 1), k * LANES : (k + 1) * LANES
                    ]

    def taps(n, per_part, first_row):
        part = jnp.where(n >= 0, 1, 0) + jnp.where(n >= per_part, 1, 0)
        col = n + per_part * (1 - part)
        return [(idx[part, first_row + k, col], wgt[part, first_row + k, col]) for k in range(4)]

    def octants(phase, plus_r, plus_i, minus_r, minus_i, count):
        real = imag = None
        for j in range(4):
            cosine, sine = phase[j : j + 1, :], phase[4 + j : 5 + j, :]
            here = slice(j * count, (j + 1) * count)
            re = plus_r[here] * cosine - minus_i[here] * sine
            im = plus_i[here] * cosine + minus_r[here] * sine
            real, imag = (re, im) if real is None else (real + re, imag + im)
        return real, imag

    def level_b(m):
        stencil_b = taps(m + plan.low_b, plan.pb, 0)
        parts = []
        for c in range(2):
            here = slice(c * count_a, (c + 1) * count_a)
            value = None
            for at, weight in stencil_b:
                term = weight * grid_a[at, here, :]
                value = term if value is None else value + term
            parts.append(split(value))
        stacked = jnp.concatenate(
            [
                jnp.concatenate([parts[0][0], parts[1][0]], axis=1),
                jnp.concatenate([parts[0][1], parts[1][1]], axis=1),
            ],
            axis=0,
        )
        picked = mm(s_b[...], stacked)
        mid = 4 * count_b
        real, imag = octants(
            phb[m], picked[:mid, :LANES], picked[:mid, LANES:], picked[mid:, :LANES], picked[mid:, LANES:], count_b
        )
        high, low = split(jnp.concatenate([real, imag], axis=0))
        return jnp.concatenate([high, low], axis=1)

    def level_c(g):
        values = []
        for i in range(GROUP):
            value = None
            for at, weight in taps(g * GROUP + i + plan.low_c, plan.pc, 4):
                term = weight * grid_b[at]
                value = term if value is None else value + term
            values.append(value)
        high, low = split(jnp.concatenate(values, axis=1))
        rr = mm(s_c[...], jnp.concatenate([high[:count_b], low[:count_b]], axis=0))
        ri = mm(s_c[...], jnp.concatenate([high[count_b:], low[count_b:]], axis=0))
        mid = 4 * count_c
        real, imag = octants(phc[g], rr[:mid], ri[:mid], rr[mid:], ri[mid:], count_c)
        base = jnp.where(
            g < plan.edge,
            plan.padded + plan.left_pad + g * plan.unit_rows,
            jnp.where(
                g < plan.edge + plan.inner,
                (g - plan.edge) * plan.unit_rows,
                plan.padded + plan.left_rows + (g - plan.edge - plan.inner) * plan.unit_rows,
            ),
        )
        for c, flat in enumerate((real, imag)):
            for t in range(plan.unit_rows // 2):
                wide_rows[pl.ds(base + 2 * t + c, own, stride=plan.total), :] = flat[:, t * LANES : (t + 1) * LANES]

    def resolve(parts):
        copies = []
        for part in parts:
            row = lax.broadcasted_iota(jnp.int32, ints.shape[1:], 0)
            start = jnp.where(row < 4, ints[part, 0:1, :], ints[part, 1:2, :])
            at, weight = stencil(plan, samp, start, floats[part])
            tables_i[part] = at
            tables_w[part] = weight
            copies.append(pltpu.make_async_copy(tables_i.at[part], idx.at[part], smem_sem.at[part]))
            copies.append(pltpu.make_async_copy(tables_w.at[part], wgt.at[part], smem_sem.at[3 + part]))
        for copy in copies:
            copy.start()
        return copies

    def rest_of_setup():
        for copy in small_copies[1:]:
            copy.wait()
        ints[1, 0:1, 0 : plan.pb] = start_b[...]
        ints[1, 1:2, 0 : plan.pc] = start_c[...]
        floats[1, 0:4, 0 : plan.pb] = weight_b[...]
        floats[1, 4:8, 0 : plan.pc] = weight_c[...]
        lists[:, 0:list_len] = src_ref[...]
        lists[:, list_len : 2 * list_len] = vec_ref[...]
        own_tables = resolve((1,))
        high, low = split(theta_bc[...].T)
        tbc[0, :theta_b] = high
        tbc[0, theta_b:] = high
        tbc[1, :theta_b] = low
        tbc[1, theta_b:] = low
        s_b[...] = one_hot(child_b[...].T, box * count_a, count_a)
        s_c[...] = one_hot(child_c[...], box * count_b, count_b)
        blank = plan.rows // 8 * 8
        wide[:, blank:, :] = jnp.zeros((own, plan.total - blank, LANES), jnp.float32)
        for copy in own_tables + in_copies[1:3]:
            copy.wait()

    def phase(ph, carry):
        def items(level):
            low, before, after, count = (pick(ph, values) for values in plan.levels[level])
            return count, lambda i: jnp.where(i < before, low + i, after + i - before)

        count, item = items(0)

        def one_a(i, carry):
            theta_blocks([item(2 * i), item(jnp.minimum(2 * i + 1, count - 1))])
            return carry

        lax.fori_loop(0, pick(ph, [-(-n // 2) for n in plan.levels[0][3]]), one_a, 0)
        if isinstance(ph, int):
            for k in range(n_block):
                when_has(core, k, lambda k=k: t_copy(k).start())
            rest_of_setup()
        count_m, item_m = items(1)

        def some_m(i, n):
            return [item_m(jnp.minimum(n * i + k, count_m - 1)) for k in range(n)]

        def one_b(i, carry):
            at = some_m(i, UNROLL_B)
            values = [level_b(m) for m in at]
            for m, value in zip(at, values):
                pattern_b[m] = value
            return carry

        def one_theta(i, carry):
            at = some_m(i, UNROLL_T)
            both = jnp.concatenate([pattern_b[m] for m in at], axis=0)
            grid = mm(both, tbc[0]) + mm(both[:, :LANES], tbc[1, :LANES])
            for k, m in enumerate(at):
                grid_b[m] = grid[2 * count_b * k : 2 * count_b * (k + 1)]
            return carry

        lax.fori_loop(0, pick(ph, [-(-n // UNROLL_B) for n in plan.levels[1][3]]), one_b, 0)
        lax.fori_loop(0, pick(ph, [-(-n // UNROLL_T) for n in plan.levels[1][3]]), one_theta, 0)
        count_g, item_g = items(2)

        def one_c(i, carry):
            level_c(item_g(i))
            return carry

        lax.fori_loop(0, count_g, one_c, 0)
        for c in range(1, 1 if isinstance(ph, int) else plan.early):
            @pl.when(ph == c)
            def _():
                send_chunk(c, lambda copy: copy.start())

        return carry

    even = lax.rem(lax.broadcasted_iota(jnp.int32, (8, LANES), 0), 2) == 0

    def turn(x):
        return jnp.where(even, pltpu.roll(x, 7, 0), pltpu.roll(x, 1, 0))

    def gather_sum(c, slot, i):
        size = plan.block_sizes[c]
        by_same = [jnp.zeros((8, LANES), jnp.float32) for _ in range(size)]
        by_turned = [jnp.zeros((8, LANES), jnp.float32) for _ in range(size)]
        for l in range(list_len):
            s = list_smem[slot, i, l]
            v = list_smem[slot, i, list_len + l]
            for g in range(size):
                here = slice(8 * g, 8 * g + 8)
                t = tbufs[c][v, here, :]
                by_same[g] = by_same[g] + t * srcs[c][s, here, :]
                by_turned[g] = by_turned[g] + t * srcs[c][s, slice(8 * (size + g), 8 * (size + g) + 8), :]
        out = []
        for g in range(size):
            x, y = by_same[g], by_turned[g]
            out.append(jnp.where(even, x - pltpu.roll(x, 7, 0), y + pltpu.roll(y, 1, 0)))
        return out

    def result_copy(c):
        return remote(
            res.at[pl.ds(pl.multiple_of((1 - core) * own, 8), own), plan.local[c], :],
            o_ref.at[:, half_rows(core, c), :],
            out_sem.at[c],
            out_sem.at[n_block + c],
            (samp, partner),
        )

    def result_wait(c):
        return remote(
            res.at[pl.ds(pl.multiple_of((1 - core) * own, 8), own), plan.local[c], :],
            o_ref.at[:, half_rows(1 - core, c), :],
            out_sem.at[c],
            out_sem.at[n_block + c],
            (samp, partner),
        )

    def p_copy(c, chip_to):
        return remote(
            psend.at[:, plan.local[c], :],
            precv.at[:, plan.local[c], :],
            p_sem.at[c],
            p_sem.at[n_block + c],
            (samp, chip_to * 2 + core),
        )

    def prepare(c):
        size = plan.block_sizes[c]
        rows = 8 * size
        srcs[c][pl.ds(pl.multiple_of(own * box, 8), own), 0:rows, :] = wide[:, half_rows(core, c), :]
        srcs[c][n_src] = jnp.zeros((2 * rows, LANES), jnp.float32)
        t_copy(c).wait()

        def arrived(other):
            for send in plan.blocks[c]:
                pltpu.make_async_copy(
                    wide.at[:, send_rows(core, send), :],
                    srcs[c].at[pl.ds(own * other, own), inner_rows(core, send), :],
                    src_recv.at[send * n_box + other],
                ).wait()

        for other in range(n_box):
            here = (box != other) & (jnp.logical_not(is_end) | (chip == other // 2))
            pl.when(here)(functools.partial(arrived, other))

        def swap_some(i, carry):
            for k in range(own):
                for g in range(size):
                    s = own * i + k
                    turned = turn(srcs[c][s, slice(8 * g, 8 * g + 8), :])
                    srcs[c][s, slice(8 * (size + g), 8 * (size + g) + 8), :] = turned
            return carry

        first = jnp.where(is_end, 2 * chip, 0)
        last = jnp.where(is_end, 2 * chip + 2, n_box)
        lax.fori_loop(first, last, swap_some, 0)

    def partial_sums(c):
        place = plan.local[c]

        @pl.when(helps)
        def _():
            def one(p, carry):
                slot, i = 2 + p // own, lax.rem(p, own)
                for g, value in enumerate(gather_sum(c, slot, i)):
                    psend[p, pl.ds(place.start + 8 * g, 8), :] = value
                return carry

            lax.fori_loop(0, 2 * own, one, 0)
            p_copy(c, helped).start()

    def own_sums(c):
        place = plan.local[c]

        def one(p, carry):
            slot, i = p // own, lax.rem(p, own)
            for g, value in enumerate(gather_sum(c, slot, i)):
                res[p, pl.ds(place.start + 8 * g, 8), :] = value
            return carry

        lax.fori_loop(0, 2 * own, one, 0)

    def finish(c):
        own_sums(c)

        @pl.when(jnp.logical_not(is_end))
        def _():
            deliver_plain(c)

    def deliver_plain(c):
        place = plan.local[c]
        o_ref[:, half_rows(core, c), :] = res[pl.ds(pl.multiple_of(core * own, 8), own), place, :]
        result_copy(c).start()

    def deliver_end(c):
        place = plan.local[c]
        p_copy(c, chip).wait_recv()
        res[:, place, :] = res[:, place, :] + precv[:, place, :]
        deliver_plain(c)

    def resolve_lists():
        list_copy(1 - core, (samp, partner), 0).wait_recv()

        @pl.when(helps)
        def _():
            for d in range(2):
                list_copy(2 + d, (samp, partner), 0).wait_recv()

        low = jnp.where(last_end, n_src - 2 * own, 0)
        high = jnp.where(first_end, 2 * own, n_src)
        low_p = jnp.where(helps_first, 2 * own, 0)
        high_p = jnp.where(helps_last, n_src - 2 * own, n_src)
        lane = lax.broadcasted_iota(jnp.int32, list_all.shape[1:], 1)
        for slot in range(4):
            a, b = (low, high) if slot < 2 else (low_p, high_p)
            value = list_all[slot]
            gone = (lane < list_len) & ((value < a) | (value >= b))
            list_all[slot] = jnp.where(gone, n_src, value)
        to_smem = pltpu.make_async_copy(list_all, list_smem, smem_sem.at[6])
        to_smem.start()
        return to_smem

    def later_phase(ph, carry):
        @pl.when(ph == plan.early)
        def _():
            for copy in table_copies:
                copy.wait_recv()
            copies = resolve((0, 2))
            to_smem = resolve_lists()
            prepare(0)
            to_smem.wait()
            partial_sums(0)
            for copy in copies:
                copy.wait()

        return phase(ph, carry)

    in_copies[0].wait()
    phase(0, 0)
    pl.semaphore_wait(barrier, n_box + 1)
    send_chunk(0, lambda copy: copy.start())
    for copy in table_copies:
        copy.start()
    list_copy(core, (samp, partner), 0).start()

    @pl.when(is_end)
    def _():
        for d in range(2):
            list_copy(2 + core, (samp, helper * 2 + d), 1 + d).start()

    list_all[core] = lists[...]
    for copy in in_copies[3:]:
        copy.wait()
    lax.fori_loop(1, plan.early + 1, later_phase, 0)
    to_left.start()
    to_right.start()

    def finish_edges():
        to_left.wait_recv()
        to_right.wait_recv()
        at_end = pl.ds(plan.end_at, halo_right.shape[1])
        wide[:, at_end, :] = wide[:, at_end, :] + halo_right[...]
        at_start = pl.ds(0, halo_left.shape[1])
        wide[:, at_start, :] = wide[:, at_start, :] + halo_left[...]
        for c in range(plan.early, n_chunk):
            send_chunk(c, lambda copy: copy.start())

    finish(0)
    if not plan.edges_late:
        finish_edges()

    def whole_block(k):
        prepare(k)
        partial_sums(k)
        if k == 1 and plan.edges_late:
            finish_edges()
        finish(k)

    for k in range(1, n_block):
        when_has(core, k, functools.partial(whole_block, k))

    for c in range(n_chunk):
        send_chunk(c, lambda copy: copy.wait_send())
    for copy in table_copies:
        copy.wait_send()
    to_left.wait_send()
    to_right.wait_send()
    list_copy(core, (samp, partner), 0).wait_send()

    @pl.when(is_end)
    def _():
        for d in range(2):
            list_copy(2 + core, (samp, helper * 2 + d), 1 + d).wait_send()

    @pl.when(is_end)
    def _():
        for k in range(n_block):
            when_has(core, k, lambda k=k: deliver_end(k))

    for k in range(n_block):
        when_has(core, k, lambda k=k: result_copy(k).wait_send())

        @pl.when(helps)
        def _():
            when_has(core, k, lambda: p_copy(k, helped).wait_send())

        when_has(1 - core, k, lambda k=k: result_wait(k).wait_recv())


def interleave(x):
    x = x.reshape(x.shape[0], 2, -1, LANES).transpose(0, 2, 1, 3)
    x = with_layout_constraint(x, Layout(major_to_minor=(0, 1, 2, 3))).reshape(x.shape[0], -1, LANES)
    return jnp.pad(x, ((0, 0), (0, -x.shape[1] % 8), (0, 0))) if x.shape[1] % 8 else x


def separate(x, rows):
    x = x[:, :rows].reshape(x.shape[0], -1, 2, LANES)
    x = with_layout_constraint(x, Layout(major_to_minor=(0, 1, 2, 3)))
    return x.transpose(0, 2, 1, 3).reshape(x.shape[0], 2, -1)


def per_device(
    n_samp, n_box,
    pattern_a, children_b, children_c, theta_ab, theta_bc,
    phi_start_b, phi_weight_b, phi_start_c, phi_weight_c,
    translation, list_src, list_vec,
):
    count_a, count_b, count_c = pattern_a.shape[0], children_b.shape[0], children_c.shape[0]
    theta_a, theta_b = theta_ab.shape
    theta_c = theta_bc.shape[1]
    pa = pattern_a.shape[2] // theta_a
    plan = Plan(n_samp, n_box, pa, phi_start_b.shape[0], phi_start_c.shape[0], theta_c)
    phb = jnp.asarray(phase_table(n_samp, plan.pb, plan.low_b, plan.high_b, theta_b, SIZE_B))
    phc = phase_table(n_samp, plan.pc, plan.low_c, plan.high_c, theta_c, SIZE_C)
    phc = phc.reshape(phc.shape[0], -1, GROUP, 8, theta_c).transpose(0, 1, 3, 2, 4)
    phc = jnp.asarray(phc.reshape(phc.shape[:3] + (-1,)))
    x = interleave(pattern_a)
    t_view = interleave(translation)
    list_len = list_src.shape[1]
    n_src = count_c * n_box
    n_chunk, n_block = len(plan.sizes), len(plan.blocks)
    half = 8 * plan.split
    list_lanes = -(-2 * list_len // LANES) * LANES
    lanes = -(-max(plan.pb, plan.pc) // LANES) * LANES
    vmem = pl.BlockSpec(memory_space=pltpu.VMEM)
    hbm = pl.BlockSpec(memory_space=pl.ANY)
    f32, bf16, i32 = jnp.float32, jnp.bfloat16, jnp.int32
    small = (
        theta_ab, theta_bc.T, children_b.T, children_c,
        phi_start_b.reshape(1, -1), phi_weight_b, phi_start_c.reshape(1, -1), phi_weight_c,
        list_src, list_vec,
    )
    out = pl.pallas_call(
        functools.partial(far_kernel, plan, list_len),
        in_specs=[hbm] * 14,
        out_specs=vmem,
        scratch_shapes=[pltpu.VMEM(a.shape, a.dtype) for a in small]
        + [
            pltpu.VMEM(x.shape, f32),
            pltpu.VMEM((pa, 2 * count_a, LANES), f32),
            pltpu.VMEM((plan.wb, 2 * count_b, 2 * theta_b), bf16),
            pltpu.VMEM((plan.wb, 2 * count_b, theta_c), f32),
            pltpu.VMEM(phb.shape[1:], f32),
            pltpu.VMEM(phc.shape[1:], f32),
            pltpu.VMEM((2, 2, 2 * LANES, 2 * theta_b), bf16),
            pltpu.VMEM((2, 2 * theta_b, theta_c), bf16),
            pltpu.VMEM((8 * count_b, 2 * count_a), bf16),
            pltpu.VMEM((8 * count_c, 2 * count_b), bf16),
            pltpu.VMEM((3, 8, lanes), i32),
            pltpu.VMEM((3, 8, lanes), f32),
            pltpu.VMEM((3, 8, lanes), i32),
            pltpu.VMEM((3, 8, lanes), f32),
            pltpu.SMEM((3, 8, lanes), i32),
            pltpu.SMEM((3, 8, lanes), f32),
            pltpu.VMEM((count_c, plan.total, LANES), f32),
            pltpu.VMEM((count_c, list_lanes), i32),
            pltpu.VMEM((4, count_c, list_lanes), i32),
            pltpu.SMEM((4, count_c, list_lanes), i32),
            pltpu.VMEM((count_c, plan.right_rows, LANES), f32),
            pltpu.VMEM((count_c, plan.left_rows, LANES), f32),
            pltpu.VMEM((2 * count_c, half, LANES), f32),
            pltpu.VMEM((2 * count_c, half, LANES), f32),
            pltpu.VMEM((2 * count_c, half, LANES), f32),
        ]
        + [pltpu.VMEM((n_src + 1, 16 * n, LANES), f32) for n in plan.block_sizes]
        + [pltpu.VMEM((t_view.shape[0], 8 * n, LANES), f32) for n in plan.block_sizes]
        + [
            pltpu.SemaphoreType.DMA((15,)),
            pltpu.SemaphoreType.DMA((8,)),
            pltpu.SemaphoreType.DMA((7,)),
            pltpu.SemaphoreType.DMA((7,)),
            pltpu.SemaphoreType.DMA((4,)),
            pltpu.SemaphoreType.DMA((n_block,)),
            pltpu.SemaphoreType.DMA((n_chunk * n_box,)),
            pltpu.SemaphoreType.DMA((n_chunk * n_box,)),
            pltpu.SemaphoreType.DMA((2 * n_block,)),
            pltpu.SemaphoreType.DMA((2 * n_block,)),
        ],
        out_shape=pltpu.VMEM((count_c, plan.padded, LANES), f32),
        compiler_params=pltpu.CompilerParams(
            collective_id=0, has_side_effects=True, vmem_limit_bytes=56 << 20
        ),
        name="far",
    )(x, *small, phb, phc, t_view)
    return separate(out, plan.rows)


def solution(mesh):
    placed = (
        P("box", None, "samp"),
        P("box", None),
        P("box", None),
        P(),
        P(),
        P("samp"),
        P(None, "samp"),
        P("samp"),
        P(None, "samp"),
        P(None, None, "samp"),
        P("box", None),
        P("box", None),
    )
    return jax.shard_map(
        functools.partial(per_device, mesh.shape["samp"], mesh.shape["box"]),
        mesh=mesh, in_specs=placed, out_specs=P("box", None, "samp"), check_vma=False,
    )
```

```python
import functools

import jax
import jax.numpy as jnp
import numpy as np
from jax import lax
from jax.experimental import pallas as pl
from jax.experimental.layout import Layout, with_layout_constraint
from jax.experimental.pallas import tpu as pltpu
from jax.sharding import PartitionSpec as P

SIZE_B = 8
SIZE_C = 16
LANES = 128
MESH = pl.DeviceIdType.MESH
GROUP = 4
CHUNKS = ((1, 2), (3,), (3,), (2,), (1,), (1,))
UNROLL_B = 6
UNROLL_T = 6
REPS = ((1, 1), (1, -1), (-1, 1), (-1, -1))


def window(first, last, n_child, n_parent):
    low = 0
    while (low - 1) * n_child // n_parent + 2 >= first:
        low -= 1
    high = 0
    while (high + 1) * n_child // n_parent - 2 <= last:
        high += 1
    return low, high + 1


def quarters(parts):
    return parts // 4 if parts % 4 == 0 else parts


def phase_table(parts, per_part, low, high, n_theta, size):
    n_phi = parts * per_part
    theta = np.pi * (np.arange(n_theta) + 0.5) / n_theta
    first = np.arange(quarters(parts))[:, None] * per_part
    phi = 2.0 * np.pi * (first + np.arange(low, high)[None]) / n_phi
    u_x = np.cos(phi)[..., None] * np.sin(theta)
    u_y = np.sin(phi)[..., None] * np.sin(theta)
    u_z = np.broadcast_to(np.cos(theta), u_x.shape)
    psi = np.stack([0.5 * np.pi * size * (s_x * u_x + s_y * u_y + u_z) for s_x, s_y in REPS], axis=2)
    return np.concatenate([np.cos(psi), np.sin(psi)], axis=2).astype(np.float32)


def octant(rep, turns):
    s_x, s_y = REPS[rep]
    for _ in range(turns):
        s_x, s_y = -s_y, s_x
    return 2 * (s_x + 1) + (s_y + 1) + 1


def split(x):
    high = x.astype(jnp.bfloat16)
    return high, (x - high.astype(jnp.float32)).astype(jnp.bfloat16)


def mm(a, b):
    return jnp.dot(a, b, preferred_element_type=jnp.float32)


def pick(index, values):
    if isinstance(index, int):
        return values[index]
    out = jnp.int32(values[0])
    for k in range(1, len(values)):
        out = jnp.where(index == k, values[k], out)
    return out


class Plan:
    def __init__(self, n_samp, n_box, pa, pb, pc, theta_c):
        self.n_samp, self.n_box = n_samp, n_box
        self.pa, self.pb, self.pc = pa, pb, pc
        n_a, n_b, n_c = n_samp * pa, n_samp * pb, n_samp * pc
        self.low_b, self.high_b = window(0, pa - 1, n_a, n_b)
        low_c, high_c = window(self.low_b, self.high_b - 1, n_b, n_c)
        self.ext = -(-max(-low_c, high_c - pc) // GROUP) * GROUP
        self.low_c, self.high_c = -self.ext, pc + self.ext
        self.wb, self.wc = self.high_b - self.low_b, self.high_c - self.low_c
        self.unit_rows = 2 * GROUP * theta_c // LANES
        self.edge, self.inner = self.ext // GROUP, pc // GROUP
        self.rows = rows = self.inner * self.unit_rows
        ext_rows = self.edge * self.unit_rows
        self.padded = -(-rows // 8) * 8
        groups = self.padded // 8
        self.split = -(-groups // 2)
        other = groups - self.split
        self.end_at = (rows - ext_rows) // 8 * 8
        self.left_rows = self.padded - self.end_at
        self.left_pad = rows - ext_rows - self.end_at
        self.right_rows = -(-ext_rows // 8) * 8
        self.left_at = pl.ds(self.padded, self.left_rows)
        self.right_at = pl.ds(self.padded + self.left_rows, self.right_rows)
        self.total = self.padded + self.left_rows + self.right_rows
        touched = max(self.left_rows, self.right_rows) // 8
        self.sizes, self.blocks = [], []
        for block in CHUNKS + ((1,),) * self.split:
            members = []
            for size in block:
                left = other - sum(self.sizes) - (0 if self.blocks else touched)
                if sum(self.sizes) < self.split and (left > 0 or self.blocks and not members):
                    members.append(len(self.sizes))
                    self.sizes.append(min(size, left) if left > 0 else 1)
            if members:
                self.blocks.append(members)
        self.starts = [sum(self.sizes[:c]) for c in range(len(self.sizes))]
        ends = [a + n for a, n in zip(self.starts, self.sizes)]
        self.both = [end <= other for end in ends]
        self.block_of = [k for k, members in enumerate(self.blocks) for _ in members]
        self.block_starts = [self.starts[members[0]] for members in self.blocks]
        self.block_sizes = [sum(self.sizes[c] for c in members) for members in self.blocks]
        self.block_both = [self.both[members[0]] for members in self.blocks]
        self.local = [pl.ds(8 * a, 8 * n) for a, n in zip(self.block_starts, self.block_sizes)]
        self.early = sum(end <= other - touched for end in ends)
        c_low, c_high, b_low, b_high, a_low, a_high = [], [], [], [], [], []
        for c in range(self.early + 1):
            first, last = 0, self.edge * 2 + self.inner
            if c < self.early:
                first = self.edge + 8 * (self.split - ends[c]) // self.unit_rows
                last = min(last, self.edge - (-8 * (self.split + ends[c]) // self.unit_rows))
            c_low.append(first)
            c_high.append(last)
            b0, b1 = 0, self.wb
            if c < self.early:
                b0 = (self.low_c + GROUP * first) * n_b // n_c - 2 - self.low_b
                b1 = (self.low_c + GROUP * last - 1) * n_b // n_c + 3 - self.low_b
                b0, b1 = max(b0, 0), min(b1, self.wb)
                if c:
                    b0, b1 = min(b0, b_low[-1]), max(b1, b_high[-1])
                inside_low, inside_high = -self.low_b, pb - self.low_b
                more = -(b1 - b0 - (b_high[-1] - b_low[-1] if c else 0)) % UNROLL_B
                for k in range(more):
                    if (k % 2 == 0 or b1 >= inside_high) and b0 > inside_low:
                        b0 -= 1
                    elif b1 < inside_high:
                        b1 += 1
            b_low.append(b0)
            b_high.append(b1)
            a0 = max((b0 + self.low_b) * n_a // n_b - 2, 0)
            a1 = min((b1 - 1 + self.low_b) * n_a // n_b + 3, pa)
            if c == self.early:
                a0, a1 = 0, pa
            a_low.append(a0 // GROUP)
            a_high.append(-(-a1 // GROUP))
        inside = [
            b0 + self.low_b >= 0 and b1 + self.low_b <= pb and self.edge <= c0 and c1 <= self.edge + self.inner
            for b0, b1, c0, c1 in zip(b_low, b_high, c_low, c_high)
        ]
        assert all(inside[: self.early]) and self.early
        assert self.early >= len(self.blocks[0]) and self.both[0]
        self.edges_late = self.block_both[1] and self.early > self.blocks[1][-1]
        self.x_low, self.x_high = 6 * a_low[0] // 8 * 8, -(-6 * a_high[0] // 8) * 8
        self.levels = (self.spans(a_low, a_high), self.spans(b_low, b_high), self.spans(c_low, c_high))

    @staticmethod
    def spans(low, high):
        before_low, before_high = [high[0]] + low[:-1], [high[0]] + high[:-1]
        left = [b - a for a, b in zip(low, before_low)]
        count = [n + b - a for n, a, b in zip(left, before_high, high)]
        return low, left, before_high, count


def stencil(plan, samp, start, weight):
    row = lax.broadcasted_iota(jnp.int32, start.shape, 0)
    at_b = row < 4
    n_a, n_b = plan.n_samp * plan.pa, plan.n_samp * plan.pb

    def choose(b, c):
        return jnp.where(at_b, b, c)

    tap = start + choose(row - samp * plan.pa, row - 4 - samp * plan.pb)
    count, half = choose(n_a, n_b), choose(n_a // 2, n_b // 2)
    low, high = choose(0, plan.low_b), choose(plan.pa, plan.high_b)
    centre = choose(plan.pa // 2, (plan.low_b + plan.high_b) // 2)
    for _ in range(2):
        tap = jnp.where(tap - centre > half, tap - count, tap)
        tap = jnp.where(tap - centre < -half, tap + count, tap)
    inside = (tap >= low) & (tap < high)
    return jnp.clip(tap - low, 0, high - low - 1), jnp.where(inside, weight, 0.0)


def far_kernel(plan, list_len, x_hbm, *rest):
    small_hbm, (phb_hbm, phc_hbm, t_hbm, o_ref), small, rest = rest[:10], rest[10:14], rest[14:24], rest[24:]
    (theta_ab, theta_bc, child_b, child_c, start_b, weight_b, start_c, weight_c, src_ref, vec_ref) = small
    (
        x_ref, grid_a, pattern_b, grid_b, phb, phc, tab, tbc,
        s_b, s_c, ints, floats, tables_i, tables_w, idx, wgt,
        wide, lists, list_all, list_smem, halo_left, halo_right, res,
        psend, precv,
        *rest,
    ) = rest
    n_chunk, n_block = len(plan.sizes), len(plan.blocks)
    srcs, tbufs = rest[:n_block], rest[n_block : 2 * n_block]
    (in_sem, table_sem, list_sem, smem_sem, halo_sem, t_sem, src_send, src_recv, p_sem, out_sem) = rest[2 * n_block :]
    samp, box = lax.axis_index("samp"), lax.axis_index("box")
    n_box, n_samp = plan.n_box, plan.n_samp
    n_chip = n_box // 2
    chip, core = box // 2, box % 2
    partner = chip * 2 + 1 - core
    own = wide.shape[0]
    n_src = own * n_box
    first_end, last_end = chip == 0, chip == n_chip - 1
    is_end = first_end | last_end
    helps_first, helps_last = chip == 1, chip == n_chip - 2
    helps = helps_first | helps_last
    helped = jnp.where(helps_first, 0, n_chip - 1)
    helper = jnp.where(first_end, 1, n_chip - 2)
    left = (lax.rem(samp + n_samp - 1, n_samp), box)
    right = (lax.rem(samp + 1, n_samp), box)
    n_base = quarters(n_samp)

    barrier = pltpu.get_barrier_semaphore()
    for other in range(n_box):
        @pl.when(box != other)
        def _():
            pl.semaphore_signal(barrier, inc=1, device_id=(samp, other), device_id_type=MESH)
    for device in (left, right):
        pl.semaphore_signal(barrier, inc=1, device_id=device, device_id_type=MESH)

    x_rows_all = x_hbm.shape[1]
    pieces = [
        (first, last - first)
        for first, last in ((plan.x_low, plan.x_high), (0, plan.x_low), (plan.x_high, x_rows_all))
        if last > first
    ]
    in_copies = []
    for k, (first, n) in enumerate(pieces):
        here = pl.ds(first, n)
        in_copies.append(pltpu.make_async_copy(x_hbm.at[:, here, :], x_ref.at[:, here, :], in_sem.at[k]))
        if k == 0:
            base = lax.rem(samp, n_base)
            in_copies.append(pltpu.make_async_copy(phb_hbm.at[base], phb, in_sem.at[3]))
            in_copies.append(pltpu.make_async_copy(phc_hbm.at[base], phc, in_sem.at[4]))
    small_copies = [
        pltpu.make_async_copy(a, b, in_sem.at[5 + k]) for k, (a, b) in enumerate(zip(small_hbm, small))
    ]
    for copy in small_copies[:1] + in_copies[:1] + small_copies[1:] + in_copies[1:]:
        copy.start()
    small_copies[0].wait()
    count_a, count_b, count_c = x_ref.shape[0], child_b.shape[1], child_c.shape[0]
    theta_a, theta_b = theta_ab.shape
    theta_c = theta_bc.shape[0]
    def remote(src, dst, send, recv, device):
        return pltpu.make_async_remote_copy(
            src_ref=src, dst_ref=dst, send_sem=send, recv_sem=recv, device_id=device, device_id_type=MESH
        )

    tab[...] = jnp.zeros(tab.shape, jnp.bfloat16)
    high, low = split(theta_ab[...])
    for pair in range(2):
        at = pair * (2 * theta_a - LANES)
        for k in range(2):
            rows = slice(at + k * theta_a, at + (k + 1) * theta_a)
            cols = slice(k * theta_b, (k + 1) * theta_b)
            tab[pair, 0, rows, cols] = high
            tab[pair, 1, rows, cols] = low
    turns = samp // n_base

    def one_hot(ids, first, count):
        lane = lax.broadcasted_iota(jnp.int32, (ids.shape[0], count), 1) + first
        plus, minus = [], []
        for rep in range(4):
            hots = []
            for flip in range(2):
                column = None
                for t in range(n_samp // n_base):
                    o = octant(rep, t)
                    o = 7 - o if flip else o
                    here = ids[:, o : o + 1]
                    column = here if column is None else jnp.where(turns == t, here, column)
                hots.append(jnp.where(column == lane, 1.0, 0.0))
            plus.append(hots[0] + hots[1])
            minus.append(hots[0] - hots[1])
        hot = jnp.concatenate(plus + minus, axis=0).astype(jnp.bfloat16)
        return jnp.concatenate([hot, hot], axis=1)

    table_copies = []
    for k, ref in enumerate((ints, floats)):
        for d, (slot, device) in enumerate(((2, left), (0, right))):
            n = 4 * k + 2 * d
            table_copies.append(remote(ref.at[1], ref.at[slot], table_sem.at[n], table_sem.at[n + 1], device))
    def rows_of(which, start, size):
        low, high = 8 * (plan.split - start - size), 8 * (plan.split + start)
        return pl.ds(pl.multiple_of(jnp.where(which == 0, low, high), 8), 8 * size)

    def send_rows(which, c):
        return rows_of(which, plan.starts[c], plan.sizes[c])

    def half_rows(which, k):
        return rows_of(which, plan.block_starts[k], plan.block_sizes[k])

    def inner_rows(which, c):
        k = plan.block_of[c]
        after = plan.starts[c] - plan.block_starts[k]
        before = plan.block_sizes[k] - after - plan.sizes[c]
        return pl.ds(pl.multiple_of(jnp.where(which == 0, 8 * before, 8 * after), 8), 8 * plan.sizes[c])

    def t_copy(c):
        return pltpu.make_async_copy(t_hbm.at[:, half_rows(core, c), :], tbufs[c], t_sem.at[c])

    def when_has(which, c, do):
        if plan.block_both[c]:
            do()
        else:
            pl.when(which == 0)(do)

    to_left = remote(wide.at[:, plan.left_at, :], halo_right, halo_sem.at[0], halo_sem.at[1], left)
    to_right = remote(wide.at[:, plan.right_at, :], halo_left, halo_sem.at[2], halo_sem.at[3], right)

    def list_copy(slot, device, k):
        return remote(lists, list_all.at[slot], list_sem.at[k], list_sem.at[3 + slot], device)

    def src_copy(c, chip_to, d):
        index = c * n_box + chip_to * 2 + d
        return remote(
            wide.at[:, send_rows(d, c), :],
            srcs[plan.block_of[c]].at[pl.ds(pl.multiple_of(own * box, 8), own), inner_rows(d, c), :],
            src_send.at[index],
            src_recv.at[c * n_box + box],
            (samp, chip_to * 2 + d),
        )

    def send_chunk(c, act):
        def to_partner():
            act(src_copy(c, chip, 1 - core))

        when_has(1 - core, plan.block_of[c], to_partner)
        for chip_to in range(1, n_chip - 1):
            @pl.when(chip != chip_to)
            def _():
                for d in range(2):
                    if d == 0 or plan.both[c]:
                        act(src_copy(c, chip_to, d))

    x_rows = x_ref.reshape(count_a * x_ref.shape[1], LANES)
    wide_rows = wide.reshape(own * plan.total, LANES)
    stride_x = x_ref.shape[1]

    def theta_blocks(blocks):
        highs, lows = [], []
        for q in blocks:
            for c in range(2):
                tiles = [split(x_rows[pl.ds(6 * q + 2 * j + c, count_a, stride=stride_x), :]) for j in range(3)]
                highs.append([t[0] for t in tiles])
                lows.append([t[1] for t in tiles])
        for pair in range(2):
            here = slice(pair, pair + 2)
            high = jnp.concatenate([jnp.concatenate(h[here], axis=1) for h in highs], axis=0)
            low = jnp.concatenate([jnp.concatenate(h[here], axis=1) for h in lows], axis=0)
            count = high.shape[0]
            twice = mm(jnp.concatenate([high, low], axis=0), tab[pair, 0])
            both = twice[:count] + twice[count:] + mm(high, tab[pair, 1])
            for n, q in enumerate(blocks):
                for k in range(2):
                    grid_a[GROUP * q + 2 * pair + k] = both[
                        2 * count_a * n : 2 * count_a * (n + 1), k * LANES : (k + 1) * LANES
                    ]

    def taps(n, per_part, first_row):
        part = jnp.where(n >= 0, 1, 0) + jnp.where(n >= per_part, 1, 0)
        col = n + per_part * (1 - part)
        return [(idx[part, first_row + k, col], wgt[part, first_row + k, col]) for k in range(4)]

    def octants(phase, plus_r, plus_i, minus_r, minus_i, count):
        real = imag = None
        for j in range(4):
            cosine, sine = phase[j : j + 1, :], phase[4 + j : 5 + j, :]
            here = slice(j * count, (j + 1) * count)
            re = plus_r[here] * cosine - minus_i[here] * sine
            im = plus_i[here] * cosine + minus_r[here] * sine
            real, imag = (re, im) if real is None else (real + re, imag + im)
        return real, imag

    def level_b(m):
        stencil_b = taps(m + plan.low_b, plan.pb, 0)
        parts = []
        for c in range(2):
            here = slice(c * count_a, (c + 1) * count_a)
            value = None
            for at, weight in stencil_b:
                term = weight * grid_a[at, here, :]
                value = term if value is None else value + term
            parts.append(split(value))
        stacked = jnp.concatenate(
            [
                jnp.concatenate([parts[0][0], parts[1][0]], axis=1),
                jnp.concatenate([parts[0][1], parts[1][1]], axis=1),
            ],
            axis=0,
        )
        picked = mm(s_b[...], stacked)
        mid = 4 * count_b
        real, imag = octants(
            phb[m], picked[:mid, :LANES], picked[:mid, LANES:], picked[mid:, :LANES], picked[mid:, LANES:], count_b
        )
        high, low = split(jnp.concatenate([real, imag], axis=0))
        return jnp.concatenate([high, low], axis=1)

    def level_c(g):
        values = []
        for i in range(GROUP):
            value = None
            for at, weight in taps(g * GROUP + i + plan.low_c, plan.pc, 4):
                term = weight * grid_b[at]
                value = term if value is None else value + term
            values.append(value)
        high, low = split(jnp.concatenate(values, axis=1))
        rr = mm(s_c[...], jnp.concatenate([high[:count_b], low[:count_b]], axis=0))
        ri = mm(s_c[...], jnp.concatenate([high[count_b:], low[count_b:]], axis=0))
        mid = 4 * count_c
        real, imag = octants(phc[g], rr[:mid], ri[:mid], rr[mid:], ri[mid:], count_c)
        base = jnp.where(
            g < plan.edge,
            plan.padded + plan.left_pad + g * plan.unit_rows,
            jnp.where(
                g < plan.edge + plan.inner,
                (g - plan.edge) * plan.unit_rows,
                plan.padded + plan.left_rows + (g - plan.edge - plan.inner) * plan.unit_rows,
            ),
        )
        for c, flat in enumerate((real, imag)):
            for t in range(plan.unit_rows // 2):
                wide_rows[pl.ds(base + 2 * t + c, own, stride=plan.total), :] = flat[:, t * LANES : (t + 1) * LANES]

    def resolve(parts):
        copies = []
        for part in parts:
            row = lax.broadcasted_iota(jnp.int32, ints.shape[1:], 0)
            start = jnp.where(row < 4, ints[part, 0:1, :], ints[part, 1:2, :])
            at, weight = stencil(plan, samp, start, floats[part])
            tables_i[part] = at
            tables_w[part] = weight
            copies.append(pltpu.make_async_copy(tables_i.at[part], idx.at[part], smem_sem.at[part]))
            copies.append(pltpu.make_async_copy(tables_w.at[part], wgt.at[part], smem_sem.at[3 + part]))
        for copy in copies:
            copy.start()
        return copies

    def rest_of_setup():
        for copy in small_copies[1:]:
            copy.wait()
        ints[1, 0:1, 0 : plan.pb] = start_b[...]
        ints[1, 1:2, 0 : plan.pc] = start_c[...]
        floats[1, 0:4, 0 : plan.pb] = weight_b[...]
        floats[1, 4:8, 0 : plan.pc] = weight_c[...]
        lists[:, 0:list_len] = src_ref[...]
        lists[:, list_len : 2 * list_len] = vec_ref[...]
        own_tables = resolve((1,))
        high, low = split(theta_bc[...].T)
        tbc[0, :theta_b] = high
        tbc[0, theta_b:] = high
        tbc[1, :theta_b] = low
        tbc[1, theta_b:] = low
        s_b[...] = one_hot(child_b[...].T, box * count_a, count_a)
        s_c[...] = one_hot(child_c[...], box * count_b, count_b)
        blank = plan.rows // 8 * 8
        wide[:, blank:, :] = jnp.zeros((own, plan.total - blank, LANES), jnp.float32)
        for copy in own_tables + in_copies[1:3]:
            copy.wait()

    def phase(ph, carry):
        def items(level):
            low, before, after, count = (pick(ph, values) for values in plan.levels[level])
            return count, lambda i: jnp.where(i < before, low + i, after + i - before)

        count, item = items(0)

        def one_a(i, carry):
            theta_blocks([item(2 * i), item(jnp.minimum(2 * i + 1, count - 1))])
            return carry

        lax.fori_loop(0, pick(ph, [-(-n // 2) for n in plan.levels[0][3]]), one_a, 0)
        if isinstance(ph, int):
            for k in range(n_block):
                when_has(core, k, lambda k=k: t_copy(k).start())
            rest_of_setup()
        count_m, item_m = items(1)

        def some_m(i, n):
            return [item_m(jnp.minimum(n * i + k, count_m - 1)) for k in range(n)]

        def one_b(i, carry):
            at = some_m(i, UNROLL_B)
            values = [level_b(m) for m in at]
            for m, value in zip(at, values):
                pattern_b[m] = value
            return carry

        def one_theta(i, carry):
            at = some_m(i, UNROLL_T)
            both = jnp.concatenate([pattern_b[m] for m in at], axis=0)
            grid = mm(both, tbc[0]) + mm(both[:, :LANES], tbc[1, :LANES])
            for k, m in enumerate(at):
                grid_b[m] = grid[2 * count_b * k : 2 * count_b * (k + 1)]
            return carry

        lax.fori_loop(0, pick(ph, [-(-n // UNROLL_B) for n in plan.levels[1][3]]), one_b, 0)
        lax.fori_loop(0, pick(ph, [-(-n // UNROLL_T) for n in plan.levels[1][3]]), one_theta, 0)
        count_g, item_g = items(2)

        def one_c(i, carry):
            level_c(item_g(i))
            return carry

        lax.fori_loop(0, count_g, one_c, 0)
        for c in range(1, 1 if isinstance(ph, int) else plan.early):
            @pl.when(ph == c)
            def _():
                send_chunk(c, lambda copy: copy.start())

        return carry

    even = lax.rem(lax.broadcasted_iota(jnp.int32, (8, LANES), 0), 2) == 0

    def turn(x):
        return jnp.where(even, pltpu.roll(x, 7, 0), pltpu.roll(x, 1, 0))

    def gather_sum(c, slot, i):
        size = plan.block_sizes[c]
        by_same = [jnp.zeros((8, LANES), jnp.float32) for _ in range(size)]
        by_turned = [jnp.zeros((8, LANES), jnp.float32) for _ in range(size)]
        for l in range(list_len):
            s = list_smem[slot, i, l]
            v = list_smem[slot, i, list_len + l]
            for g in range(size):
                here = slice(8 * g, 8 * g + 8)
                t = tbufs[c][v, here, :]
                by_same[g] = by_same[g] + t * srcs[c][s, here, :]
                by_turned[g] = by_turned[g] + t * srcs[c][s, slice(8 * (size + g), 8 * (size + g) + 8), :]
        out = []
        for g in range(size):
            x, y = by_same[g], by_turned[g]
            out.append(jnp.where(even, x - pltpu.roll(x, 7, 0), y + pltpu.roll(y, 1, 0)))
        return out

    def result_copy(c):
        return remote(
            res.at[pl.ds(pl.multiple_of((1 - core) * own, 8), own), plan.local[c], :],
            o_ref.at[:, half_rows(core, c), :],
            out_sem.at[c],
            out_sem.at[n_block + c],
            (samp, partner),
        )

    def result_wait(c):
        return remote(
            res.at[pl.ds(pl.multiple_of((1 - core) * own, 8), own), plan.local[c], :],
            o_ref.at[:, half_rows(1 - core, c), :],
            out_sem.at[c],
            out_sem.at[n_block + c],
            (samp, partner),
        )

    def p_copy(c, chip_to):
        return remote(
            psend.at[:, plan.local[c], :],
            precv.at[:, plan.local[c], :],
            p_sem.at[c],
            p_sem.at[n_block + c],
            (samp, chip_to * 2 + core),
        )

    def prepare(c):
        size = plan.block_sizes[c]
        rows = 8 * size
        srcs[c][pl.ds(pl.multiple_of(own * box, 8), own), 0:rows, :] = wide[:, half_rows(core, c), :]
        srcs[c][n_src] = jnp.zeros((2 * rows, LANES), jnp.float32)
        t_copy(c).wait()

        def arrived(other):
            for send in plan.blocks[c]:
                pltpu.make_async_copy(
                    wide.at[:, send_rows(core, send), :],
                    srcs[c].at[pl.ds(own * other, own), inner_rows(core, send), :],
                    src_recv.at[send * n_box + other],
                ).wait()

        for other in range(n_box):
            here = (box != other) & (jnp.logical_not(is_end) | (chip == other // 2))
            pl.when(here)(functools.partial(arrived, other))

        def swap_some(i, carry):
            for k in range(own):
                for g in range(size):
                    s = own * i + k
                    turned = turn(srcs[c][s, slice(8 * g, 8 * g + 8), :])
                    srcs[c][s, slice(8 * (size + g), 8 * (size + g) + 8), :] = turned
            return carry

        first = jnp.where(is_end, 2 * chip, 0)
        last = jnp.where(is_end, 2 * chip + 2, n_box)
        lax.fori_loop(first, last, swap_some, 0)

    def partial_sums(c):
        place = plan.local[c]

        @pl.when(helps)
        def _():
            def one(p, carry):
                slot, i = 2 + p // own, lax.rem(p, own)
                for g, value in enumerate(gather_sum(c, slot, i)):
                    psend[p, pl.ds(place.start + 8 * g, 8), :] = value
                return carry

            lax.fori_loop(0, 2 * own, one, 0)
            p_copy(c, helped).start()

    def own_sums(c):
        place = plan.local[c]

        def one(p, carry):
            slot, i = p // own, lax.rem(p, own)
            for g, value in enumerate(gather_sum(c, slot, i)):
                res[p, pl.ds(place.start + 8 * g, 8), :] = value
            return carry

        lax.fori_loop(0, 2 * own, one, 0)

    def finish(c):
        own_sums(c)

        @pl.when(jnp.logical_not(is_end))
        def _():
            deliver_plain(c)

    def deliver_plain(c):
        place = plan.local[c]
        o_ref[:, half_rows(core, c), :] = res[pl.ds(pl.multiple_of(core * own, 8), own), place, :]
        result_copy(c).start()

    def deliver_end(c):
        place = plan.local[c]
        p_copy(c, chip).wait_recv()
        res[:, place, :] = res[:, place, :] + precv[:, place, :]
        deliver_plain(c)

    def resolve_lists():
        list_copy(1 - core, (samp, partner), 0).wait_recv()

        @pl.when(helps)
        def _():
            for d in range(2):
                list_copy(2 + d, (samp, partner), 0).wait_recv()

        low = jnp.where(last_end, n_src - 2 * own, 0)
        high = jnp.where(first_end, 2 * own, n_src)
        low_p = jnp.where(helps_first, 2 * own, 0)
        high_p = jnp.where(helps_last, n_src - 2 * own, n_src)
        lane = lax.broadcasted_iota(jnp.int32, list_all.shape[1:], 1)
        for slot in range(4):
            a, b = (low, high) if slot < 2 else (low_p, high_p)
            value = list_all[slot]
            gone = (lane < list_len) & ((value < a) | (value >= b))
            list_all[slot] = jnp.where(gone, n_src, value)
        to_smem = pltpu.make_async_copy(list_all, list_smem, smem_sem.at[6])
        to_smem.start()
        return to_smem

    def later_phase(ph, carry):
        @pl.when(ph == plan.early)
        def _():
            for copy in table_copies:
                copy.wait_recv()
            copies = resolve((0, 2))
            to_smem = resolve_lists()
            prepare(0)
            to_smem.wait()
            partial_sums(0)
            for copy in copies:
                copy.wait()

        return phase(ph, carry)

    in_copies[0].wait()
    phase(0, 0)
    pl.semaphore_wait(barrier, n_box + 1)
    send_chunk(0, lambda copy: copy.start())
    for copy in table_copies:
        copy.start()
    list_copy(core, (samp, partner), 0).start()

    @pl.when(is_end)
    def _():
        for d in range(2):
            list_copy(2 + core, (samp, helper * 2 + d), 1 + d).start()

    list_all[core] = lists[...]
    for copy in in_copies[3:]:
        copy.wait()
    lax.fori_loop(1, plan.early + 1, later_phase, 0)
    to_left.start()
    to_right.start()

    def finish_edges():
        to_left.wait_recv()
        to_right.wait_recv()
        at_end = pl.ds(plan.end_at, halo_right.shape[1])
        wide[:, at_end, :] = wide[:, at_end, :] + halo_right[...]
        at_start = pl.ds(0, halo_left.shape[1])
        wide[:, at_start, :] = wide[:, at_start, :] + halo_left[...]
        for c in range(plan.early, n_chunk):
            send_chunk(c, lambda copy: copy.start())

    finish(0)
    if not plan.edges_late:
        finish_edges()

    def whole_block(k):
        prepare(k)
        partial_sums(k)
        if k == 1 and plan.edges_late:
            finish_edges()
        finish(k)

    for k in range(1, n_block):
        when_has(core, k, functools.partial(whole_block, k))

    for c in range(n_chunk):
        send_chunk(c, lambda copy: copy.wait_send())
    for copy in table_copies:
        copy.wait_send()
    to_left.wait_send()
    to_right.wait_send()
    list_copy(core, (samp, partner), 0).wait_send()

    @pl.when(is_end)
    def _():
        for d in range(2):
            list_copy(2 + core, (samp, helper * 2 + d), 1 + d).wait_send()

    @pl.when(is_end)
    def _():
        for k in range(n_block):
            when_has(core, k, lambda k=k: deliver_end(k))

    for k in range(n_block):
        when_has(core, k, lambda k=k: result_copy(k).wait_send())

        @pl.when(helps)
        def _():
            when_has(core, k, lambda: p_copy(k, helped).wait_send())

        when_has(1 - core, k, lambda k=k: result_wait(k).wait_recv())


def interleave(x):
    x = x.reshape(x.shape[0], 2, -1, LANES).transpose(0, 2, 1, 3)
    x = with_layout_constraint(x, Layout(major_to_minor=(0, 1, 2, 3))).reshape(x.shape[0], -1, LANES)
    return jnp.pad(x, ((0, 0), (0, -x.shape[1] % 8), (0, 0))) if x.shape[1] % 8 else x


def separate(x, rows):
    x = x[:, :rows].reshape(x.shape[0], -1, 2, LANES)
    x = with_layout_constraint(x, Layout(major_to_minor=(0, 1, 2, 3)))
    return x.transpose(0, 2, 1, 3).reshape(x.shape[0], 2, -1)


def per_device(
    n_samp, n_box,
    pattern_a, children_b, children_c, theta_ab, theta_bc,
    phi_start_b, phi_weight_b, phi_start_c, phi_weight_c,
    translation, list_src, list_vec,
):
    count_a, count_b, count_c = pattern_a.shape[0], children_b.shape[0], children_c.shape[0]
    theta_a, theta_b = theta_ab.shape
    theta_c = theta_bc.shape[1]
    pa = pattern_a.shape[2] // theta_a
    plan = Plan(n_samp, n_box, pa, phi_start_b.shape[0], phi_start_c.shape[0], theta_c)
    phb = jnp.asarray(phase_table(n_samp, plan.pb, plan.low_b, plan.high_b, theta_b, SIZE_B))
    phc = phase_table(n_samp, plan.pc, plan.low_c, plan.high_c, theta_c, SIZE_C)
    phc = phc.reshape(phc.shape[0], -1, GROUP, 8, theta_c).transpose(0, 1, 3, 2, 4)
    phc = jnp.asarray(phc.reshape(phc.shape[:3] + (-1,)))
    x = interleave(pattern_a)
    t_view = interleave(translation)
    list_len = list_src.shape[1]
    n_src = count_c * n_box
    n_chunk, n_block = len(plan.sizes), len(plan.blocks)
    half = 8 * plan.split
    list_lanes = -(-2 * list_len // LANES) * LANES
    lanes = -(-max(plan.pb, plan.pc) // LANES) * LANES
    vmem = pl.BlockSpec(memory_space=pltpu.VMEM)
    hbm = pl.BlockSpec(memory_space=pl.ANY)
    f32, bf16, i32 = jnp.float32, jnp.bfloat16, jnp.int32
    small = (
        theta_ab, theta_bc.T, children_b.T, children_c,
        phi_start_b.reshape(1, -1), phi_weight_b, phi_start_c.reshape(1, -1), phi_weight_c,
        list_src, list_vec,
    )
    out = pl.pallas_call(
        functools.partial(far_kernel, plan, list_len),
        in_specs=[hbm] * 14,
        out_specs=vmem,
        scratch_shapes=[pltpu.VMEM(a.shape, a.dtype) for a in small]
        + [
            pltpu.VMEM(x.shape, f32),
            pltpu.VMEM((pa, 2 * count_a, LANES), f32),
            pltpu.VMEM((plan.wb, 2 * count_b, 2 * theta_b), bf16),
            pltpu.VMEM((plan.wb, 2 * count_b, theta_c), f32),
            pltpu.VMEM(phb.shape[1:], f32),
            pltpu.VMEM(phc.shape[1:], f32),
            pltpu.VMEM((2, 2, 2 * LANES, 2 * theta_b), bf16),
            pltpu.VMEM((2, 2 * theta_b, theta_c), bf16),
            pltpu.VMEM((8 * count_b, 2 * count_a), bf16),
            pltpu.VMEM((8 * count_c, 2 * count_b), bf16),
            pltpu.VMEM((3, 8, lanes), i32),
            pltpu.VMEM((3, 8, lanes), f32),
            pltpu.VMEM((3, 8, lanes), i32),
            pltpu.VMEM((3, 8, lanes), f32),
            pltpu.SMEM((3, 8, lanes), i32),
            pltpu.SMEM((3, 8, lanes), f32),
            pltpu.VMEM((count_c, plan.total, LANES), f32),
            pltpu.VMEM((count_c, list_lanes), i32),
            pltpu.VMEM((4, count_c, list_lanes), i32),
            pltpu.SMEM((4, count_c, list_lanes), i32),
            pltpu.VMEM((count_c, plan.right_rows, LANES), f32),
            pltpu.VMEM((count_c, plan.left_rows, LANES), f32),
            pltpu.VMEM((2 * count_c, half, LANES), f32),
            pltpu.VMEM((2 * count_c, half, LANES), f32),
            pltpu.VMEM((2 * count_c, half, LANES), f32),
        ]
        + [pltpu.VMEM((n_src + 1, 16 * n, LANES), f32) for n in plan.block_sizes]
        + [pltpu.VMEM((t_view.shape[0], 8 * n, LANES), f32) for n in plan.block_sizes]
        + [
            pltpu.SemaphoreType.DMA((15,)),
            pltpu.SemaphoreType.DMA((8,)),
            pltpu.SemaphoreType.DMA((7,)),
            pltpu.SemaphoreType.DMA((7,)),
            pltpu.SemaphoreType.DMA((4,)),
            pltpu.SemaphoreType.DMA((n_block,)),
            pltpu.SemaphoreType.DMA((n_chunk * n_box,)),
            pltpu.SemaphoreType.DMA((n_chunk * n_box,)),
            pltpu.SemaphoreType.DMA((2 * n_block,)),
            pltpu.SemaphoreType.DMA((2 * n_block,)),
        ],
        out_shape=pltpu.VMEM((count_c, plan.padded, LANES), f32),
        compiler_params=pltpu.CompilerParams(
            collective_id=0, has_side_effects=True, vmem_limit_bytes=56 << 20
        ),
        name="far",
    )(x, *small, phb, phc, t_view)
    return separate(out, plan.rows)


def solution(mesh):
    placed = (
        P("box", None, "samp"),
        P("box", None),
        P("box", None),
        P(),
        P(),
        P("samp"),
        P(None, "samp"),
        P("samp"),
        P(None, "samp"),
        P(None, None, "samp"),
        P("box", None),
        P("box", None),
    )
    return jax.shard_map(
        functools.partial(per_device, mesh.shape["samp"], mesh.shape["box"]),
        mesh=mesh, in_specs=placed, out_specs=P("box", None, "samp"), check_vma=False,
    )
```
